32 devices in a mesh: dp: 8 (over y, x, core), group: 4 (over z).
Axes of the slice: x: 2, y: 2, z: 4, core: 2. Of those that a mesh axis runs over, the one named last changes fastest.
Arguments:
- stream: float32 [8192, 1024], P(('dp', 'group')), may hold values from -6 to 6
- cotangent: float32 [8192, 1024], P(('dp', 'group')), may hold values from -6 to 6
- bounds: int32 [8192, 2], P(('dp', 'group')), may hold values from 0 to 8192, as said below
- joined_proj: float32 [1024, 3072], P(('dp', 'group'))
- out_proj: float32 [1024, 1024], P(('dp', 'group')), may hold values from -3 to 3
- wide_proj: float32 [1024, 5248], P(('dp', 'group')), may hold values from -0.1875 to 0.1875
- down_proj: float32 [1024, 2624], P(('dp', 'group')), may hold values from -0.125 to 0.125
- gain_first: float32 [1024], P(('dp', 'group')), may hold values from 0.5 to 1.5
- gain_second: float32 [1024], P(('dp', 'group')), may hold values from 0.5 to 1.5
- joined_momentum: float32 [1024, 3072], P(('dp', 'group')), may hold values from -6 to 6
- out_momentum: float32 [1024, 1024], P(('dp', 'group')), may hold values from -6 to 6
- wide_momentum: float32 [1024, 5248], P(('dp', 'group')), may hold values from -6 to 6
- down_momentum: float32 [1024, 2624], P(('dp', 'group')), may hold values from -6 to 6
- gain_first_momentum: float32 [1024], P(('dp', 'group')), may hold values from -6 to 6
- gain_second_momentum: float32 [1024], P(('dp', 'group')), may hold values from -6 to 6
- joined_variance: float32 [1024, 3072], P(('dp', 'group')), may hold values from 1 to 100
- out_variance: float32 [1024, 1024], P(('dp', 'group')), may hold values from 1 to 100
- wide_variance: float32 [1024, 5248], P(('dp', 'group')), may hold values from 1 to 100
- down_variance: float32 [1024, 2624], P(('dp', 'group')), may hold values from 1 to 100
- gain_first_variance: float32 [1024], P(('dp', 'group')), may hold values from 1 to 100
- gain_second_variance: float32 [1024], P(('dp', 'group')), may hold values from 1 to 100
Outputs:
- output: float32 [8192, 1024], P(('dp', 'group'))
- stream_grad: float32 [8192, 1024], P(('dp', 'group'))
- joined_grad: float32 [1024, 3072], P(('dp', 'group'))
- out_grad: float32 [1024, 1024], P(('dp', 'group'))
- wide_grad: float32 [1024, 5248], P(('dp', 'group'))
- down_grad: float32 [1024, 2624], P(('dp', 'group'))
- gain_first_grad: float32 [1024], P(('dp', 'group'))
- gain_second_grad: float32 [1024], P(('dp', 'group'))
- joined_new: float32 [1024, 3072], P(('dp', 'group'))
- out_new: float32 [1024, 1024], P(('dp', 'group'))
- wide_new: float32 [1024, 5248], P(('dp', 'group'))
- down_new: float32 [1024, 2624], P(('dp', 'group'))
- gain_first_new: float32 [1024], P(('dp', 'group'))
- gain_second_new: float32 [1024], P(('dp', 'group'))
- joined_momentum_new: float32 [1024, 3072], P(('dp', 'group'))
- out_momentum_new: float32 [1024, 1024], P(('dp', 'group'))
- wide_momentum_new: float32 [1024, 5248], P(('dp', 'group'))
- down_momentum_new: float32 [1024, 2624], P(('dp', 'group'))
- gain_first_momentum_new: float32 [1024], P(('dp', 'group'))
- gain_second_momentum_new: float32 [1024], P(('dp', 'group'))
- joined_variance_new: float32 [1024, 3072], P(('dp', 'group'))
- out_variance_new: float32 [1024, 1024], P(('dp', 'group'))
- wide_variance_new: float32 [1024, 5248], P(('dp', 'group'))
- down_variance_new: float32 [1024, 2624], P(('dp', 'group'))
- gain_first_variance_new: float32 [1024], P(('dp', 'group'))
- gain_second_variance_new: float32 [1024], P(('dp', 'group'))
The draws below stay inside these ranges and needn't reach their ends.
Inputs may be any that keep to these rules, and one draw needn't show every extreme that they name: `bounds`: each row holds the first token index and one past the last token index of that token's sequence; sequences are contiguous, cover all tokens in order and hold 1 to 1024 tokens, exactly 1024 for one of them, 128 or more for all but the last.
All inputs are finite; a program needn't handle non-finite values.
Results may differ from the reference program's by a relative error of at most 0.018.
Values may be sent and summed in bfloat16 or wider, within the bound.
A program may use at most 320 MiB of HBM per device.

```python
import math
import jax
import jax.numpy as jnp
from jax import lax

D = 1024
HEAD_DIM = 64
FF = 2624
LMAX = 1024
LMIN = 128
STEP = 4
TOKENS = 8192


def draw_bounds(key, part):
    count = TOKENS // LMIN + 1
    lengths = jax.random.randint(jax.random.fold_in(key, 21), (count,), LMIN, LMAX + 1)
    chosen_seq = jax.random.randint(jax.random.fold_in(key, 22), (), 0, 8)
    lengths = jnp.where(jnp.arange(count) == chosen_seq, LMAX, lengths)
    seq_ends = jnp.cumsum(lengths)
    seq_starts = seq_ends - lengths
    token_index = jnp.arange(TOKENS)
    owner = jnp.sum((seq_ends[None, :] <= token_index[:, None]).astype(jnp.int32), axis=1)
    first_token = jnp.take(seq_starts, owner)
    last_token = jnp.minimum(jnp.take(seq_ends, owner), TOKENS)
    return jnp.stack([first_token, last_token], axis=1).astype(jnp.int32)


def draw_joined_proj(key, part):
    base = jax.random.normal(jax.random.fold_in(key, 11), (D, 3 * D), jnp.float32) * D ** (-0.5)
    return base


def steps_of(rng, extent, shards, low, top_value):
    gain = 1.0
    for dim, blocks in shards:
        heights = jax.random.uniform(jax.random.fold_in(jax.random.fold_in(rng, 6), dim), (blocks,), jnp.float32, low / len(shards), top_value / len(shards))
        gain = gain * jnp.repeat(jnp.exp(heights), extent[dim] // blocks).reshape((-1,) + (1,) * (len(extent) - 1 - dim))
    return gain


def bell_draw(stream_key, shape, scale, bound, pieces=(), kind=jnp.bfloat16):
    factor_of = steps_of(stream_key, shape, pieces, -0.22, 0.18) if pieces else 1.0
    drawn = jax.random.normal(stream_key, shape, jnp.float32) * scale * factor_of
    return jnp.minimum(jnp.maximum(drawn, -bound), bound).astype(kind)


def setup_inputs(seed: int = 0) -> dict:
    seeds = jax.random.split(jax.random.key(seed), 22)
    stream = bell_draw(seeds[0], (TOKENS, D), 1.0, 6.0, ((0, 32),), jnp.float32)
    cotangent = bell_draw(seeds[1], (TOKENS, D), 1.0, 6.0, ((0, 32),), jnp.float32)
    bounds = draw_bounds(jax.random.fold_in(seeds[21], 71), 0)
    joined_proj = draw_joined_proj(jax.random.fold_in(seeds[21], 71), 0)
    out_proj = bell_draw(seeds[4], (D, D), (max(D // 256, 1)) ** -0.5, 3.0, ((0, 32),), jnp.float32)
    wide_proj = bell_draw(seeds[5], (D, 2 * FF), D ** -0.5, 0.1875, ((0, 32),), jnp.float32)
    down_proj = bell_draw(seeds[6], (D, FF), FF ** -0.5, 0.125, ((0, 32),), jnp.float32)
    gain_first = jnp.clip(1.0 + 0.1 * jax.random.normal(seeds[7], (D,), jnp.float32), 0.5, 1.5)
    gain_second = jnp.clip(1.0 + 0.1 * jax.random.normal(seeds[8], (D,), jnp.float32), 0.5, 1.5)
    joined_momentum = bell_draw(seeds[9], (D, 3 * D), 1.0, 6.0, ((0, 32),), jnp.float32)
    out_momentum = bell_draw(seeds[10], (D, D), 1.0, 6.0, ((0, 32),), jnp.float32)
    wide_momentum = bell_draw(seeds[11], (D, 2 * FF), 1.0, 6.0, ((0, 32),), jnp.float32)
    down_momentum = bell_draw(seeds[12], (D, FF), 1.0, 6.0, ((0, 32),), jnp.float32)
    gain_first_momentum = bell_draw(seeds[13], (D,), 1.0, 6.0, ((0, 32),), jnp.float32)
    gain_second_momentum = bell_draw(seeds[14], (D,), 1.0, 6.0, ((0, 32),), jnp.float32)
    joined_variance = jnp.clip(jnp.exp(math.log(100.0) - 4.6051702 * jax.random.uniform(seeds[15], (D, 3 * D), jnp.float32) ** steps_of(seeds[15], (D, 3 * D), ((0, 32),), -0.2, 0.2)), 1.0, 100.0)
    out_variance = jnp.clip(jnp.exp(math.log(100.0) - 4.6051702 * jax.random.uniform(seeds[16], (D, D), jnp.float32) ** steps_of(seeds[16], (D, D), ((0, 32),), -0.2, 0.2)), 1.0, 100.0)
    wide_variance = jnp.clip(jnp.exp(math.log(100.0) - 4.6051702 * jax.random.uniform(seeds[17], (D, 2 * FF), jnp.float32) ** steps_of(seeds[17], (D, 2 * FF), ((0, 32),), -0.2, 0.2)), 1.0, 100.0)
    down_variance = jnp.clip(jnp.exp(math.log(100.0) - 4.6051702 * jax.random.uniform(seeds[18], (D, FF), jnp.float32) ** steps_of(seeds[18], (D, FF), ((0, 32),), -0.2, 0.2)), 1.0, 100.0)
    gain_first_variance = jnp.clip(jnp.exp(math.log(100.0) - 4.6051702 * jax.random.uniform(seeds[19], (D,), jnp.float32) ** steps_of(seeds[19], (D,), ((0, 32),), -0.2, 0.2)), 1.0, 100.0)
    gain_second_variance = jnp.clip(jnp.exp(math.log(100.0) - 4.6051702 * jax.random.uniform(seeds[20], (D,), jnp.float32) ** steps_of(seeds[20], (D,), ((0, 32),), -0.2, 0.2)), 1.0, 100.0)
    return dict(stream=stream, cotangent=cotangent, bounds=bounds, joined_proj=joined_proj, out_proj=out_proj, wide_proj=wide_proj, down_proj=down_proj, gain_first=gain_first, gain_second=gain_second, joined_momentum=joined_momentum, out_momentum=out_momentum, wide_momentum=wide_momentum, down_momentum=down_momentum, gain_first_momentum=gain_first_momentum, gain_second_momentum=gain_second_momentum, joined_variance=joined_variance, out_variance=out_variance, wide_variance=wide_variance, down_variance=down_variance, gain_first_variance=gain_first_variance, gain_second_variance=gain_second_variance)


EPSILON = 1e-05
ROPE_BASE = 160000.0
LEARN_RATE = 0.02
BETA_ONE = 0.9
BETA_TWO = 0.98
ADAM_EPSILON = 1e-06
WEIGHT_DECAY = 0.1
NEG_LARGE = -1e+30

def normalize(values):
    centred = values - lax.optimization_barrier(jnp.mean(values, axis=1, keepdims=True))
    row_scale = lax.rsqrt(lax.optimization_barrier(jnp.mean(centred * centred, axis=1, keepdims=True)) + EPSILON)
    return (centred * row_scale, row_scale)

def norm_back(grad_hat, normed, row_scale):
    mean_one = lax.optimization_barrier(jnp.mean(grad_hat, axis=1, keepdims=True))
    mean_two = lax.optimization_barrier(jnp.mean(grad_hat * normed, axis=1, keepdims=True))
    return row_scale * (grad_hat - mean_one - normed * mean_two)

def rope_tables(positions):
    half_dim = HEAD_DIM // 2
    freqs = jnp.exp(jnp.arange(half_dim, dtype=jnp.float32) * (-2.0 * math.log(ROPE_BASE) / HEAD_DIM))
    angles = positions.astype(jnp.float32)[:, None] * freqs[None, :]
    return (jnp.cos(angles), jnp.sin(angles))

def rotate(values, cosine, sine_table, sign):
    half_dim = values.shape[-1] // 2
    front_half = values[..., :half_dim]
    second = values[..., half_dim:]
    cos_part = cosine[:, None, :]
    sin_part = sine_table[:, None, :] * sign
    return jnp.concatenate([front_half * cos_part - second * sin_part, second * cos_part + front_half * sin_part], axis=-1)

def gelu_parts(inner_part):
    cdf_part = 0.5 * (1.0 + lax.erf(inner_part * (1.0 / math.sqrt(2.0))))
    activation = inner_part * cdf_part
    gelu_slope = cdf_part + inner_part * jnp.exp(-0.5 * inner_part * inner_part) * (1.0 / math.sqrt(2.0 * math.pi))
    return (activation, gelu_slope)

def score_block(queries, win_keys, key_mask):
    scores = jnp.einsum('rhd,khd->hrk', queries.astype(jnp.float32), win_keys.astype(jnp.float32)) * HEAD_DIM ** (-0.5)
    return jnp.where(key_mask[None], scores, NEG_LARGE)

def attend_forward(queries, win_keys, win_values, key_mask):
    scores = score_block(queries, win_keys, key_mask)
    row_peak = lax.optimization_barrier(jnp.max(scores, axis=2, keepdims=True))
    sum_exp = lax.optimization_barrier(jnp.sum(jnp.exp(scores - row_peak), axis=2, keepdims=True))
    log_norm = row_peak + jnp.log(sum_exp)
    prob_round = jnp.exp(scores - log_norm).astype(jnp.bfloat16)
    mixed = jnp.einsum('hrk,khd->rhd', prob_round.astype(jnp.float32), win_values.astype(jnp.float32))
    return (mixed, log_norm[..., 0])

def attend_backward(queries, win_keys, win_values, key_mask, log_norm, attended, grad_attended):
    scores = score_block(queries, win_keys, key_mask)
    probs = jnp.exp(scores - log_norm[..., None])
    prob_round = probs.astype(jnp.bfloat16)
    grad_prob = jnp.einsum('rhd,khd->hrk', grad_attended.astype(jnp.float32), win_values.astype(jnp.float32))
    row_delta = lax.optimization_barrier(jnp.sum(grad_attended.astype(jnp.float32) * attended.astype(jnp.float32), axis=2)).T
    grad_score = (probs * (grad_prob - row_delta[..., None])).astype(jnp.bfloat16)
    grad_query = jnp.einsum('hrk,khd->rhd', grad_score.astype(jnp.float32), win_keys.astype(jnp.float32)) * HEAD_DIM ** (-0.5)
    grad_key = jnp.einsum('hrk,rhd->khd', grad_score.astype(jnp.float32), queries.astype(jnp.float32)) * HEAD_DIM ** (-0.5)
    grad_value = jnp.einsum('hrk,rhd->khd', prob_round.astype(jnp.float32), grad_attended.astype(jnp.float32))
    return (grad_query, grad_key, grad_value)

def adam_step(weight, gradient, momentum, variance, decay_rate):
    new_momentum = BETA_ONE * momentum + (1.0 - BETA_ONE) * gradient
    new_variance = BETA_TWO * variance + (1.0 - BETA_TWO) * gradient * gradient
    update = new_momentum / (1.0 - BETA_ONE ** STEP) / (jnp.sqrt(new_variance / (1.0 - BETA_TWO ** STEP)) + ADAM_EPSILON)
    return (weight - LEARN_RATE * (update + decay_rate * weight), new_momentum, new_variance)

def reference(stream, cotangent, bounds, joined_proj, out_proj, wide_proj, down_proj, gain_first, gain_second, joined_momentum, out_momentum, wide_momentum, down_momentum, gain_first_momentum, gain_second_momentum, joined_variance, out_variance, wide_variance, down_variance, gain_first_variance, gain_second_variance):
    joined_half = joined_proj.astype(jnp.bfloat16)
    out_half = out_proj.astype(jnp.bfloat16)
    wide_half = wide_proj.astype(jnp.bfloat16)
    down_half = down_proj.astype(jnp.bfloat16)
    gain_one = lax.optimization_barrier(gain_first.astype(jnp.bfloat16)).astype(jnp.float32)
    gain_two = lax.optimization_barrier(gain_second.astype(jnp.bfloat16)).astype(jnp.float32)
    heads = D // HEAD_DIM
    block_rows = min(4096, TOKENS)
    blocks = TOKENS // block_rows
    seq_starts = bounds[:, 0]
    seq_ends = bounds[:, 1]
    cosine, sine_table = rope_tables(jnp.arange(TOKENS, dtype=jnp.int32) - seq_starts)

    def front(block_index):
        first_row = (block_index * block_rows).astype(jnp.int32)
        row_block = lax.dynamic_slice_in_dim(stream, first_row, block_rows, 0)
        cos_block = lax.dynamic_slice_in_dim(cosine, first_row, block_rows, 0)
        sin_block = lax.dynamic_slice_in_dim(sine_table, first_row, block_rows, 0)
        normed, row_scale = normalize(row_block)
        normed_in = (normed * gain_one).astype(jnp.bfloat16)
        joined_act = jnp.dot(normed_in, joined_half, preferred_element_type=jnp.float32)
        queries = rotate(joined_act[:, :D].reshape(block_rows, heads, HEAD_DIM), cos_block, sin_block, 1.0)
        win_keys = rotate(joined_act[:, D:2 * D].reshape(block_rows, heads, HEAD_DIM), cos_block, sin_block, 1.0)
        queries = queries.astype(jnp.bfloat16).reshape(block_rows, D)
        pairs = jnp.concatenate([win_keys.astype(jnp.bfloat16).reshape(block_rows, D), joined_act[:, 2 * D:].astype(jnp.bfloat16)], axis=1)
        return (normed_in, queries, pairs)
    normed_in, queries, pairs = lax.map(front, jnp.arange(blocks, dtype=jnp.int32))
    normed_in = normed_in.reshape(TOKENS, D)
    queries = queries.reshape(TOKENS, D)
    pairs = pairs.reshape(TOKENS, 2 * D)
    query_rows = min(512, TOKENS)
    query_blocks = TOKENS // query_rows
    key_span = query_rows + 2 * LMAX
    padded = jnp.pad(pairs, ((LMAX, LMAX), (0, 0)))

    def window_of(block_index):
        first_row = (block_index * query_rows).astype(jnp.int32)
        window = lax.dynamic_slice_in_dim(padded, first_row, key_span, 0)
        key_index = first_row - LMAX + jnp.arange(key_span, dtype=jnp.int32)
        start_rows = lax.dynamic_slice_in_dim(seq_starts, first_row, query_rows, 0)
        end_rows = lax.dynamic_slice_in_dim(seq_ends, first_row, query_rows, 0)
        key_mask = (key_index[None, :] >= start_rows[:, None]) & (key_index[None, :] < end_rows[:, None])
        win_keys = window[:, :D].reshape(key_span, heads, HEAD_DIM)
        win_values = window[:, D:].reshape(key_span, heads, HEAD_DIM)
        query_block = lax.dynamic_slice_in_dim(queries, first_row, query_rows, 0).reshape(query_rows, heads, HEAD_DIM)
        return (first_row, query_block, win_keys, win_values, key_mask)

    def attend_block(block_index):
        first_row, query_block, win_keys, win_values, key_mask = window_of(block_index)
        mixed, log_norm = attend_forward(query_block, win_keys, win_values, key_mask)
        return (mixed.astype(jnp.bfloat16).reshape(query_rows, D), log_norm)
    attended, log_norms = lax.map(attend_block, jnp.arange(query_blocks, dtype=jnp.int32))
    attended = attended.reshape(TOKENS, D)

    def middle(block_index):
        first_row = (block_index * block_rows).astype(jnp.int32)
        row_block = lax.dynamic_slice_in_dim(stream, first_row, block_rows, 0)
        cot_block = lax.dynamic_slice_in_dim(cotangent, first_row, block_rows, 0)
        att_block = lax.dynamic_slice_in_dim(attended, first_row, block_rows, 0)
        residual = row_block + jnp.dot(att_block, out_half, preferred_element_type=jnp.float32)
        normed, row_scale = normalize(residual)
        hidden_in = (normed * gain_two).astype(jnp.bfloat16)
        wide_act = jnp.dot(hidden_in, wide_half, preferred_element_type=jnp.float32)
        inner_part = wide_act[:, :FF]
        gate_part = wide_act[:, FF:]
        activation, gelu_slope = gelu_parts(inner_part)
        gated = (activation * gate_part).astype(jnp.bfloat16)
        output = residual + jnp.dot(gated, down_half.T, preferred_element_type=jnp.float32)
        cot_half = cot_block.astype(jnp.bfloat16)
        down_part = jnp.dot(cot_half.T, gated, preferred_element_type=jnp.float32)
        grad_gated = jnp.dot(cot_half, down_half, preferred_element_type=jnp.float32)
        grad_wide = jnp.concatenate([grad_gated * gate_part * gelu_slope, grad_gated * activation], axis=1).astype(jnp.bfloat16)
        wide_part = jnp.dot(hidden_in.T, grad_wide, preferred_element_type=jnp.float32)
        grad_hidden = jnp.dot(grad_wide, wide_half.T, preferred_element_type=jnp.float32)
        gain_two_part = lax.optimization_barrier(jnp.sum(grad_hidden * normed, axis=0))
        grad_resid = cot_block + norm_back(grad_hidden * gain_two, normed, row_scale)
        resid_half = grad_resid.astype(jnp.bfloat16)
        out_part = jnp.dot(att_block.T, resid_half, preferred_element_type=jnp.float32)
        grad_attended = jnp.dot(resid_half, out_half.T, preferred_element_type=jnp.float32).astype(jnp.bfloat16)
        return (output, grad_resid, grad_attended, down_part, wide_part, out_part, gain_two_part)
    output, grad_resid, grad_attended, down_parts, wide_parts, out_parts, gain_two_parts = lax.map(middle, jnp.arange(blocks, dtype=jnp.int32))
    output = output.reshape(TOKENS, D)
    grad_resid = grad_resid.reshape(TOKENS, D)
    grad_attended = grad_attended.reshape(TOKENS, D)
    down_grad = lax.optimization_barrier(jnp.sum(down_parts, axis=0))
    wide_grad = lax.optimization_barrier(jnp.sum(wide_parts, axis=0))
    out_grad = lax.optimization_barrier(jnp.sum(out_parts, axis=0))
    gain_second_grad = lax.optimization_barrier(jnp.sum(gain_two_parts, axis=0))

    def back_step(accum, block_index):
        first_row, query_block, win_keys, win_values, key_mask = window_of(block_index)
        att_block = lax.dynamic_slice_in_dim(attended, first_row, query_rows, 0).reshape(query_rows, heads, HEAD_DIM)
        grad_block = lax.dynamic_slice_in_dim(grad_attended, first_row, query_rows, 0).reshape(query_rows, heads, HEAD_DIM)
        log_norm = log_norms[block_index]
        grad_query, grad_key, grad_value = attend_backward(query_block, win_keys, win_values, key_mask, log_norm, att_block, grad_block)
        grad_window = jnp.concatenate([grad_key.reshape(key_span, D), grad_value.reshape(key_span, D)], axis=1)
        current = lax.dynamic_slice_in_dim(accum, first_row, key_span, 0)
        accum = lax.dynamic_update_slice_in_dim(accum, current + grad_window, first_row, 0)
        return (accum, grad_query.reshape(query_rows, D))
    accum, grad_queries = lax.scan(back_step, jnp.zeros((TOKENS + 2 * LMAX, 2 * D), jnp.float32), jnp.arange(query_blocks, dtype=jnp.int32))
    pair_grad = accum[LMAX:LMAX + TOKENS]
    grad_queries = grad_queries.reshape(TOKENS, D)

    def rear(block_index):
        first_row = (block_index * block_rows).astype(jnp.int32)
        row_block = lax.dynamic_slice_in_dim(stream, first_row, block_rows, 0)
        cos_block = lax.dynamic_slice_in_dim(cosine, first_row, block_rows, 0)
        sin_block = lax.dynamic_slice_in_dim(sine_table, first_row, block_rows, 0)
        query_grad_block = lax.dynamic_slice_in_dim(grad_queries, first_row, block_rows, 0)
        pair_block = lax.dynamic_slice_in_dim(pair_grad, first_row, block_rows, 0)
        resid_block = lax.dynamic_slice_in_dim(grad_resid, first_row, block_rows, 0)
        normed_block = lax.dynamic_slice_in_dim(normed_in, first_row, block_rows, 0)
        normed, row_scale = normalize(row_block)
        query_back = rotate(query_grad_block.reshape(block_rows, heads, HEAD_DIM), cos_block, sin_block, -1.0)
        key_back = rotate(pair_block[:, :D].reshape(block_rows, heads, HEAD_DIM), cos_block, sin_block, -1.0)
        grad_joined = jnp.concatenate([query_back.reshape(block_rows, D), key_back.reshape(block_rows, D), pair_block[:, D:]], axis=1).astype(jnp.bfloat16)
        joined_part = jnp.dot(normed_block.T, grad_joined, preferred_element_type=jnp.float32)
        grad_normed = jnp.dot(grad_joined, joined_half.T, preferred_element_type=jnp.float32)
        gain_one_part = lax.optimization_barrier(jnp.sum(grad_normed * normed, axis=0))
        stream_part = resid_block + norm_back(grad_normed * gain_one, normed, row_scale)
        return (stream_part, joined_part, gain_one_part)
    stream_grad, joined_parts, gain_one_parts = lax.map(rear, jnp.arange(blocks, dtype=jnp.int32))
    stream_grad = stream_grad.reshape(TOKENS, D)
    joined_grad = lax.optimization_barrier(jnp.sum(joined_parts, axis=0))
    gain_first_grad = lax.optimization_barrier(jnp.sum(gain_one_parts, axis=0))
    joined_new, joined_momentum_new, joined_variance_new = adam_step(joined_proj, joined_grad, joined_momentum, joined_variance, WEIGHT_DECAY)
    out_new, out_momentum_new, out_variance_new = adam_step(out_proj, out_grad, out_momentum, out_variance, WEIGHT_DECAY)
    wide_new, wide_momentum_new, wide_variance_new = adam_step(wide_proj, wide_grad, wide_momentum, wide_variance, WEIGHT_DECAY)
    down_new, down_momentum_new, down_variance_new = adam_step(down_proj, down_grad, down_momentum, down_variance, WEIGHT_DECAY)
    gain_first_new, gain_first_momentum_new, gain_first_variance_new = adam_step(gain_first, gain_first_grad, gain_first_momentum, gain_first_variance, 0.0)
    gain_second_new, gain_second_momentum_new, gain_second_variance_new = adam_step(gain_second, gain_second_grad, gain_second_momentum, gain_second_variance, 0.0)
    return (output, stream_grad, joined_grad, out_grad, wide_grad, down_grad, gain_first_grad, gain_second_grad, joined_new, out_new, wide_new, down_new, gain_first_new, gain_second_new, joined_momentum_new, out_momentum_new, wide_momentum_new, down_momentum_new, gain_first_momentum_new, gain_second_momentum_new, joined_variance_new, out_variance_new, wide_variance_new, down_variance_new, gain_first_variance_new, gain_second_variance_new)
```

```python
import functools
import math

import jax
import jax.numpy as jnp
from jax import lax
from jax.experimental import pallas as pl
from jax.experimental.pallas import tpu as pltpu
from jax.sharding import PartitionSpec as P

HEAD_DIM = 64
LMAX = 1024
STEP = 4
GAIN_PAD = 384
OUT_PAD = 128


EPSILON = 1e-05
ROPE_BASE = 160000.0
LEARN_RATE = 0.02
BETA_ONE = 0.9
BETA_TWO = 0.98
ADAM_EPSILON = 1e-06
WEIGHT_DECAY = 0.1
NEG_LARGE = -1e30
MESH = pl.DeviceIdType.MESH


def extended(x, sides, width):
    for axis, dim in sides:
        peers, length = (lax.axis_size(axis), x.shape[dim])
        up = [(i, (i + 1) % peers) for i in range(peers - 1)]
        down = [(j, i) for i, j in up]
        last = lax.slice_in_dim(x, length - width, length, axis=dim)
        initial = lax.slice_in_dim(x, 0, width, axis=dim)
        before = lax.ppermute(last, axis, up)
        after = lax.ppermute(initial, axis, down)
        x = jnp.concatenate([before, x, after], axis=dim)
    return x


def normalize(values):
    centred = values - jnp.mean(values, axis=1, keepdims=True)
    row_scale = lax.rsqrt(jnp.mean(centred * centred, axis=1, keepdims=True) + EPSILON)
    return (centred * row_scale, row_scale)


def norm_back(grad_hat, normed, row_scale):
    mean_one = jnp.mean(grad_hat, axis=1, keepdims=True)
    mean_two = jnp.mean(grad_hat * normed, axis=1, keepdims=True)
    return row_scale * (grad_hat - mean_one - normed * mean_two)


def rope_tables(positions):
    half_dim = HEAD_DIM // 2
    freqs = jnp.exp(
        jnp.arange(half_dim, dtype=jnp.float32) * (-2.0 * math.log(ROPE_BASE) / HEAD_DIM)
    )
    angles = positions.astype(jnp.float32)[:, None] * freqs[None, :]
    return (jnp.cos(angles), jnp.sin(angles))


def rotate(values, cosine, sine_table, sign):
    half_dim = values.shape[-1] // 2
    front_half = values[..., :half_dim]
    second = values[..., half_dim:]
    cos_part = cosine[:, None, :]
    sin_part = sine_table[:, None, :] * sign
    return jnp.concatenate(
        [front_half * cos_part - second * sin_part, second * cos_part + front_half * sin_part],
        axis=-1,
    )


def gelu_parts(inner_part):
    cdf_part = 0.5 * (1.0 + lax.erf(inner_part * (1.0 / math.sqrt(2.0))))
    activation = inner_part * cdf_part
    gelu_slope = cdf_part + inner_part * jnp.exp(-0.5 * inner_part * inner_part) * (
        1.0 / math.sqrt(2.0 * math.pi)
    )
    return (activation, gelu_slope)


def score_block(queries, win_keys, key_mask):
    scores = jnp.einsum(
        "rhd,khd->hrk", queries, win_keys, preferred_element_type=jnp.float32
    ) * HEAD_DIM ** (-0.5)
    return jnp.where(key_mask[None], scores, NEG_LARGE)


def attend_forward(queries, win_keys, win_values, key_mask):
    scores = score_block(queries, win_keys, key_mask)
    row_peak = jnp.max(scores, axis=2, keepdims=True)
    sum_exp = jnp.sum(jnp.exp(scores - row_peak), axis=2, keepdims=True)
    log_norm = row_peak + jnp.log(sum_exp)
    prob_round = jnp.exp(scores - log_norm).astype(jnp.bfloat16)
    mixed = jnp.einsum("hrk,khd->rhd", prob_round, win_values, preferred_element_type=jnp.float32)
    return (mixed, log_norm[..., 0])


def attend_backward(queries, win_keys, win_values, key_mask, log_norm, attended, grad_attended):
    scores = score_block(queries, win_keys, key_mask)
    probs = jnp.exp(scores - log_norm[..., None])
    prob_round = probs.astype(jnp.bfloat16)
    grad_prob = jnp.einsum(
        "rhd,khd->hrk", grad_attended, win_values, preferred_element_type=jnp.float32
    )
    row_delta = jnp.sum(grad_attended.astype(jnp.float32) * attended.astype(jnp.float32), axis=2).T
    grad_score = (probs * (grad_prob - row_delta[..., None])).astype(jnp.bfloat16)
    grad_query = jnp.einsum(
        "hrk,khd->rhd", grad_score, win_keys, preferred_element_type=jnp.float32
    ) * HEAD_DIM ** (-0.5)
    grad_key = jnp.einsum(
        "hrk,rhd->khd", grad_score, queries, preferred_element_type=jnp.float32
    ) * HEAD_DIM ** (-0.5)
    grad_value = jnp.einsum(
        "hrk,rhd->khd", prob_round, grad_attended, preferred_element_type=jnp.float32
    )
    return (grad_query, grad_key, grad_value)


def adam_step(weight, gradient, momentum, variance, decay_rate):
    new_momentum = BETA_ONE * momentum + (1.0 - BETA_ONE) * gradient
    new_variance = BETA_TWO * variance + (1.0 - BETA_TWO) * gradient * gradient
    update = (
        new_momentum
        / (1.0 - BETA_ONE**STEP)
        / (jnp.sqrt(new_variance / (1.0 - BETA_TWO**STEP)) + ADAM_EPSILON)
    )
    return (weight - LEARN_RATE * (update + decay_rate * weight), new_momentum, new_variance)


def grid_place(peers, groups):
    place, member = lax.axis_index("dp"), lax.axis_index("group")
    parity = lax.rem(place, 2)
    bits = []
    power = 2
    while power < peers:
        bits.append((1 - 2 * lax.rem(place // power, 2)) * power)
        power *= 2
    hops = [(1 - parity) * a + parity * b for a, b in zip(bits, reversed(bits))]
    return place, member, hops, 1 - 2 * parity


def combos(count):
    return [tuple((i >> p) & 1 for p in range(count)) for i in range(2**count)]


def offset(combo, hops):
    total = 0
    for taken, hop in zip(combo, hops):
        if taken:
            total = total + hop
    return total


def meet(place, member, hops, last, groups):
    barrier = pltpu.get_barrier_semaphore()
    for step in range(1, groups):
        pl.semaphore_signal(
            barrier, inc=1, device_id=(place, lax.rem(member + step, groups)), device_id_type=MESH
        )
    for hop in list(hops) + [last]:
        pl.semaphore_signal(barrier, inc=1, device_id=(place + hop, member), device_id_type=MESH)
    pl.semaphore_wait(barrier, groups - 1 + len(hops) + 1)


def pieces(widths, largest=2688):
    found = []
    for a, width in enumerate(widths):
        if width <= largest or width % 128:
            found.append((a, 0, width))
            continue
        parts = -(-width // largest)
        part = -(-width // (128 * parts)) * 128
        for lo in range(0, width, part):
            found.append((a, lo, min(part, width - lo)))
    return tuple(found)


def gather_kernel(peers, groups, chunks, count, *refs):
    ins, outs = refs[:count], refs[count : 2 * count]
    send_sem, recv_sem, own_sem = refs[2 * count :]
    place, member, hops, last = grid_place(peers, groups)
    meet(place, member, hops, last, groups)
    phases = len(hops)
    n_chunks = len(chunks)

    def copy(src, dst, k, slot, device):
        return pltpu.make_async_remote_copy(
            src_ref=src, dst_ref=dst, send_sem=send_sem.at[k, slot], recv_sem=recv_sem.at[k, slot],
            device_id=device, device_id_type=MESH,
        )

    flight = []
    first, own = [], []
    for k, (a, lo, width) in enumerate(chunks):
        rows = ins[a].shape[0]
        mine = outs[a].at[pl.ds((place * groups + member) * rows, rows), pl.ds(lo, width)]
        src = ins[a].at[:, pl.ds(lo, width)]
        row = []
        for step in range(1, groups):
            c = copy(src, mine, k, step - 1, (place, lax.rem(member + step, groups)))
            c.start()
            row.append(c)
        keep = pltpu.make_async_copy(src, mine, own_sem.at[k])
        keep.start()
        first.append(row)
        own.append(keep)

    def block(k, combo):
        a, lo, width = chunks[k]
        rows = ins[a].shape[0] * groups
        at = (place + offset(combo, hops)) * rows
        return outs[a].at[pl.ds(at, rows), pl.ds(lo, width)]

    base = groups - 1
    pending = [dict() for _ in range(n_chunks)]

    def launch(k, combo):
        done = max([p + 1 for p, taken in enumerate(combo) if taken], default=0)
        ref = block(k, combo)
        for p in range(done, phases):
            slot = base + sum(2**q for q in range(p)) + sum(t << q for q, t in enumerate(combo[:p]))
            c = copy(ref, ref, k, slot, (place + hops[p], member))
            c.start()
            pending[k].setdefault(p, []).append((c, combo))
        slot = base + (2**phases - 1) + sum(t << q for q, t in enumerate(combo))
        c = copy(ref, ref, k, slot, (place + last, member))
        c.start()
        pending[k].setdefault(phases, []).append((c, combo))

    for step in range(n_chunks + phases):
        for level in range(phases + 1):
            k = step - level
            if not 0 <= k < n_chunks:
                continue
            if level == 0:
                for c in first[k]:
                    c.wait_recv()
                own[k].wait()
                launch(k, (0,) * phases)
            else:
                p = level - 1
                for c, combo in pending[k][p]:
                    c.wait_recv()
                    launch(k, tuple(1 if q == p else t for q, t in enumerate(combo)))
    for k in range(n_chunks):
        for c, _ in pending[k][phases]:
            c.wait_recv()
    for k in range(n_chunks):
        for c in first[k]:
            c.wait_send()
        for p in pending[k]:
            for c, _ in pending[k][p]:
                c.wait_send()


def gather_all(arrays, chunks, collective_id):
    peers, groups = lax.axis_size("dp"), lax.axis_size("group")
    phases = peers.bit_length() - 2
    slots = groups - 1 + 2 ** (phases + 1) - 1
    return pl.pallas_call(
        functools.partial(gather_kernel, peers, groups, chunks, len(arrays)),
        out_shape=[
            jax.ShapeDtypeStruct((a.shape[0] * peers * groups, a.shape[1]), a.dtype) for a in arrays
        ],
        in_specs=[pl.BlockSpec(memory_space=pl.ANY)] * len(arrays),
        out_specs=[pl.BlockSpec(memory_space=pl.ANY)] * len(arrays),
        scratch_shapes=[
            pltpu.SemaphoreType.DMA((len(chunks), slots)),
            pltpu.SemaphoreType.DMA((len(chunks), slots)),
            pltpu.SemaphoreType.DMA((len(chunks),)),
        ],
        compiler_params=pltpu.CompilerParams(collective_id=collective_id, has_side_effects=True),
    )(*arrays)


def scatter_kernel(peers, groups, chunks, count, phases, *refs):
    ins, outs = refs[:count], refs[count : 2 * count]
    n_chunks = len(chunks)
    rest = list(refs[2 * count :])
    send_sem, recv_sem, own_sem = rest[-3:]
    mine, from_core, from_group = (rest[i * n_chunks : (i + 1) * n_chunks] for i in range(3))
    from_hops = [rest[(3 + p) * n_chunks : (4 + p) * n_chunks] for p in range(phases)]
    place, member, hops, last = grid_place(peers, groups)
    meet(place, member, hops, last, groups)
    every = combos(phases)
    rows = mine[0].shape[1]
    shard = rows // groups
    tile = 16

    def copy(src, dst, k, slot, device):
        return pltpu.make_async_remote_copy(
            src_ref=src, dst_ref=dst, send_sem=send_sem.at[k, slot], recv_sem=recv_sem.at[k, slot],
            device_id=device, device_id_type=MESH,
        )

    def number(combo):
        return sum(t << q for q, t in enumerate(combo))

    def add_rows(target, source, at):
        def body(i, carry):
            span = pl.ds(pl.multiple_of(i * tile, tile), tile)
            total = target[at, span].astype(jnp.float32) + source[at, span].astype(jnp.float32)
            target[at, span] = total.astype(target.dtype)
            return carry

        lax.fori_loop(0, rows // tile, body, 0)

    core_copies, own_copies = [], []
    for k, (a, lo, width) in enumerate(chunks):
        cols = pl.ds(lo, width)
        sent, kept = [], []
        for combo in every:
            s = number(combo)
            theirs = place + last + offset(combo, hops[::-1])
            c = copy(
                ins[a].at[pl.ds(theirs * rows, rows), cols], from_core[k].at[s], k, s,
                (place + last, member),
            )
            c.start()
            sent.append(c)
            ours = place + offset(combo, hops)
            c = pltpu.make_async_copy(
                ins[a].at[pl.ds(ours * rows, rows), cols], mine[k].at[s], own_sem.at[k, s]
            )
            c.start()
            kept.append(c)
        core_copies.append(sent)
        own_copies.append(kept)

    hop_copies = [[[] for _ in range(phases)] for _ in range(n_chunks)]
    group_copies = [[] for _ in range(n_chunks)]

    def send_on(k, p):
        if p < 0:
            for step in range(1, groups):
                to = lax.rem(member + step, groups)
                c = copy(
                    mine[k].at[0, pl.ds(pl.multiple_of(to * shard, shard), shard)],
                    from_group[k].at[step - 1],
                    k, 2 ** (phases + 1) - 1 + step - 1, (place, to),
                )
                c.start()
                group_copies[k].append(c)
            return
        base = 2**phases + sum(2**q for q in range(p))
        for combo in combos(p):
            s = number(combo)
            c = copy(
                mine[k].at[s + 2**p], from_hops[p][k].at[s], k, base + s,
                (place + hops[p], member),
            )
            c.start()
            hop_copies[k][p].append(c)

    for step in range(n_chunks + phases + 1):
        for level in range(phases + 2):
            k = step - level
            if not 0 <= k < n_chunks:
                continue
            a, lo, width = chunks[k]
            if level == 0:
                for combo in every:
                    s = number(combo)
                    core_copies[k][s].wait_recv()
                    own_copies[k][s].wait()
                    add_rows(mine[k], from_core[k], s)
                send_on(k, phases - 1)
            elif level <= phases:
                p = phases - level
                for s, c in enumerate(hop_copies[k][p]):
                    c.wait_recv()
                    add_rows(mine[k], from_hops[p][k], s)
                send_on(k, p - 1)
            else:
                for c in group_copies[k]:
                    c.wait_recv()
                own = pl.ds(pl.multiple_of(member * shard, shard), shard)
                total = mine[k][0, own].astype(jnp.float32)
                for step_in in range(groups - 1):
                    total = total + from_group[k][step_in].astype(jnp.float32)
                outs[a][:, pl.ds(lo, width)] = total
    for k in range(n_chunks):
        for c in core_copies[k] + group_copies[k]:
            c.wait_send()
        for p in range(phases):
            for c in hop_copies[k][p]:
                c.wait_send()


def scatter_all(arrays, chunks, collective_id):
    peers, groups = lax.axis_size("dp"), lax.axis_size("group")
    phases = peers.bit_length() - 2
    slots = groups - 1 + 2 ** (phases + 1) - 1
    rows = arrays[0].shape[0] // peers
    shard = rows // groups
    kind = arrays[0].dtype
    return pl.pallas_call(
        functools.partial(scatter_kernel, peers, groups, chunks, len(arrays), phases),
        out_shape=[jax.ShapeDtypeStruct((shard, a.shape[1]), jnp.float32) for a in arrays],
        in_specs=[pl.BlockSpec(memory_space=pl.ANY)] * len(arrays),
        out_specs=[pl.BlockSpec(memory_space=pltpu.VMEM)] * len(arrays),
        scratch_shapes=[
            pltpu.VMEM((depth, height, width), kind)
            for depth, height in [(2**phases, rows)] * 2
            + [(groups - 1, shard)]
            + [(2**p, rows) for p in range(phases)]
            for _, _, width in chunks
        ]
        + [
            pltpu.SemaphoreType.DMA((len(chunks), slots)),
            pltpu.SemaphoreType.DMA((len(chunks), slots)),
            pltpu.SemaphoreType.DMA((len(chunks), 2**phases)),
        ],
        compiler_params=pltpu.CompilerParams(
            collective_id=collective_id, has_side_effects=True, vmem_limit_bytes=60 * 2**20
        ),
    )(*arrays)


def with_column(matrix, column, extra):
    return jnp.concatenate([matrix, jnp.pad(column[:, None], ((0, 0), (0, extra - 1)))], axis=1)


def on_device(
    stream,
    cotangent,
    bounds,
    joined_proj,
    out_proj,
    wide_proj,
    down_proj,
    gain_first,
    gain_second,
    joined_momentum,
    out_momentum,
    wide_momentum,
    down_momentum,
    gain_first_momentum,
    gain_second_momentum,
    joined_variance,
    out_variance,
    wide_variance,
    down_variance,
    gain_first_variance,
    gain_second_variance,
):
    row_count = stream.shape[0]
    width = stream.shape[1]
    heads = width // HEAD_DIM
    both = ("dp", "group")
    gains = jnp.stack([gain_first, gain_second], axis=1)
    gains = jnp.pad(gains, ((0, 0), (0, GAIN_PAD - 2)))
    joined_gains = jnp.concatenate([joined_proj, gains], axis=1).astype(jnp.bfloat16)
    joined_gains, out_half, wide_half, down_half = gather_all(
        [
            joined_gains,
            out_proj.astype(jnp.bfloat16),
            wide_proj.astype(jnp.bfloat16),
            down_proj.astype(jnp.bfloat16),
        ],
        pieces([joined_gains.shape[1], width, wide_proj.shape[1], down_proj.shape[1]]),
        1,
    )
    joined_half = joined_gains[:, : 3 * width]
    gain_one_half = joined_gains[:, 3 * width]
    gain_two_half = joined_gains[:, 3 * width + 1]
    gain_one = gain_one_half.astype(jnp.float32)
    gain_two = gain_two_half.astype(jnp.float32)
    ff_width = down_half.shape[1]
    first_row = lax.axis_index(("dp", "group")) * row_count
    token_index = first_row + jnp.arange(row_count, dtype=jnp.int32)
    seq_starts = bounds[:, 0]
    seq_ends = bounds[:, 1]
    cosine, sine_table = rope_tables(token_index - seq_starts)
    normed_one, scale_one = normalize(stream)
    normed_in = (normed_one * gain_one).astype(jnp.bfloat16)
    joined_act = jnp.dot(normed_in, joined_half, preferred_element_type=jnp.float32)
    queries = rotate(
        joined_act[:, :width].reshape(row_count, heads, HEAD_DIM), cosine, sine_table, 1.0
    ).astype(jnp.bfloat16)
    own_keys = rotate(
        joined_act[:, width : 2 * width].reshape(row_count, heads, HEAD_DIM),
        cosine,
        sine_table,
        1.0,
    )
    pairs = jnp.concatenate(
        [
            own_keys.astype(jnp.bfloat16).reshape(row_count, width),
            joined_act[:, 2 * width :].astype(jnp.bfloat16),
        ],
        axis=1,
    )
    key_span = row_count + 2 * LMAX
    group_block = lax.all_gather(pairs, "group", axis=0, tiled=True)
    padded = extended(group_block, (("dp", 0),), LMAX)
    window = lax.dynamic_slice_in_dim(padded, lax.axis_index("group") * row_count, key_span, 0)
    key_index = first_row - LMAX + jnp.arange(key_span, dtype=jnp.int32)
    key_mask = (key_index[None, :] >= seq_starts[:, None]) & (
        key_index[None, :] < seq_ends[:, None]
    )
    win_keys = window[:, :width].reshape(key_span, heads, HEAD_DIM)
    win_values = window[:, width:].reshape(key_span, heads, HEAD_DIM)
    mixed_parts = []
    norm_parts = []
    for head_start in range(0, heads, 4):
        mixed, log_norm = attend_forward(
            queries[:, head_start : head_start + 4],
            win_keys[:, head_start : head_start + 4],
            win_values[:, head_start : head_start + 4],
            key_mask,
        )
        mixed_parts.append(mixed)
        norm_parts.append(log_norm)
    attended = jnp.concatenate(mixed_parts, axis=1).astype(jnp.bfloat16).reshape(row_count, width)
    residual = stream + jnp.dot(attended, out_half, preferred_element_type=jnp.float32)
    normed_two, scale_two = normalize(residual)
    hidden_in = (normed_two * gain_two).astype(jnp.bfloat16)
    wide_act = jnp.dot(hidden_in, wide_half, preferred_element_type=jnp.float32)
    inner_part = wide_act[:, :ff_width]
    gate_part = wide_act[:, ff_width:]
    activation, gelu_slope = gelu_parts(inner_part)
    gated = (activation * gate_part).astype(jnp.bfloat16)
    output = residual + jnp.einsum(
        "rf,df->rd", gated, down_half, preferred_element_type=jnp.float32
    )
    cot_half = cotangent.astype(jnp.bfloat16)
    down_local = jnp.einsum("rd,rf->df", cot_half, gated, preferred_element_type=jnp.float32)
    grad_gated = jnp.dot(cot_half, down_half, preferred_element_type=jnp.float32)
    grad_inner = (grad_gated * gate_part * gelu_slope).astype(jnp.bfloat16)
    grad_gate = (grad_gated * activation).astype(jnp.bfloat16)
    grad_wide = jnp.concatenate([grad_inner, grad_gate], axis=1)
    inner_local = jnp.einsum("rd,rf->df", hidden_in, grad_inner, preferred_element_type=jnp.float32)
    gate_local = jnp.einsum("rd,rf->df", hidden_in, grad_gate, preferred_element_type=jnp.float32)
    grad_hidden = jnp.einsum("rf,df->rd", grad_wide, wide_half, preferred_element_type=jnp.float32)
    gain_two_local = jnp.sum(grad_hidden * normed_two, axis=0)
    grad_resid = cotangent + norm_back(grad_hidden * gain_two, normed_two, scale_two)
    resid_half = grad_resid.astype(jnp.bfloat16)
    out_local = jnp.einsum("rd,re->de", attended, resid_half, preferred_element_type=jnp.float32)
    out_local = with_column(out_local, gain_two_local, OUT_PAD)
    grad_attended = jnp.einsum(
        "re,de->rd", resid_half, out_half, preferred_element_type=jnp.float32
    ).astype(jnp.bfloat16)
    attended_heads = attended.reshape(row_count, heads, HEAD_DIM)
    grad_heads = grad_attended.reshape(row_count, heads, HEAD_DIM)
    query_parts = []
    key_parts = []
    value_parts = []
    for part_index, head_start in enumerate(range(0, heads, 4)):
        grad_query, grad_key, grad_value = attend_backward(
            queries[:, head_start : head_start + 4],
            win_keys[:, head_start : head_start + 4],
            win_values[:, head_start : head_start + 4],
            key_mask,
            norm_parts[part_index],
            attended_heads[:, head_start : head_start + 4],
            grad_heads[:, head_start : head_start + 4],
        )
        query_parts.append(grad_query)
        key_parts.append(grad_key)
        value_parts.append(grad_value)
    grad_queries = jnp.concatenate(query_parts, axis=1)
    grad_window = jnp.concatenate(
        [
            jnp.concatenate(key_parts, axis=1).reshape(key_span, width),
            jnp.concatenate(value_parts, axis=1).reshape(key_span, width),
        ],
        axis=1,
    )
    block_rows = row_count * lax.axis_size("group")
    holder = jnp.zeros((block_rows + 2 * LMAX, 2 * width), jnp.bfloat16)
    holder = lax.dynamic_update_slice_in_dim(
        holder, grad_window.astype(jnp.bfloat16), lax.axis_index("group") * row_count, 0
    )
    rim_rows = jnp.concatenate([holder[:LMAX], holder[block_rows + LMAX :]], axis=0)
    moved = extended(rim_rows, (("dp", 0),), LMAX).astype(jnp.float32)
    centre = holder[LMAX : LMAX + block_rows].astype(jnp.float32)
    centre = centre.at[:LMAX].add(moved[:LMAX])
    centre = centre.at[block_rows - LMAX :].add(moved[3 * LMAX :])
    pair_grad = lax.psum_scatter(
        centre.astype(jnp.bfloat16), "group", scatter_dimension=0, tiled=True
    ).astype(jnp.float32)
    query_back = rotate(grad_queries, cosine, sine_table, -1.0).reshape(row_count, width)
    key_back = rotate(
        pair_grad[:, :width].reshape(row_count, heads, HEAD_DIM), cosine, sine_table, -1.0
    )
    grad_joined = jnp.concatenate(
        [query_back, key_back.reshape(row_count, width), pair_grad[:, width:]], axis=1
    ).astype(jnp.bfloat16)
    joined_local = jnp.einsum(
        "rd,re->de", normed_in, grad_joined, preferred_element_type=jnp.float32
    )
    grad_normed = jnp.einsum(
        "re,de->rd", grad_joined, joined_half, preferred_element_type=jnp.float32
    )
    gain_one_local = jnp.sum(grad_normed * normed_one, axis=0)
    stream_grad = grad_resid + norm_back(grad_normed * gain_one, normed_one, scale_one)
    joined_local = with_column(joined_local, gain_one_local, GAIN_PAD)
    locals_half = [
        v.astype(jnp.bfloat16)
        for v in (down_local, inner_local, gate_local, out_local, joined_local)
    ]
    down_sum, inner_sum, gate_sum, out_sum, joined_sum = scatter_all(
        locals_half, pieces([v.shape[1] for v in locals_half]), 2
    )
    joined_grad = joined_sum[:, : 3 * width]
    gain_first_grad = joined_sum[:, 3 * width]
    out_grad = out_sum[:, :width]
    gain_second_grad = out_sum[:, width]
    wide_grad = jnp.concatenate([inner_sum, gate_sum], axis=1)
    down_grad = down_sum
    joined_new, joined_momentum_new, joined_variance_new = adam_step(
        joined_proj, joined_grad, joined_momentum, joined_variance, WEIGHT_DECAY
    )
    out_new, out_momentum_new, out_variance_new = adam_step(
        out_proj, out_grad, out_momentum, out_variance, WEIGHT_DECAY
    )
    wide_new, wide_momentum_new, wide_variance_new = adam_step(
        wide_proj, wide_grad, wide_momentum, wide_variance, WEIGHT_DECAY
    )
    down_new, down_momentum_new, down_variance_new = adam_step(
        down_proj, down_grad, down_momentum, down_variance, WEIGHT_DECAY
    )
    gain_first_new, gain_first_momentum_new, gain_first_variance_new = adam_step(
        gain_first, gain_first_grad, gain_first_momentum, gain_first_variance, 0.0
    )
    gain_second_new, gain_second_momentum_new, gain_second_variance_new = adam_step(
        gain_second, gain_second_grad, gain_second_momentum, gain_second_variance, 0.0
    )
    return (
        output,
        stream_grad,
        joined_grad,
        out_grad,
        wide_grad,
        down_grad,
        gain_first_grad,
        gain_second_grad,
        joined_new,
        out_new,
        wide_new,
        down_new,
        gain_first_new,
        gain_second_new,
        joined_momentum_new,
        out_momentum_new,
        wide_momentum_new,
        down_momentum_new,
        gain_first_momentum_new,
        gain_second_momentum_new,
        joined_variance_new,
        out_variance_new,
        wide_variance_new,
        down_variance_new,
        gain_first_variance_new,
        gain_second_variance_new,
    )


def solution(mesh):
    placed = (
        P(("dp", "group"), None),
        P(("dp", "group"), None),
        P(("dp", "group"), None),
        P(("dp", "group"), None),
        P(("dp", "group"), None),
        P(("dp", "group"), None),
        P(("dp", "group"), None),
        P(("dp", "group")),
        P(("dp", "group")),
        P(("dp", "group"), None),
        P(("dp", "group"), None),
        P(("dp", "group"), None),
        P(("dp", "group"), None),
        P(("dp", "group")),
        P(("dp", "group")),
        P(("dp", "group"), None),
        P(("dp", "group"), None),
        P(("dp", "group"), None),
        P(("dp", "group"), None),
        P(("dp", "group")),
        P(("dp", "group")),
    )
    return jax.shard_map(
        on_device,
        mesh=mesh,
        in_specs=placed,
        out_specs=(
            P(("dp", "group"), None),
            P(("dp", "group"), None),
            P(("dp", "group"), None),
            P(("dp", "group"), None),
            P(("dp", "group"), None),
            P(("dp", "group"), None),
            P(("dp", "group")),
            P(("dp", "group")),
            P(("dp", "group"), None),
            P(("dp", "group"), None),
            P(("dp", "group"), None),
            P(("dp", "group"), None),
            P(("dp", "group")),
            P(("dp", "group")),
            P(("dp", "group"), None),
            P(("dp", "group"), None),
            P(("dp", "group"), None),
            P(("dp", "group"), None),
            P(("dp", "group")),
            P(("dp", "group")),
            P(("dp", "group"), None),
            P(("dp", "group"), None),
            P(("dp", "group"), None),
            P(("dp", "group"), None),
            P(("dp", "group")),
            P(("dp", "group")),
        ),
        check_vma=False,
    )
```

```python
import functools
import math

import jax
import jax.numpy as jnp
from jax import lax
from jax.experimental import pallas as pl
from jax.experimental.pallas import tpu as pltpu
from jax.sharding import PartitionSpec as P

HEAD_DIM = 64
LMAX = 1024
STEP = 4
GAIN_PAD = 384
OUT_PAD = 128


EPSILON = 1e-05
ROPE_BASE = 160000.0
LEARN_RATE = 0.02
BETA_ONE = 0.9
BETA_TWO = 0.98
ADAM_EPSILON = 1e-06
WEIGHT_DECAY = 0.1
NEG_LARGE = -1e30
MESH = pl.DeviceIdType.MESH


def normalize(values):
    centred = values - jnp.mean(values, axis=1, keepdims=True)
    row_scale = lax.rsqrt(jnp.mean(centred * centred, axis=1, keepdims=True) + EPSILON)
    return (centred * row_scale, row_scale)


def norm_back(grad_hat, normed, row_scale):
    mean_one = jnp.mean(grad_hat, axis=1, keepdims=True)
    mean_two = jnp.mean(grad_hat * normed, axis=1, keepdims=True)
    return row_scale * (grad_hat - mean_one - normed * mean_two)


def rope_tables(positions):
    half_dim = HEAD_DIM // 2
    freqs = jnp.exp(
        jnp.arange(half_dim, dtype=jnp.float32) * (-2.0 * math.log(ROPE_BASE) / HEAD_DIM)
    )
    angles = positions.astype(jnp.float32)[:, None] * freqs[None, :]
    return (jnp.cos(angles), jnp.sin(angles))


def rotate(values, cosine, sine_table, sign):
    half_dim = values.shape[-1] // 2
    front_half = values[..., :half_dim]
    second = values[..., half_dim:]
    cos_part = cosine[:, None, :]
    sin_part = sine_table[:, None, :] * sign
    return jnp.concatenate(
        [front_half * cos_part - second * sin_part, second * cos_part + front_half * sin_part],
        axis=-1,
    )


def gelu_parts(inner_part):
    cdf_part = 0.5 * (1.0 + lax.erf(inner_part * (1.0 / math.sqrt(2.0))))
    activation = inner_part * cdf_part
    gelu_slope = cdf_part + inner_part * jnp.exp(-0.5 * inner_part * inner_part) * (
        1.0 / math.sqrt(2.0 * math.pi)
    )
    return (activation, gelu_slope)


def adam_step(weight, gradient, momentum, variance, decay_rate):
    new_momentum = BETA_ONE * momentum + (1.0 - BETA_ONE) * gradient
    new_variance = BETA_TWO * variance + (1.0 - BETA_TWO) * gradient * gradient
    update = (
        new_momentum
        / (1.0 - BETA_ONE**STEP)
        / (jnp.sqrt(new_variance / (1.0 - BETA_TWO**STEP)) + ADAM_EPSILON)
    )
    return (weight - LEARN_RATE * (update + decay_rate * weight), new_momentum, new_variance)


def grid_place(peers, groups):
    place, member = lax.axis_index("dp"), lax.axis_index("group")
    parity = lax.rem(place, 2)
    bits = []
    power = 2
    while power < peers:
        bits.append((1 - 2 * lax.rem(place // power, 2)) * power)
        power *= 2
    hops = [(1 - parity) * a + parity * b for a, b in zip(bits, reversed(bits))]
    return place, member, hops, 1 - 2 * parity


def combos(count):
    return [tuple((i >> p) & 1 for p in range(count)) for i in range(2**count)]


def offset(combo, hops):
    total = 0
    for taken, hop in zip(combo, hops):
        if taken:
            total = total + hop
    return total


def meet(place, member, hops, last, groups):
    barrier = pltpu.get_barrier_semaphore()
    for step in range(1, groups):
        pl.semaphore_signal(
            barrier, inc=1, device_id=(place, lax.rem(member + step, groups)), device_id_type=MESH
        )
    for hop in list(hops) + [last]:
        pl.semaphore_signal(barrier, inc=1, device_id=(place + hop, member), device_id_type=MESH)
    pl.semaphore_wait(barrier, groups - 1 + len(hops) + 1)


def pieces(widths, largest=2688):
    found = []
    for a, width in enumerate(widths):
        if width <= largest or width % 128:
            found.append((a, 0, width))
            continue
        parts = -(-width // largest)
        part = -(-width // (128 * parts)) * 128
        for lo in range(0, width, part):
            found.append((a, lo, min(part, width - lo)))
    return tuple(found)


def gather_kernel(peers, groups, chunks, count, *refs):
    ins, outs = refs[:count], refs[count : 2 * count]
    send_sem, recv_sem, own_sem = refs[2 * count :]
    place, member, hops, last = grid_place(peers, groups)
    meet(place, member, hops, last, groups)
    phases = len(hops)
    n_chunks = len(chunks)

    def copy(src, dst, k, slot, device):
        return pltpu.make_async_remote_copy(
            src_ref=src, dst_ref=dst, send_sem=send_sem.at[k, slot], recv_sem=recv_sem.at[k, slot],
            device_id=device, device_id_type=MESH,
        )

    flight = []
    first, own = [], []
    for k, (a, lo, width) in enumerate(chunks):
        rows = ins[a].shape[0]
        mine = outs[a].at[pl.ds((place * groups + member) * rows, rows), pl.ds(lo, width)]
        src = ins[a].at[:, pl.ds(lo, width)]
        row = []
        for step in range(1, groups):
            c = copy(src, mine, k, step - 1, (place, lax.rem(member + step, groups)))
            c.start()
            row.append(c)
        keep = pltpu.make_async_copy(src, mine, own_sem.at[k])
        keep.start()
        first.append(row)
        own.append(keep)

    def block(k, combo):
        a, lo, width = chunks[k]
        rows = ins[a].shape[0] * groups
        at = (place + offset(combo, hops)) * rows
        return outs[a].at[pl.ds(at, rows), pl.ds(lo, width)]

    base = groups - 1
    pending = [dict() for _ in range(n_chunks)]

    def launch(k, combo):
        done = max([p + 1 for p, taken in enumerate(combo) if taken], default=0)
        ref = block(k, combo)
        for p in range(done, phases):
            slot = base + sum(2**q for q in range(p)) + sum(t << q for q, t in enumerate(combo[:p]))
            c = copy(ref, ref, k, slot, (place + hops[p], member))
            c.start()
            pending[k].setdefault(p, []).append((c, combo))
        slot = base + (2**phases - 1) + sum(t << q for q, t in enumerate(combo))
        c = copy(ref, ref, k, slot, (place + last, member))
        c.start()
        pending[k].setdefault(phases, []).append((c, combo))

    for step in range(n_chunks + phases):
        for level in range(phases + 1):
            k = step - level
            if not 0 <= k < n_chunks:
                continue
            if level == 0:
                for c in first[k]:
                    c.wait_recv()
                own[k].wait()
                launch(k, (0,) * phases)
            else:
                p = level - 1
                for c, combo in pending[k][p]:
                    c.wait_recv()
                    launch(k, tuple(1 if q == p else t for q, t in enumerate(combo)))
    for k in range(n_chunks):
        for c, _ in pending[k][phases]:
            c.wait_recv()
    for k in range(n_chunks):
        for c in first[k]:
            c.wait_send()
        for p in pending[k]:
            for c, _ in pending[k][p]:
                c.wait_send()


def gather_all(arrays, chunks, collective_id):
    peers, groups = lax.axis_size("dp"), lax.axis_size("group")
    phases = peers.bit_length() - 2
    slots = groups - 1 + 2 ** (phases + 1) - 1
    return pl.pallas_call(
        functools.partial(gather_kernel, peers, groups, chunks, len(arrays)),
        out_shape=[
            jax.ShapeDtypeStruct((a.shape[0] * peers * groups, a.shape[1]), a.dtype) for a in arrays
        ],
        in_specs=[pl.BlockSpec(memory_space=pl.ANY)] * len(arrays),
        out_specs=[pl.BlockSpec(memory_space=pl.ANY)] * len(arrays),
        scratch_shapes=[
            pltpu.SemaphoreType.DMA((len(chunks), slots)),
            pltpu.SemaphoreType.DMA((len(chunks), slots)),
            pltpu.SemaphoreType.DMA((len(chunks),)),
        ],
        compiler_params=pltpu.CompilerParams(collective_id=collective_id, has_side_effects=True),
    )(*arrays)


def scatter_kernel(peers, groups, chunks, count, phases, *refs):
    ins, outs = refs[:count], refs[count : 2 * count]
    n_chunks = len(chunks)
    rest = list(refs[2 * count :])
    send_sem, recv_sem, own_sem = rest[-3:]
    mine, from_core, from_group = (rest[i * n_chunks : (i + 1) * n_chunks] for i in range(3))
    from_hops = [rest[(3 + p) * n_chunks : (4 + p) * n_chunks] for p in range(phases)]
    place, member, hops, last = grid_place(peers, groups)
    meet(place, member, hops, last, groups)
    every = combos(phases)
    rows = mine[0].shape[1]
    shard = rows // groups
    tile = 16

    def copy(src, dst, k, slot, device):
        return pltpu.make_async_remote_copy(
            src_ref=src, dst_ref=dst, send_sem=send_sem.at[k, slot], recv_sem=recv_sem.at[k, slot],
            device_id=device, device_id_type=MESH,
        )

    def number(combo):
        return sum(t << q for q, t in enumerate(combo))

    def add_rows(target, source, at):
        def body(i, carry):
            span = pl.ds(pl.multiple_of(i * tile, tile), tile)
            total = target[at, span].astype(jnp.float32) + source[at, span].astype(jnp.float32)
            target[at, span] = total.astype(target.dtype)
            return carry

        lax.fori_loop(0, rows // tile, body, 0)

    core_copies, own_copies = [], []
    for k, (a, lo, width) in enumerate(chunks):
        cols = pl.ds(lo, width)
        sent, kept = [], []
        for combo in every:
            s = number(combo)
            theirs = place + last + offset(combo, hops[::-1])
            c = copy(
                ins[a].at[pl.ds(theirs * rows, rows), cols], from_core[k].at[s], k, s,
                (place + last, member),
            )
            c.start()
            sent.append(c)
            ours = place + offset(combo, hops)
            c = pltpu.make_async_copy(
                ins[a].at[pl.ds(ours * rows, rows), cols], mine[k].at[s], own_sem.at[k, s]
            )
            c.start()
            kept.append(c)
        core_copies.append(sent)
        own_copies.append(kept)

    hop_copies = [[[] for _ in range(phases)] for _ in range(n_chunks)]
    group_copies = [[] for _ in range(n_chunks)]

    def send_on(k, p):
        if p < 0:
            for step in range(1, groups):
                to = lax.rem(member + step, groups)
                c = copy(
                    mine[k].at[0, pl.ds(pl.multiple_of(to * shard, shard), shard)],
                    from_group[k].at[step - 1],
                    k, 2 ** (phases + 1) - 1 + step - 1, (place, to),
                )
                c.start()
                group_copies[k].append(c)
            return
        base = 2**phases + sum(2**q for q in range(p))
        for combo in combos(p):
            s = number(combo)
            c = copy(
                mine[k].at[s + 2**p], from_hops[p][k].at[s], k, base + s,
                (place + hops[p], member),
            )
            c.start()
            hop_copies[k][p].append(c)

    for step in range(n_chunks + phases + 1):
        for level in range(phases + 2):
            k = step - level
            if not 0 <= k < n_chunks:
                continue
            a, lo, width = chunks[k]
            if level == 0:
                for combo in every:
                    s = number(combo)
                    core_copies[k][s].wait_recv()
                    own_copies[k][s].wait()
                    add_rows(mine[k], from_core[k], s)
                send_on(k, phases - 1)
            elif level <= phases:
                p = phases - level
                for s, c in enumerate(hop_copies[k][p]):
                    c.wait_recv()
                    add_rows(mine[k], from_hops[p][k], s)
                send_on(k, p - 1)
            else:
                for c in group_copies[k]:
                    c.wait_recv()
                own = pl.ds(pl.multiple_of(member * shard, shard), shard)
                total = mine[k][0, own].astype(jnp.float32)
                for step_in in range(groups - 1):
                    total = total + from_group[k][step_in].astype(jnp.float32)
                outs[a][:, pl.ds(lo, width)] = total
    for k in range(n_chunks):
        for c in core_copies[k] + group_copies[k]:
            c.wait_send()
        for p in range(phases):
            for c in hop_copies[k][p]:
                c.wait_send()


def scatter_all(arrays, chunks, collective_id):
    peers, groups = lax.axis_size("dp"), lax.axis_size("group")
    phases = peers.bit_length() - 2
    slots = groups - 1 + 2 ** (phases + 1) - 1
    rows = arrays[0].shape[0] // peers
    shard = rows // groups
    kind = arrays[0].dtype
    return pl.pallas_call(
        functools.partial(scatter_kernel, peers, groups, chunks, len(arrays), phases),
        out_shape=[jax.ShapeDtypeStruct((shard, a.shape[1]), jnp.float32) for a in arrays],
        in_specs=[pl.BlockSpec(memory_space=pl.ANY)] * len(arrays),
        out_specs=[pl.BlockSpec(memory_space=pltpu.VMEM)] * len(arrays),
        scratch_shapes=[
            pltpu.VMEM((depth, height, width), kind)
            for depth, height in [(2**phases, rows)] * 2
            + [(groups - 1, shard)]
            + [(2**p, rows) for p in range(phases)]
            for _, _, width in chunks
        ]
        + [
            pltpu.SemaphoreType.DMA((len(chunks), slots)),
            pltpu.SemaphoreType.DMA((len(chunks), slots)),
            pltpu.SemaphoreType.DMA((len(chunks), 2**phases)),
        ],
        compiler_params=pltpu.CompilerParams(
            collective_id=collective_id, has_side_effects=True, vmem_limit_bytes=60 * 2**20
        ),
    )(*arrays)


def window_kernel(peers, groups, halo, rows, *refs):
    pack, marks, window, marks_all, send_sem, recv_sem, own_sem = refs
    place, member = lax.axis_index("dp"), lax.axis_index("group")
    slab = pack.shape[1] // groups
    third = slab // 3
    block = rows * groups
    has_up = place < peers - 1
    has_down = place > 0

    barrier = pltpu.get_barrier_semaphore()
    for step in range(1, groups):
        pl.semaphore_signal(
            barrier, inc=1, device_id=(place, lax.rem(member + step, groups)), device_id_type=MESH
        )
    for near, there in ((1, has_up), (-1, has_down)):

        @pl.when(there)
        def _():
            pl.semaphore_signal(
                barrier, inc=1, device_id=(place + near, member), device_id_type=MESH
            )

    sides = (place + peers - 1) // peers + 1 - place // (peers - 1)
    pl.semaphore_wait(barrier, groups - 1 + sides)

    def columns(of):
        return pl.ds(pl.multiple_of(of * slab, slab), slab)

    def copy(src, dst, slot, device):
        return pltpu.make_async_remote_copy(
            src_ref=src, dst_ref=dst, send_sem=send_sem.at[slot], recv_sem=recv_sem.at[slot],
            device_id=device, device_id_type=MESH,
        )

    mine = window.at[pl.ds(halo + member * rows, rows), :]
    from_group = []
    for step in range(1, groups):
        to = lax.rem(member + step, groups)
        c = copy(pack.at[:, columns(to)], mine, step - 1, (place, to))
        c.start()
        m = copy(marks.at[...], marks_all.at[member], groups - 2 + step, (place, to))
        m.start()
        from_group.append((c, m))
    own = pltpu.make_async_copy(pack.at[:, columns(member)], mine, own_sem.at[0])
    own.start()
    own_marks = pltpu.make_async_copy(marks.at[...], marks_all.at[member], own_sem.at[1])
    own_marks.start()

    def halo_copies(step):
        of = lax.rem(member + groups - step, groups)
        src = window.at[pl.ds(halo + of * rows, rows), pl.ds(third, 2 * third)]
        up = copy(
            src, window.at[pl.ds(of * rows + halo - block, rows), pl.ds(third, 2 * third)],
            2 * groups - 2 + step, (place + 1, member),
        ) if halo == block else None
        down = copy(
            src, window.at[pl.ds(halo + block + of * rows, rows), pl.ds(third, 2 * third)],
            3 * groups - 2 + step, (place - 1, member),
        ) if halo == block else None
        return up, down

    if halo == block:
        moved = []
        for step in range(groups):
            if step == 0:
                own.wait()
            else:
                from_group[step - 1][0].wait_recv()
            up, down = halo_copies(step)

            @pl.when(has_up)
            def _():
                up.start()

            @pl.when(has_down)
            def _():
                down.start()

            moved.append((up, down))
    else:
        own.wait()
        for c, _ in from_group:
            c.wait_recv()
        up = copy(
            window.at[pl.ds(block, halo), pl.ds(third, 2 * third)],
            window.at[pl.ds(0, halo), pl.ds(third, 2 * third)],
            2 * groups - 2, (place + 1, member),
        )
        down = copy(
            window.at[pl.ds(halo, halo), pl.ds(third, 2 * third)],
            window.at[pl.ds(halo + block, halo), pl.ds(third, 2 * third)],
            3 * groups - 2, (place - 1, member),
        )

        @pl.when(has_up)
        def _():
            up.start()

        @pl.when(has_down)
        def _():
            down.start()

        moved = [(up, down)]
    own_marks.wait()
    for c, m in from_group:
        m.wait_recv()
        c.wait_send()
        m.wait_send()
    for up, down in moved:

        @pl.when(has_up)
        def _():
            up.wait_send()
            down.wait_recv()

        @pl.when(has_down)
        def _():
            down.wait_send()
            up.wait_recv()


def window_of(pack, marks, halo, collective_id):
    peers, groups = lax.axis_size("dp"), lax.axis_size("group")
    rows = pack.shape[0]
    span = rows * groups + 2 * halo
    return pl.pallas_call(
        functools.partial(window_kernel, peers, groups, halo, rows),
        out_shape=[
            jax.ShapeDtypeStruct((span, pack.shape[1] // groups), pack.dtype),
            jax.ShapeDtypeStruct((groups, *marks.shape), marks.dtype),
        ],
        in_specs=[pl.BlockSpec(memory_space=pl.ANY)] * 2,
        out_specs=[pl.BlockSpec(memory_space=pl.ANY)] * 2,
        scratch_shapes=[
            pltpu.SemaphoreType.DMA((4 * groups,)),
            pltpu.SemaphoreType.DMA((4 * groups,)),
            pltpu.SemaphoreType.DMA((2,)),
        ],
        compiler_params=pltpu.CompilerParams(collective_id=collective_id, has_side_effects=True),
    )(pack, marks)


def swap_kernel(groups, to_heads, x, y, send_sem, recv_sem, own_sem):
    place, member = lax.axis_index("dp"), lax.axis_index("group")
    barrier = pltpu.get_barrier_semaphore()
    for step in range(1, groups):
        pl.semaphore_signal(
            barrier, inc=1, device_id=(place, lax.rem(member + step, groups)), device_id_type=MESH
        )
    pl.semaphore_wait(barrier, groups - 1)
    rows = x.shape[0] if to_heads else y.shape[0]
    slab = y.shape[1] if to_heads else x.shape[1]

    def ends(to):
        if to_heads:
            src = x.at[:, pl.ds(pl.multiple_of(to * slab, slab), slab)]
            return src, y.at[pl.ds(member * rows, rows), :]
        src = x.at[pl.ds(to * rows, rows), :]
        return src, y.at[:, pl.ds(pl.multiple_of(member * slab, slab), slab)]

    copies = []
    for step in range(1, groups):
        to = lax.rem(member + step, groups)
        src, dst = ends(to)
        c = pltpu.make_async_remote_copy(
            src_ref=src, dst_ref=dst, send_sem=send_sem.at[step - 1],
            recv_sem=recv_sem.at[step - 1], device_id=(place, to), device_id_type=MESH,
        )
        c.start()
        copies.append(c)
    own = pltpu.make_async_copy(*ends(member), own_sem.at[0])
    own.start()
    own.wait()
    for c in copies:
        c.wait()


def swap(x, to_heads, collective_id):
    groups = lax.axis_size("group")
    rows, columns = x.shape
    shape = (rows * groups, columns // groups) if to_heads else (rows // groups, columns * groups)
    return pl.pallas_call(
        functools.partial(swap_kernel, groups, to_heads),
        out_shape=jax.ShapeDtypeStruct(shape, x.dtype),
        in_specs=[pl.BlockSpec(memory_space=pl.ANY)],
        out_specs=pl.BlockSpec(memory_space=pl.ANY),
        scratch_shapes=[
            pltpu.SemaphoreType.DMA((groups - 1,)),
            pltpu.SemaphoreType.DMA((groups - 1,)),
            pltpu.SemaphoreType.DMA((1,)),
        ],
        compiler_params=pltpu.CompilerParams(collective_id=collective_id, has_side_effects=True),
    )(x)


KEY_TILE = 256
PAIR = 2 * HEAD_DIM


def dot(a, b):
    return jnp.dot(a, b, preferred_element_type=jnp.float32)


def dot_rows(a, b):
    return lax.dot_general(a, b, (((1,), (1,)), ((), ())), preferred_element_type=jnp.float32)


def only_head(values, which):
    lane = lax.broadcasted_iota(jnp.int32, values.shape, 1)
    inside = (lane >= which * HEAD_DIM) & (lane < (which + 1) * HEAD_DIM)
    return jnp.where(inside, values, jnp.zeros_like(values))


def inside_mask(marks_ref, tile, rows):
    key = tile * KEY_TILE + lax.broadcasted_iota(jnp.int32, (KEY_TILE, rows), 0)
    return (key >= marks_ref[0, 0:1, :]) & (key < marks_ref[0, 1:2, :])


def attend_kernel(halo, ranges, query_ref, window_ref, marks_ref, out_ref, norm_ref, peak, total, acc):
    block = pl.program_id(0)
    rows = query_ref.shape[0]
    heads = query_ref.shape[1] // 3 // HEAD_DIM
    third = heads * HEAD_DIM
    peak[...] = jnp.full_like(peak, NEG_LARGE)
    total[...] = jnp.zeros_like(total)
    acc[...] = jnp.zeros_like(acc)

    def step(tile, carry):
        keys_at = pl.ds(pl.multiple_of(tile * KEY_TILE, KEY_TILE), KEY_TILE)
        inside = inside_mask(marks_ref, tile, rows)
        for pair in range(heads // 2):
            lo = pair * PAIR
            keys = window_ref[keys_at, third + lo : third + lo + PAIR]
            values_t = window_ref[keys_at, 2 * third + lo : 2 * third + lo + PAIR].T
            queries = query_ref[:, lo : lo + PAIR]
            for which in range(2):
                h = 2 * pair + which
                scores = dot_rows(keys, only_head(queries, which)) * HEAD_DIM ** (-0.5)
                scores = jnp.where(inside, scores, NEG_LARGE)
                old = peak[h : h + 1]
                new = jnp.maximum(old, jnp.max(scores, axis=0, keepdims=True))
                probs = jnp.exp(scores - new)
                fade = jnp.exp(old - new)
                peak[h : h + 1] = new
                total[h : h + 1] = total[h : h + 1] * fade + jnp.sum(probs, axis=0, keepdims=True)
                mixed = dot(
                    values_t[which * HEAD_DIM : (which + 1) * HEAD_DIM], probs.astype(jnp.bfloat16)
                )
                acc[h] = acc[h] * fade + mixed
        return carry

    lax.fori_loop(ranges[block, 0], ranges[block, 1], step, 0)
    for pair in range(heads // 2):
        parts = [acc[h] / total[h : h + 1] for h in (2 * pair, 2 * pair + 1)]
        both = jnp.concatenate(parts, axis=0).T
        out_ref[:, pair * PAIR : (pair + 1) * PAIR] = both.astype(out_ref.dtype)
    norm_ref[0] = peak[...] + jnp.log(total[...])


def attend(ranges, window, marks, halo):
    groups, _, rows = marks.shape
    span, slab = window.shape
    third = slab // 3
    heads = third // HEAD_DIM
    first = halo // rows
    return pl.pallas_call(
        functools.partial(attend_kernel, halo),
        grid_spec=pltpu.PrefetchScalarGridSpec(
            num_scalar_prefetch=1,
            grid=(groups,),
            in_specs=[
                pl.BlockSpec((rows, slab), lambda i, r: (first + i, 0)),
                pl.BlockSpec((span, slab), lambda i, r: (0, 0)),
                pl.BlockSpec((1, 8, rows), lambda i, r: (i, 0, 0)),
            ],
            out_specs=[
                pl.BlockSpec((rows, third), lambda i, r: (i, 0)),
                pl.BlockSpec((1, heads, rows), lambda i, r: (i, 0, 0)),
            ],
            scratch_shapes=[
                pltpu.VMEM((heads, rows), jnp.float32),
                pltpu.VMEM((heads, rows), jnp.float32),
                pltpu.VMEM((heads, HEAD_DIM, rows), jnp.float32),
            ],
        ),
        out_shape=[
            jax.ShapeDtypeStruct((groups * rows, third), jnp.bfloat16),
            jax.ShapeDtypeStruct((groups, heads, rows), jnp.float32),
        ],
        compiler_params=pltpu.CompilerParams(vmem_limit_bytes=56 * 2**20),
    )(ranges, window, window, marks)


def attend_back_kernel(
    ranges, query_ref, window_ref, marks_ref, norm_ref, out_ref, grad_ref,
    grad_query_ref, grad_pair_ref, acc,
):
    block = pl.program_id(0)
    rows = query_ref.shape[0]
    heads = query_ref.shape[1] // 3 // HEAD_DIM
    third = heads * HEAD_DIM

    @pl.when(block == 0)
    def _():
        grad_pair_ref[...] = jnp.zeros_like(grad_pair_ref)

    acc[...] = jnp.zeros_like(acc)
    deltas = []
    for pair in range(heads // 2):
        at = slice(pair * PAIR, (pair + 1) * PAIR)
        product = grad_ref[:, at].astype(jnp.float32) * out_ref[:, at].astype(jnp.float32)
        product = product.T
        for which in range(2):
            part = product[which * HEAD_DIM : (which + 1) * HEAD_DIM]
            deltas.append(jnp.sum(part, axis=0, keepdims=True))

    def step(tile, carry):
        keys_at = pl.ds(pl.multiple_of(tile * KEY_TILE, KEY_TILE), KEY_TILE)
        inside = inside_mask(marks_ref, tile, rows)
        for pair in range(heads // 2):
            lo = pair * PAIR
            keys = window_ref[keys_at, third + lo : third + lo + PAIR]
            keys_t = keys.T
            values = window_ref[keys_at, 2 * third + lo : 2 * third + lo + PAIR]
            queries = query_ref[:, lo : lo + PAIR]
            grads = grad_ref[:, lo : lo + PAIR]
            probs_both, scores_both, queries_both, grads_both = [], [], [], []
            for which in range(2):
                h = 2 * pair + which
                query, grad = only_head(queries, which), only_head(grads, which)
                scores = dot_rows(keys, query) * HEAD_DIM ** (-0.5)
                probs = jnp.where(inside, jnp.exp(scores - norm_ref[0, h : h + 1]), 0.0)
                grad_prob = dot_rows(values, grad)
                grad_score = (probs * (grad_prob - deltas[h])).astype(jnp.bfloat16)
                acc[h] += dot(keys_t[which * HEAD_DIM : (which + 1) * HEAD_DIM], grad_score)
                probs_both.append(probs.astype(jnp.bfloat16))
                scores_both.append(grad_score)
                queries_both.append(query)
                grads_both.append(grad)
            grad_key = dot(
                jnp.concatenate(scores_both, axis=1), jnp.concatenate(queries_both, axis=0)
            ) * HEAD_DIM ** (-0.5)
            grad_value = dot(
                jnp.concatenate(probs_both, axis=1), jnp.concatenate(grads_both, axis=0)
            )
            grad_pair_ref[keys_at, lo : lo + PAIR] += grad_key
            grad_pair_ref[keys_at, third + lo : third + lo + PAIR] += grad_value
        return carry

    lax.fori_loop(ranges[block, 0], ranges[block, 1], step, 0)
    for pair in range(heads // 2):
        both = jnp.concatenate([acc[2 * pair], acc[2 * pair + 1]], axis=0).T
        grad_query_ref[:, pair * PAIR : (pair + 1) * PAIR] = both * HEAD_DIM ** (-0.5)


def attend_back(ranges, window, marks, log_norm, attended, grad_attended, halo):
    groups, _, rows = marks.shape
    span, slab = window.shape
    third = slab // 3
    heads = third // HEAD_DIM
    first = halo // rows
    return pl.pallas_call(
        attend_back_kernel,
        grid_spec=pltpu.PrefetchScalarGridSpec(
            num_scalar_prefetch=1,
            grid=(groups,),
            in_specs=[
                pl.BlockSpec((rows, slab), lambda i, r: (first + i, 0)),
                pl.BlockSpec((span, slab), lambda i, r: (0, 0)),
                pl.BlockSpec((1, 8, rows), lambda i, r: (i, 0, 0)),
                pl.BlockSpec((1, heads, rows), lambda i, r: (i, 0, 0)),
                pl.BlockSpec((rows, third), lambda i, r: (i, 0)),
                pl.BlockSpec((rows, third), lambda i, r: (i, 0)),
            ],
            out_specs=[
                pl.BlockSpec((rows, third), lambda i, r: (i, 0)),
                pl.BlockSpec((span, 2 * third), lambda i, r: (0, 0)),
            ],
            scratch_shapes=[pltpu.VMEM((heads, HEAD_DIM, rows), jnp.float32)],
        ),
        out_shape=[
            jax.ShapeDtypeStruct((groups * rows, third), jnp.float32),
            jax.ShapeDtypeStruct((span, 2 * third), jnp.float32),
        ],
        compiler_params=pltpu.CompilerParams(vmem_limit_bytes=56 * 2**20),
    )(ranges, window, window, marks, log_norm, attended, grad_attended)


def with_column(matrix, column, extra):
    return jnp.concatenate([matrix, jnp.pad(column[:, None], ((0, 0), (0, extra - 1)))], axis=1)


def on_device(
    stream,
    cotangent,
    bounds,
    joined_proj,
    out_proj,
    wide_proj,
    down_proj,
    gain_first,
    gain_second,
    joined_momentum,
    out_momentum,
    wide_momentum,
    down_momentum,
    gain_first_momentum,
    gain_second_momentum,
    joined_variance,
    out_variance,
    wide_variance,
    down_variance,
    gain_first_variance,
    gain_second_variance,
):
    row_count = stream.shape[0]
    width = stream.shape[1]
    heads = width // HEAD_DIM
    both = ("dp", "group")
    gains = jnp.stack([gain_first, gain_second], axis=1)
    gains = jnp.pad(gains, ((0, 0), (0, GAIN_PAD - 2)))
    joined_gains = jnp.concatenate([joined_proj, gains], axis=1).astype(jnp.bfloat16)
    joined_gains, out_half, wide_half, down_half = gather_all(
        [
            joined_gains,
            out_proj.astype(jnp.bfloat16),
            wide_proj.astype(jnp.bfloat16),
            down_proj.astype(jnp.bfloat16),
        ],
        pieces([joined_gains.shape[1], width, wide_proj.shape[1], down_proj.shape[1]]),
        1,
    )
    joined_half = joined_gains[:, : 3 * width]
    gain_one_half = joined_gains[:, 3 * width]
    gain_two_half = joined_gains[:, 3 * width + 1]
    gain_one = gain_one_half.astype(jnp.float32)
    gain_two = gain_two_half.astype(jnp.float32)
    ff_width = down_half.shape[1]
    first_row = lax.axis_index(("dp", "group")) * row_count
    token_index = first_row + jnp.arange(row_count, dtype=jnp.int32)
    seq_starts = bounds[:, 0]
    seq_ends = bounds[:, 1]
    cosine, sine_table = rope_tables(token_index - seq_starts)
    normed_one, scale_one = normalize(stream)
    normed_in = (normed_one * gain_one).astype(jnp.bfloat16)
    joined_act = jnp.dot(normed_in, joined_half, preferred_element_type=jnp.float32)
    groups = lax.axis_size("group")
    block_rows = row_count * groups
    slab = width // groups

    def turned(columns):
        heads_part = columns.reshape(row_count, heads, HEAD_DIM)
        return rotate(heads_part, cosine, sine_table, 1.0).reshape(row_count, groups, slab)

    pack = jnp.stack(
        [
            turned(joined_act[:, :width]),
            turned(joined_act[:, width : 2 * width]),
            joined_act[:, 2 * width :].reshape(row_count, groups, slab),
        ],
        axis=2,
    )
    pack = pack.astype(jnp.bfloat16).reshape(row_count, 3 * width)
    block_first = lax.axis_index("dp") * block_rows
    marks = jnp.pad(bounds.T - (block_first - LMAX), ((0, 6), (0, 0)))
    window, marks_all = window_of(pack, marks, LMAX, 3)
    ranges = jnp.stack(
        [marks_all[:, 0, 0] // KEY_TILE, (marks_all[:, 1, row_count - 1] + KEY_TILE - 1) // KEY_TILE],
        axis=1,
    )
    attended_heads, log_norm = attend(ranges, window, marks_all, LMAX)
    attended = swap(attended_heads, False, 4)
    residual = stream + jnp.dot(attended, out_half, preferred_element_type=jnp.float32)
    normed_two, scale_two = normalize(residual)
    hidden_in = (normed_two * gain_two).astype(jnp.bfloat16)
    wide_act = jnp.dot(hidden_in, wide_half, preferred_element_type=jnp.float32)
    inner_part = wide_act[:, :ff_width]
    gate_part = wide_act[:, ff_width:]
    activation, gelu_slope = gelu_parts(inner_part)
    gated = (activation * gate_part).astype(jnp.bfloat16)
    output = residual + jnp.einsum(
        "rf,df->rd", gated, down_half, preferred_element_type=jnp.float32
    )
    cot_half = cotangent.astype(jnp.bfloat16)
    spare = -ff_width % 128
    down_local = jnp.einsum(
        "rd,rf->df", cot_half, jnp.pad(gated, ((0, 0), (0, spare))), preferred_element_type=jnp.float32
    )
    grad_gated = jnp.dot(cot_half, down_half, preferred_element_type=jnp.float32)
    grad_inner = (grad_gated * gate_part * gelu_slope).astype(jnp.bfloat16)
    grad_gate = (grad_gated * activation).astype(jnp.bfloat16)
    grad_wide = jnp.concatenate([grad_inner, grad_gate], axis=1)
    wide_local = jnp.einsum("rd,rf->df", hidden_in, grad_wide, preferred_element_type=jnp.float32)
    grad_hidden = jnp.einsum("rf,df->rd", grad_wide, wide_half, preferred_element_type=jnp.float32)
    gain_two_local = jnp.sum(grad_hidden * normed_two, axis=0)
    grad_resid = cotangent + norm_back(grad_hidden * gain_two, normed_two, scale_two)
    resid_half = grad_resid.astype(jnp.bfloat16)
    out_local = jnp.einsum("rd,re->de", attended, resid_half, preferred_element_type=jnp.float32)
    out_local = with_column(out_local, gain_two_local, OUT_PAD)
    grad_attended = jnp.einsum(
        "re,de->rd", resid_half, out_half, preferred_element_type=jnp.float32
    ).astype(jnp.bfloat16)
    grad_heads = swap(grad_attended, True, 5)
    grad_query, grad_window = attend_back(
        ranges, window, marks_all, log_norm, attended_heads, grad_heads, LMAX
    )
    peers = lax.axis_size("dp")
    up = [(i, i + 1) for i in range(peers - 1)]
    down = [(j, i) for i, j in up]
    rim = grad_window[:LMAX].astype(jnp.bfloat16), grad_window[block_rows + LMAX :].astype(jnp.bfloat16)
    from_next = lax.ppermute(rim[0], "dp", down).astype(jnp.float32)
    from_previous = lax.ppermute(rim[1], "dp", up).astype(jnp.float32)
    centre = grad_window[LMAX : LMAX + block_rows]
    extra = block_rows - LMAX
    centre = centre + jnp.pad(from_previous, ((0, extra), (0, 0)))
    centre = centre + jnp.pad(from_next, ((extra, 0), (0, 0)))
    block_tokens = block_first - LMAX + jnp.arange(LMAX, LMAX + block_rows, dtype=jnp.int32)
    block_starts = marks_all[:, 0, :].reshape(block_rows) + (block_first - LMAX)
    block_cos, block_sin = rope_tables(block_tokens - block_starts)

    def turned_back(columns):
        heads_part = columns.reshape(block_rows, heads // groups, HEAD_DIM)
        return rotate(heads_part, block_cos, block_sin, -1.0).reshape(block_rows, slab)

    grad_pack = jnp.concatenate(
        [turned_back(grad_query), turned_back(centre[:, :slab]), centre[:, slab:]], axis=1
    ).astype(jnp.bfloat16)
    grad_joined = swap(grad_pack, False, 6)
    grad_joined = grad_joined.reshape(row_count, groups, 3, slab)
    grad_joined = grad_joined.transpose(0, 2, 1, 3).reshape(row_count, 3 * width)
    joined_local = jnp.einsum(
        "rd,re->de", normed_in, grad_joined, preferred_element_type=jnp.float32
    )
    grad_normed = jnp.einsum(
        "re,de->rd", grad_joined, joined_half, preferred_element_type=jnp.float32
    )
    gain_one_local = jnp.sum(grad_normed * normed_one, axis=0)
    stream_grad = grad_resid + norm_back(grad_normed * gain_one, normed_one, scale_one)
    joined_local = with_column(joined_local, gain_one_local, GAIN_PAD)
    locals_half = [
        v.astype(jnp.bfloat16)
        for v in (wide_local, down_local, out_local, joined_local)
    ]
    wide_grad, down_sum, out_sum, joined_sum = scatter_all(
        locals_half, pieces([v.shape[1] for v in locals_half]), 2
    )
    joined_grad = joined_sum[:, : 3 * width]
    gain_first_grad = joined_sum[:, 3 * width]
    out_grad = out_sum[:, :width]
    gain_second_grad = out_sum[:, width]
    down_grad = down_sum[:, :ff_width]
    joined_new, joined_momentum_new, joined_variance_new = adam_step(
        joined_proj, joined_grad, joined_momentum, joined_variance, WEIGHT_DECAY
    )
    out_new, out_momentum_new, out_variance_new = adam_step(
        out_proj, out_grad, out_momentum, out_variance, WEIGHT_DECAY
    )
    wide_new, wide_momentum_new, wide_variance_new = adam_step(
        wide_proj, wide_grad, wide_momentum, wide_variance, WEIGHT_DECAY
    )
    down_new, down_momentum_new, down_variance_new = adam_step(
        down_proj, down_grad, down_momentum, down_variance, WEIGHT_DECAY
    )
    gain_first_new, gain_first_momentum_new, gain_first_variance_new = adam_step(
        gain_first, gain_first_grad, gain_first_momentum, gain_first_variance, 0.0
    )
    gain_second_new, gain_second_momentum_new, gain_second_variance_new = adam_step(
        gain_second, gain_second_grad, gain_second_momentum, gain_second_variance, 0.0
    )
    return (
        output,
        stream_grad,
        joined_grad,
        out_grad,
        wide_grad,
        down_grad,
        gain_first_grad,
        gain_second_grad,
        joined_new,
        out_new,
        wide_new,
        down_new,
        gain_first_new,
        gain_second_new,
        joined_momentum_new,
        out_momentum_new,
        wide_momentum_new,
        down_momentum_new,
        gain_first_momentum_new,
        gain_second_momentum_new,
        joined_variance_new,
        out_variance_new,
        wide_variance_new,
        down_variance_new,
        gain_first_variance_new,
        gain_second_variance_new,
    )


def solution(mesh):
    placed = (
        P(("dp", "group"), None),
        P(("dp", "group"), None),
        P(("dp", "group"), None),
        P(("dp", "group"), None),
        P(("dp", "group"), None),
        P(("dp", "group"), None),
        P(("dp", "group"), None),
        P(("dp", "group")),
        P(("dp", "group")),
        P(("dp", "group"), None),
        P(("dp", "group"), None),
        P(("dp", "group"), None),
        P(("dp", "group"), None),
        P(("dp", "group")),
        P(("dp", "group")),
        P(("dp", "group"), None),
        P(("dp", "group"), None),
        P(("dp", "group"), None),
        P(("dp", "group"), None),
        P(("dp", "group")),
        P(("dp", "group")),
    )
    return jax.shard_map(
        on_device,
        mesh=mesh,
        in_specs=placed,
        out_specs=(
            P(("dp", "group"), None),
            P(("dp", "group"), None),
            P(("dp", "group"), None),
            P(("dp", "group"), None),
            P(("dp", "group"), None),
            P(("dp", "group"), None),
            P(("dp", "group")),
            P(("dp", "group")),
            P(("dp", "group"), None),
            P(("dp", "group"), None),
            P(("dp", "group"), None),
            P(("dp", "group"), None),
            P(("dp", "group")),
            P(("dp", "group")),
            P(("dp", "group"), None),
            P(("dp", "group"), None),
            P(("dp", "group"), None),
            P(("dp", "group"), None),
            P(("dp", "group")),
            P(("dp", "group")),
            P(("dp", "group"), None),
            P(("dp", "group"), None),
            P(("dp", "group"), None),
            P(("dp", "group"), None),
            P(("dp", "group")),
            P(("dp", "group")),
        ),
        check_vma=False,
    )
```

```python
import functools
import math

import jax
import jax.numpy as jnp
from jax import lax
from jax.experimental import pallas as pl
from jax.experimental.pallas import tpu as pltpu
from jax.sharding import PartitionSpec as P

HEAD_DIM = 64
LMAX = 1024
STEP = 4
GAIN_PAD = 384
OUT_PAD = 128


EPSILON = 1e-05
ROPE_BASE = 160000.0
LEARN_RATE = 0.02
BETA_ONE = 0.9
BETA_TWO = 0.98
ADAM_EPSILON = 1e-06
WEIGHT_DECAY = 0.1
NEG_LARGE = -1e30
MESH = pl.DeviceIdType.MESH


def normalize(values):
    centred = values - jnp.mean(values, axis=1, keepdims=True)
    row_scale = lax.rsqrt(jnp.mean(centred * centred, axis=1, keepdims=True) + EPSILON)
    return (centred * row_scale, row_scale)


def norm_back(grad_hat, normed, row_scale):
    mean_one = jnp.mean(grad_hat, axis=1, keepdims=True)
    mean_two = jnp.mean(grad_hat * normed, axis=1, keepdims=True)
    return row_scale * (grad_hat - mean_one - normed * mean_two)


def rope_tables(positions):
    half_dim = HEAD_DIM // 2
    freqs = jnp.exp(
        jnp.arange(half_dim, dtype=jnp.float32) * (-2.0 * math.log(ROPE_BASE) / HEAD_DIM)
    )
    angles = positions.astype(jnp.float32)[:, None] * freqs[None, :]
    return (jnp.cos(angles), jnp.sin(angles))


def rotate(values, cosine, sine_table, sign):
    half_dim = values.shape[-1] // 2
    front_half = values[..., :half_dim]
    second = values[..., half_dim:]
    cos_part = cosine[:, None, :]
    sin_part = sine_table[:, None, :] * sign
    return jnp.concatenate(
        [front_half * cos_part - second * sin_part, second * cos_part + front_half * sin_part],
        axis=-1,
    )


def gelu_parts(inner_part):
    cdf_part = 0.5 * (1.0 + lax.erf(inner_part * (1.0 / math.sqrt(2.0))))
    activation = inner_part * cdf_part
    gelu_slope = cdf_part + inner_part * jnp.exp(-0.5 * inner_part * inner_part) * (
        1.0 / math.sqrt(2.0 * math.pi)
    )
    return (activation, gelu_slope)


def adam_step(weight, gradient, momentum, variance, decay_rate):
    new_momentum = BETA_ONE * momentum + (1.0 - BETA_ONE) * gradient
    new_variance = BETA_TWO * variance + (1.0 - BETA_TWO) * gradient * gradient
    update = (
        new_momentum
        / (1.0 - BETA_ONE**STEP)
        / (jnp.sqrt(new_variance / (1.0 - BETA_TWO**STEP)) + ADAM_EPSILON)
    )
    return (weight - LEARN_RATE * (update + decay_rate * weight), new_momentum, new_variance)


def grid_place(peers, groups):
    place, member = lax.axis_index("dp"), lax.axis_index("group")
    parity = lax.rem(place, 2)
    bits = []
    power = 2
    while power < peers:
        bits.append((1 - 2 * lax.rem(place // power, 2)) * power)
        power *= 2
    hops = [(1 - parity) * a + parity * b for a, b in zip(bits, reversed(bits))]
    return place, member, hops, 1 - 2 * parity


def combos(count):
    return [tuple((i >> p) & 1 for p in range(count)) for i in range(2**count)]


def offset(combo, hops):
    total = 0
    for taken, hop in zip(combo, hops):
        if taken:
            total = total + hop
    return total


def meet(place, member, hops, last, groups):
    barrier = pltpu.get_barrier_semaphore()
    for step in range(1, groups):
        pl.semaphore_signal(
            barrier, inc=1, device_id=(place, lax.rem(member + step, groups)), device_id_type=MESH
        )
    for hop in list(hops) + [last]:
        pl.semaphore_signal(barrier, inc=1, device_id=(place + hop, member), device_id_type=MESH)
    pl.semaphore_wait(barrier, groups - 1 + len(hops) + 1)


def pieces(widths, largest=2688):
    found = []
    for a, width in enumerate(widths):
        if width <= largest:
            found.append((a, 0, width))
            continue
        parts = -(-width // largest)
        part = -(-width // (128 * parts)) * 128
        for lo in range(0, width, part):
            found.append((a, lo, min(part, width - lo)))
    return tuple(found)


def gather_steps(position, groups, chunks, ins, outs, sems, modes):
    place, member, hops, last = position
    send_sem, recv_sem, own_sem = sems
    phases = len(hops)
    n_chunks = len(chunks)
    base = groups - 1

    def copy(src, dst, k, slot, device):
        return pltpu.make_async_remote_copy(
            src_ref=src, dst_ref=dst, send_sem=send_sem.at[k, slot], recv_sem=recv_sem.at[k, slot],
            device_id=device, device_id_type=MESH,
        )

    def block(k, combo):
        a, lo, width = chunks[k]
        rows = ins[a].shape[0] * (groups if modes[a] == "full" else 1)
        at = (place + offset(combo, hops)) * rows
        return outs[a].at[pl.ds(at, rows), pl.ds(lo, width)]

    pending = [{p: [] for p in range(phases + 1)} for _ in range(n_chunks)]

    def launch(k, combo):
        done = max([p + 1 for p, taken in enumerate(combo) if taken], default=0)
        ref = block(k, combo)
        for p in range(done, phases):
            slot = base + sum(2**q for q in range(p)) + sum(t << q for q, t in enumerate(combo[:p]))
            c = copy(ref, ref, k, slot, (place + hops[p], member))
            c.start()
            pending[k][p].append((c, combo))
        slot = base + (2**phases - 1) + sum(t << q for q, t in enumerate(combo))
        c = copy(ref, ref, k, slot, (place + last, member))
        c.start()
        pending[k][phases].append((c, combo))

    first, own = [], []
    for k, (a, lo, width) in enumerate(chunks):
        rows = ins[a].shape[0]
        start = {"full": (place * groups + member) * rows, "group": member * rows, "grouped": place * rows}
        mine = outs[a].at[pl.ds(start[modes[a]], rows), pl.ds(lo, width)]
        src = ins[a].at[:, pl.ds(lo, width)]
        keep = pltpu.make_async_copy(src, mine, own_sem.at[k])
        keep.start()
        row = []
        if modes[a] != "grouped":
            for step in range(1, groups):
                c = copy(src, mine, k, step - 1, (place, lax.rem(member + step, groups)))
                c.start()
                row.append(c)
        first.append(row)
        own.append(keep)
    for k, (a, _, _) in enumerate(chunks):
        if modes[a] == "grouped":
            own[k].wait()
            launch(k, (0,) * phases)
    yield

    for step in range(n_chunks + phases):
        for level in range(phases + 1):
            k = step - level
            if not 0 <= k < n_chunks:
                continue
            if level == 0:
                if modes[chunks[k][0]] == "grouped":
                    continue
                for c in first[k]:
                    c.wait_recv()
                own[k].wait()
                if modes[chunks[k][0]] == "full":
                    launch(k, (0,) * phases)
            else:
                p = level - 1
                for c, combo in pending[k][p]:
                    c.wait_recv()
                    launch(k, tuple(1 if q == p else t for q, t in enumerate(combo)))
        yield
    for k in range(n_chunks):
        for c, _ in pending[k][phases]:
            c.wait_recv()
    for k in range(n_chunks):
        for c in first[k]:
            c.wait_send()
        for p in pending[k]:
            for c, _ in pending[k][p]:
                c.wait_send()


def gather_kernel(peers, groups, chunks, modes, *refs):
    count = len(modes)
    ins, outs = refs[:count], refs[count : 2 * count]
    position = grid_place(peers, groups)
    meet(*position, groups)
    for _ in gather_steps(position, groups, chunks, ins, outs, refs[2 * count :], modes):
        pass


def gathered_shape(a, mode, peers, groups):
    copies = {"full": peers * groups, "group": groups, "grouped": peers}[mode]
    return jax.ShapeDtypeStruct((a.shape[0] * copies, a.shape[1]), a.dtype)


def gather_all(arrays, chunks, modes, collective_id):
    peers, groups = lax.axis_size("dp"), lax.axis_size("group")
    phases = peers.bit_length() - 2
    slots = groups - 1 + 2 ** (phases + 1) - 1
    return pl.pallas_call(
        functools.partial(gather_kernel, peers, groups, chunks, modes),
        out_shape=[gathered_shape(a, m, peers, groups) for a, m in zip(arrays, modes)],
        in_specs=[pl.BlockSpec(memory_space=pl.ANY)] * len(arrays),
        out_specs=[pl.BlockSpec(memory_space=pl.ANY)] * len(arrays),
        scratch_shapes=[
            pltpu.SemaphoreType.DMA((len(chunks), slots)),
            pltpu.SemaphoreType.DMA((len(chunks), slots)),
            pltpu.SemaphoreType.DMA((len(chunks),)),
        ],
        compiler_params=pltpu.CompilerParams(collective_id=collective_id, has_side_effects=True),
    )(*arrays)


def scatter_kernel(peers, groups, chunks, count, phases, *refs):
    ins, outs = refs[:count], refs[count : 2 * count]
    n_chunks = len(chunks)
    rest = list(refs[2 * count :])
    send_sem, recv_sem, own_sem = rest[-3:]
    mine, from_core, from_group = (rest[i * n_chunks : (i + 1) * n_chunks] for i in range(3))
    from_hops = [rest[(3 + p) * n_chunks : (4 + p) * n_chunks] for p in range(phases)]
    place, member, hops, last = grid_place(peers, groups)
    meet(place, member, hops, last, groups)
    every = combos(phases)
    rows = mine[0].shape[1]
    shard = rows // groups
    tile = 16

    def copy(src, dst, k, slot, device):
        return pltpu.make_async_remote_copy(
            src_ref=src, dst_ref=dst, send_sem=send_sem.at[k, slot], recv_sem=recv_sem.at[k, slot],
            device_id=device, device_id_type=MESH,
        )

    def number(combo):
        return sum(t << q for q, t in enumerate(combo))

    def add_rows(target, source, at):
        def body(i, carry):
            span = pl.ds(pl.multiple_of(i * tile, tile), tile)
            total = target[at, span].astype(jnp.float32) + source[at, span].astype(jnp.float32)
            target[at, span] = total.astype(target.dtype)
            return carry

        lax.fori_loop(0, rows // tile, body, 0)

    core_copies, own_copies = [], []
    for k, (a, lo, width) in enumerate(chunks):
        cols = pl.ds(lo, width)
        sent, kept = [], []
        for combo in every:
            s = number(combo)
            theirs = place + last + offset(combo, hops[::-1])
            c = copy(
                ins[a].at[pl.ds(theirs * rows, rows), cols], from_core[k].at[s], k, s,
                (place + last, member),
            )
            c.start()
            sent.append(c)
            ours = place + offset(combo, hops)
            c = pltpu.make_async_copy(
                ins[a].at[pl.ds(ours * rows, rows), cols], mine[k].at[s], own_sem.at[k, s]
            )
            c.start()
            kept.append(c)
        core_copies.append(sent)
        own_copies.append(kept)

    hop_copies = [[[] for _ in range(phases)] for _ in range(n_chunks)]
    group_copies = [[] for _ in range(n_chunks)]

    def send_on(k, p):
        if p < 0:
            for step in range(1, groups):
                to = lax.rem(member + step, groups)
                c = copy(
                    mine[k].at[0, pl.ds(pl.multiple_of(to * shard, shard), shard)],
                    from_group[k].at[step - 1],
                    k, 2 ** (phases + 1) - 1 + step - 1, (place, to),
                )
                c.start()
                group_copies[k].append(c)
            return
        base = 2**phases + sum(2**q for q in range(p))
        for combo in combos(p):
            s = number(combo)
            c = copy(
                mine[k].at[s + 2**p], from_hops[p][k].at[s], k, base + s,
                (place + hops[p], member),
            )
            c.start()
            hop_copies[k][p].append(c)

    for step in range(n_chunks + phases + 1):
        for level in range(phases + 2):
            k = step - level
            if not 0 <= k < n_chunks:
                continue
            a, lo, width = chunks[k]
            if level == 0:
                for combo in every:
                    s = number(combo)
                    core_copies[k][s].wait_recv()
                    own_copies[k][s].wait()
                    add_rows(mine[k], from_core[k], s)
                send_on(k, phases - 1)
            elif level <= phases:
                p = phases - level
                for s, c in enumerate(hop_copies[k][p]):
                    c.wait_recv()
                    add_rows(mine[k], from_hops[p][k], s)
                send_on(k, p - 1)
            else:
                for c in group_copies[k]:
                    c.wait_recv()
                own = pl.ds(pl.multiple_of(member * shard, shard), shard)
                total = mine[k][0, own].astype(jnp.float32)
                for step_in in range(groups - 1):
                    total = total + from_group[k][step_in].astype(jnp.float32)
                outs[a][:, pl.ds(lo, width)] = total
    for k in range(n_chunks):
        for c in core_copies[k] + group_copies[k]:
            c.wait_send()
        for p in range(phases):
            for c in hop_copies[k][p]:
                c.wait_send()


def scatter_all(arrays, chunks, collective_id):
    peers, groups = lax.axis_size("dp"), lax.axis_size("group")
    phases = peers.bit_length() - 2
    slots = groups - 1 + 2 ** (phases + 1) - 1
    rows = arrays[0].shape[0] // peers
    shard = rows // groups
    kind = arrays[0].dtype
    return pl.pallas_call(
        functools.partial(scatter_kernel, peers, groups, chunks, len(arrays), phases),
        out_shape=[jax.ShapeDtypeStruct((shard, a.shape[1]), jnp.float32) for a in arrays],
        in_specs=[pl.BlockSpec(memory_space=pl.ANY)] * len(arrays),
        out_specs=[pl.BlockSpec(memory_space=pltpu.VMEM)] * len(arrays),
        scratch_shapes=[
            pltpu.VMEM((depth, height, width), kind)
            for depth, height in [(2**phases, rows)] * 2
            + [(groups - 1, shard)]
            + [(2**p, rows) for p in range(phases)]
            for _, _, width in chunks
        ]
        + [
            pltpu.SemaphoreType.DMA((len(chunks), slots)),
            pltpu.SemaphoreType.DMA((len(chunks), slots)),
            pltpu.SemaphoreType.DMA((len(chunks), 2**phases)),
        ],
        compiler_params=pltpu.CompilerParams(
            collective_id=collective_id, has_side_effects=True, vmem_limit_bytes=60 * 2**20
        ),
    )(*arrays)


def swap_kernel(groups, to_heads, x, y, send_sem, recv_sem, own_sem):
    place, member = lax.axis_index("dp"), lax.axis_index("group")
    barrier = pltpu.get_barrier_semaphore()
    for step in range(1, groups):
        pl.semaphore_signal(
            barrier, inc=1, device_id=(place, lax.rem(member + step, groups)), device_id_type=MESH
        )
    pl.semaphore_wait(barrier, groups - 1)
    rows = x.shape[0] if to_heads else y.shape[0]
    slab = y.shape[1] if to_heads else x.shape[1]

    def ends(to):
        if to_heads:
            src = x.at[:, pl.ds(pl.multiple_of(to * slab, slab), slab)]
            return src, y.at[pl.ds(member * rows, rows), :]
        src = x.at[pl.ds(to * rows, rows), :]
        return src, y.at[:, pl.ds(pl.multiple_of(member * slab, slab), slab)]

    copies = []
    for step in range(1, groups):
        to = lax.rem(member + step, groups)
        src, dst = ends(to)
        c = pltpu.make_async_remote_copy(
            src_ref=src, dst_ref=dst, send_sem=send_sem.at[step - 1],
            recv_sem=recv_sem.at[step - 1], device_id=(place, to), device_id_type=MESH,
        )
        c.start()
        copies.append(c)
    own = pltpu.make_async_copy(*ends(member), own_sem.at[0])
    own.start()
    own.wait()
    for c in copies:
        c.wait()


def swap(x, to_heads, collective_id):
    groups = lax.axis_size("group")
    rows, columns = x.shape
    shape = (rows * groups, columns // groups) if to_heads else (rows // groups, columns * groups)
    return pl.pallas_call(
        functools.partial(swap_kernel, groups, to_heads),
        out_shape=jax.ShapeDtypeStruct(shape, x.dtype),
        in_specs=[pl.BlockSpec(memory_space=pl.ANY)],
        out_specs=pl.BlockSpec(memory_space=pl.ANY),
        scratch_shapes=[
            pltpu.SemaphoreType.DMA((groups - 1,)),
            pltpu.SemaphoreType.DMA((groups - 1,)),
            pltpu.SemaphoreType.DMA((1,)),
        ],
        compiler_params=pltpu.CompilerParams(collective_id=collective_id, has_side_effects=True),
    )(x)


KEY_TILE = 256
PAIR = 2 * HEAD_DIM


def dot(a, b):
    return jnp.dot(a, b, preferred_element_type=jnp.float32)


def dot_rows(a, b):
    return lax.dot_general(a, b, (((1,), (1,)), ((), ())), preferred_element_type=jnp.float32)


def only_head(values, which):
    lane = lax.broadcasted_iota(jnp.int32, values.shape, 1)
    inside = (lane >= which * HEAD_DIM) & (lane < (which + 1) * HEAD_DIM)
    return jnp.where(inside, values, jnp.zeros_like(values))


def inside_mask(marks_ref, tile, rows):
    key = tile * KEY_TILE + lax.broadcasted_iota(jnp.int32, (KEY_TILE, rows), 0)
    return (key >= marks_ref[0, 0:1, :]) & (key < marks_ref[0, 1:2, :])


def front_kernel(peers, groups, halo, chunks, modes, *refs):
    count = len(modes)
    pack, marks, *shards = refs[: 2 + count]
    rest = refs[2 + count :]
    window_out, marks_out, heads_out, norm_out, attended_out, *gathered = rest[: 5 + count]
    (
        window, marks_all, peak, total, acc, send_sem, recv_sem, own_sem, swap_send, swap_recv,
        *gather_sems,
    ) = rest[5 + count :]
    position = grid_place(peers, groups)
    place, member, hops, last = position
    rows = pack.shape[0]
    slab = window.shape[1]
    third = slab // 3
    heads = third // HEAD_DIM
    block = rows * groups
    has_up = place < peers - 1
    has_down = place > 0
    sides = (place + peers - 1) // peers + 1 - place // (peers - 1)

    barrier = pltpu.get_barrier_semaphore()
    for step in range(1, groups):
        pl.semaphore_signal(
            barrier, inc=1, device_id=(place, lax.rem(member + step, groups)), device_id_type=MESH
        )
    for hop in list(hops) + [last]:
        pl.semaphore_signal(barrier, inc=1, device_id=(place + hop, member), device_id_type=MESH)
    for near, there in ((1, has_up), (-1, has_down)):

        @pl.when(there)
        def _():
            pl.semaphore_signal(
                barrier, inc=1, device_id=(place + near, member), device_id_type=MESH
            )

    pl.semaphore_wait(barrier, groups + len(hops) + sides)

    def columns(of):
        return pl.ds(pl.multiple_of(of * slab, slab), slab)

    def copy(src, dst, slot, device):
        return pltpu.make_async_remote_copy(
            src_ref=src, dst_ref=dst, send_sem=send_sem.at[slot], recv_sem=recv_sem.at[slot],
            device_id=device, device_id_type=MESH,
        )

    mine = window.at[pl.ds(halo + member * rows, rows), :]
    from_group = []
    for step in range(1, groups):
        to = lax.rem(member + step, groups)
        c = copy(pack.at[:, columns(to)], mine, step - 1, (place, to))
        c.start()
        m = copy(marks.at[...], marks_all.at[member], groups - 2 + step, (place, to))
        m.start()
        from_group.append((c, m))
    own = pltpu.make_async_copy(pack.at[:, columns(member)], mine, own_sem.at[0])
    own.start()
    own_marks = pltpu.make_async_copy(marks.at[...], marks_all.at[member], own_sem.at[1])
    own_marks.start()

    gather = gather_steps(position, groups, chunks, shards, gathered, gather_sems, modes)
    next(gather)

    pairs_at = pl.ds(third, 2 * third)

    @pl.when(place == 0)
    def _():
        window[pl.ds(0, halo), :] = jnp.zeros((halo, slab), window.dtype)

    @pl.when(place == peers - 1)
    def _():
        window[pl.ds(halo + block, halo), :] = jnp.zeros((halo, slab), window.dtype)

    peak[...] = jnp.full_like(peak, NEG_LARGE)
    total[...] = jnp.zeros_like(total)
    acc[...] = jnp.zeros_like(acc)

    moved = []
    if halo == block:
        for step in range(groups):
            if step == 0:
                own.wait()
            else:
                from_group[step - 1][0].wait_recv()
            of = lax.rem(member + groups - step, groups)
            src = window.at[pl.ds(halo + of * rows, rows), pairs_at]
            up = copy(
                src, window.at[pl.ds(of * rows, rows), pairs_at],
                2 * groups - 2 + step, (place + 1, member),
            )
            down = copy(
                src, window.at[pl.ds(halo + block + of * rows, rows), pairs_at],
                3 * groups - 2 + step, (place - 1, member),
            )
            moved.append((up, down))

            @pl.when(has_up)
            def _():
                up.start()

            @pl.when(has_down)
            def _():
                down.start()

            next(gather, None)
    else:
        own.wait()
        for c, _ in from_group:
            c.wait_recv()
        up = copy(
            window.at[pl.ds(block, halo), pairs_at], window.at[pl.ds(0, halo), pairs_at],
            2 * groups - 2, (place + 1, member),
        )
        down = copy(
            window.at[pl.ds(halo, halo), pairs_at], window.at[pl.ds(halo + block, halo), pairs_at],
            3 * groups - 2, (place - 1, member),
        )
        moved.append((up, down))

        @pl.when(has_up)
        def _():
            up.start()

        @pl.when(has_down)
        def _():
            down.start()

    own_marks.wait()
    for _, m in from_group:
        m.wait_recv()

    def visit(i, first, stop):
        at = pl.ds(halo + i * rows, rows)

        def step(tile, carry):
            keys_at = pl.ds(pl.multiple_of(tile * KEY_TILE, KEY_TILE), KEY_TILE)
            key = tile * KEY_TILE + lax.broadcasted_iota(jnp.int32, (KEY_TILE, rows), 0)
            inside = (key >= marks_all[i, 0:1, :]) & (key < marks_all[i, 1:2, :])
            for pair in range(heads // 2):
                lo = pair * PAIR
                keys = window[keys_at, third + lo : third + lo + PAIR]
                values_t = window[keys_at, 2 * third + lo : 2 * third + lo + PAIR].T
                queries = window[at, lo : lo + PAIR]
                for which in range(2):
                    h = 2 * pair + which
                    scores = dot_rows(keys, only_head(queries, which)) * HEAD_DIM ** (-0.5)
                    scores = jnp.where(inside, scores, NEG_LARGE)
                    old = peak[i, h : h + 1]
                    new = jnp.maximum(old, jnp.max(scores, axis=0, keepdims=True))
                    probs = jnp.exp(scores - new)
                    fade = jnp.exp(old - new)
                    peak[i, h : h + 1] = new
                    total[i, h : h + 1] = total[i, h : h + 1] * fade + jnp.sum(
                        probs, axis=0, keepdims=True
                    )
                    mixed = dot(
                        values_t[which * HEAD_DIM : (which + 1) * HEAD_DIM],
                        probs.astype(jnp.bfloat16),
                    )
                    acc[i, h] = acc[i, h] * fade + mixed
            return carry

        if stop > first:
            lax.fori_loop(first, stop, step, 0)

    own_first, own_stop = halo // KEY_TILE, (halo + block) // KEY_TILE
    for i in range(groups):
        visit(i, own_first, own_stop)
        next(gather, None)

    for up, down in moved:

        @pl.when(has_up)
        def _():
            down.wait_recv()

        @pl.when(has_down)
        def _():
            up.wait_recv()

    keep = pltpu.make_async_copy(window, window_out, own_sem.at[2])
    keep.start()

    def give(i):
        return pltpu.make_async_remote_copy(
            src_ref=heads_out.at[pl.ds(i * rows, rows), :],
            dst_ref=attended_out.at[:, pl.ds(pl.multiple_of(member * third, third), third)],
            send_sem=swap_send.at[i], recv_sem=swap_recv.at[member],
            device_id=(place, i), device_id_type=MESH,
        )

    def keep_own(i):
        return pltpu.make_async_copy(
            heads_out.at[pl.ds(i * rows, rows), :],
            attended_out.at[:, pl.ds(i * third, third)],
            own_sem.at[3],
        )

    for i in range(groups):
        span = (i * rows // KEY_TILE, -(-(i * rows + rows + 2 * halo) // KEY_TILE))
        visit(i, span[0], min(own_first, span[1]))
        visit(i, max(own_stop, span[0]), span[1])
        for pair in range(heads // 2):
            parts = [acc[i, h] / total[i, h : h + 1] for h in (2 * pair, 2 * pair + 1)]
            both = jnp.concatenate(parts, axis=0).T
            heads_out[i * rows : (i + 1) * rows, pair * PAIR : (pair + 1) * PAIR] = both.astype(
                heads_out.dtype
            )

        @pl.when(member != i)
        def _():
            give(i).start()

        @pl.when(member == i)
        def _():
            keep_own(i).start()

        next(gather, None)
    norm_out[...] = peak[...] + jnp.log(total[...])
    marks_out[...] = marks_all[...]
    for _ in gather:
        pass

    for c, m in from_group:
        c.wait_send()
        m.wait_send()
    for up, down in moved:

        @pl.when(has_up)
        def _():
            up.wait_send()

        @pl.when(has_down)
        def _():
            down.wait_send()

    for i in range(groups):

        @pl.when(member != i)
        def _():
            give(i).wait_send()
            pltpu.make_async_remote_copy(
                src_ref=heads_out.at[pl.ds(i * rows, rows), :],
                dst_ref=attended_out.at[:, pl.ds(i * third, third)],
                send_sem=swap_send.at[i], recv_sem=swap_recv.at[i],
                device_id=(place, i), device_id_type=MESH,
            ).wait_recv()

        @pl.when(member == i)
        def _():
            keep_own(i).wait()

    keep.wait()


def front(pack, marks, shards, chunks, modes, halo, collective_id):
    peers, groups = lax.axis_size("dp"), lax.axis_size("group")
    rows, columns = pack.shape
    block = rows * groups
    span = block + 2 * halo
    slab = columns // groups
    third = slab // 3
    heads = third // HEAD_DIM
    phases = peers.bit_length() - 2
    slots = groups - 1 + 2 ** (phases + 1) - 1
    count = len(shards)
    anywhere, inside = pl.BlockSpec(memory_space=pl.ANY), pl.BlockSpec(memory_space=pltpu.VMEM)
    return pl.pallas_call(
        functools.partial(front_kernel, peers, groups, halo, chunks, modes),
        out_shape=[
            jax.ShapeDtypeStruct((span, slab), pack.dtype),
            jax.ShapeDtypeStruct((groups, *marks.shape), marks.dtype),
            jax.ShapeDtypeStruct((block, third), pack.dtype),
            jax.ShapeDtypeStruct((groups, heads, rows), jnp.float32),
            jax.ShapeDtypeStruct((rows, third * groups), pack.dtype),
        ]
        + [gathered_shape(a, m, peers, groups) for a, m in zip(shards, modes)],
        in_specs=[anywhere] * (2 + count),
        out_specs=[anywhere, inside, inside, inside, anywhere] + [anywhere] * count,
        scratch_shapes=[
            pltpu.VMEM((span, slab), pack.dtype),
            pltpu.VMEM((groups, *marks.shape), marks.dtype),
            pltpu.VMEM((groups, heads, rows), jnp.float32),
            pltpu.VMEM((groups, heads, rows), jnp.float32),
            pltpu.VMEM((groups, heads, HEAD_DIM, rows), jnp.float32),
            pltpu.SemaphoreType.DMA((4 * groups,)),
            pltpu.SemaphoreType.DMA((4 * groups,)),
            pltpu.SemaphoreType.DMA((4,)),
            pltpu.SemaphoreType.DMA((groups,)),
            pltpu.SemaphoreType.DMA((groups,)),
            pltpu.SemaphoreType.DMA((len(chunks), slots)),
            pltpu.SemaphoreType.DMA((len(chunks), slots)),
            pltpu.SemaphoreType.DMA((len(chunks),)),
        ],
        compiler_params=pltpu.CompilerParams(
            collective_id=collective_id, has_side_effects=True, vmem_limit_bytes=48 * 2**20
        ),
    )(pack, marks, *shards)


def attend_back_kernel(
    ranges, query_ref, window_ref, marks_ref, norm_ref, out_ref, grad_ref,
    grad_query_ref, grad_pair_ref, acc,
):
    block = pl.program_id(0)
    rows = query_ref.shape[0]
    heads = query_ref.shape[1] // 3 // HEAD_DIM
    third = heads * HEAD_DIM

    @pl.when(block == 0)
    def _():
        grad_pair_ref[...] = jnp.zeros_like(grad_pair_ref)

    acc[...] = jnp.zeros_like(acc)
    deltas = []
    for pair in range(heads // 2):
        at = slice(pair * PAIR, (pair + 1) * PAIR)
        product = grad_ref[:, at].astype(jnp.float32) * out_ref[:, at].astype(jnp.float32)
        product = product.T
        for which in range(2):
            part = product[which * HEAD_DIM : (which + 1) * HEAD_DIM]
            deltas.append(jnp.sum(part, axis=0, keepdims=True))

    def step(tile, carry):
        keys_at = pl.ds(pl.multiple_of(tile * KEY_TILE, KEY_TILE), KEY_TILE)
        inside = inside_mask(marks_ref, tile, rows)
        for pair in range(heads // 2):
            lo = pair * PAIR
            keys = window_ref[keys_at, third + lo : third + lo + PAIR]
            keys_t = keys.T
            values = window_ref[keys_at, 2 * third + lo : 2 * third + lo + PAIR]
            queries = query_ref[:, lo : lo + PAIR]
            grads = grad_ref[:, lo : lo + PAIR]
            probs_both, scores_both, queries_both, grads_both = [], [], [], []
            for which in range(2):
                h = 2 * pair + which
                query, grad = only_head(queries, which), only_head(grads, which)
                scores = dot_rows(keys, query) * HEAD_DIM ** (-0.5)
                probs = jnp.where(inside, jnp.exp(scores - norm_ref[0, h : h + 1]), 0.0)
                grad_prob = dot_rows(values, grad)
                grad_score = (probs * (grad_prob - deltas[h])).astype(jnp.bfloat16)
                acc[h] += dot(keys_t[which * HEAD_DIM : (which + 1) * HEAD_DIM], grad_score)
                probs_both.append(probs.astype(jnp.bfloat16))
                scores_both.append(grad_score)
                queries_both.append(query)
                grads_both.append(grad)
            grad_key = dot(
                jnp.concatenate(scores_both, axis=1), jnp.concatenate(queries_both, axis=0)
            ) * HEAD_DIM ** (-0.5)
            grad_value = dot(
                jnp.concatenate(probs_both, axis=1), jnp.concatenate(grads_both, axis=0)
            )
            grad_pair_ref[keys_at, lo : lo + PAIR] += grad_key
            grad_pair_ref[keys_at, third + lo : third + lo + PAIR] += grad_value
        return carry

    lax.fori_loop(ranges[block, 0], ranges[block, 1], step, 0)
    for pair in range(heads // 2):
        both = jnp.concatenate([acc[2 * pair], acc[2 * pair + 1]], axis=0).T
        grad_query_ref[:, pair * PAIR : (pair + 1) * PAIR] = both * HEAD_DIM ** (-0.5)


def attend_back(ranges, window, marks, log_norm, attended, grad_attended, halo):
    groups, _, rows = marks.shape
    span, slab = window.shape
    third = slab // 3
    heads = third // HEAD_DIM
    first = halo // rows
    return pl.pallas_call(
        attend_back_kernel,
        grid_spec=pltpu.PrefetchScalarGridSpec(
            num_scalar_prefetch=1,
            grid=(groups,),
            in_specs=[
                pl.BlockSpec((rows, slab), lambda i, r: (first + i, 0)),
                pl.BlockSpec((span, slab), lambda i, r: (0, 0)),
                pl.BlockSpec((1, 8, rows), lambda i, r: (i, 0, 0)),
                pl.BlockSpec((1, heads, rows), lambda i, r: (i, 0, 0)),
                pl.BlockSpec((rows, third), lambda i, r: (i, 0)),
                pl.BlockSpec((rows, third), lambda i, r: (i, 0)),
            ],
            out_specs=[
                pl.BlockSpec((rows, third), lambda i, r: (i, 0)),
                pl.BlockSpec((span, 2 * third), lambda i, r: (0, 0)),
            ],
            scratch_shapes=[pltpu.VMEM((heads, HEAD_DIM, rows), jnp.float32)],
        ),
        out_shape=[
            jax.ShapeDtypeStruct((groups * rows, third), jnp.float32),
            jax.ShapeDtypeStruct((span, 2 * third), jnp.float32),
        ],
        compiler_params=pltpu.CompilerParams(vmem_limit_bytes=56 * 2**20),
    )(ranges, window, window, marks, log_norm, attended, grad_attended)


def with_column(matrix, column, extra):
    return jnp.concatenate([matrix, jnp.pad(column[:, None], ((0, 0), (0, extra - 1)))], axis=1)


def on_device(
    stream,
    cotangent,
    bounds,
    joined_proj,
    out_proj,
    wide_proj,
    down_proj,
    gain_first,
    gain_second,
    joined_momentum,
    out_momentum,
    wide_momentum,
    down_momentum,
    gain_first_momentum,
    gain_second_momentum,
    joined_variance,
    out_variance,
    wide_variance,
    down_variance,
    gain_first_variance,
    gain_second_variance,
):
    row_count = stream.shape[0]
    width = stream.shape[1]
    heads = width // HEAD_DIM
    both = ("dp", "group")
    gains = jnp.stack([gain_first, gain_second], axis=1)
    gains = jnp.pad(gains, ((0, 0), (0, GAIN_PAD - 2)))
    joined_gains = jnp.concatenate([joined_proj, gains], axis=1).astype(jnp.bfloat16)
    wide_shard = wide_proj.astype(jnp.bfloat16)
    joined_gains, wide_shard = gather_all(
        [joined_gains, wide_shard],
        pieces([joined_gains.shape[1], wide_shard.shape[1]], 1152),
        ("full", "group"),
        1,
    )
    shards = [wide_shard, out_proj.astype(jnp.bfloat16), down_proj.astype(jnp.bfloat16)]
    joined_half = joined_gains[:, : 3 * width]
    gain_one_half = joined_gains[:, 3 * width]
    gain_two_half = joined_gains[:, 3 * width + 1]
    gain_one = gain_one_half.astype(jnp.float32)
    gain_two = gain_two_half.astype(jnp.float32)
    ff_width = down_proj.shape[1]
    first_row = lax.axis_index(("dp", "group")) * row_count
    token_index = first_row + jnp.arange(row_count, dtype=jnp.int32)
    seq_starts = bounds[:, 0]
    seq_ends = bounds[:, 1]
    cosine, sine_table = rope_tables(token_index - seq_starts)
    normed_one, scale_one = normalize(stream)
    normed_in = (normed_one * gain_one).astype(jnp.bfloat16)
    joined_act = jnp.dot(normed_in, joined_half, preferred_element_type=jnp.float32)
    groups = lax.axis_size("group")
    block_rows = row_count * groups
    slab = width // groups

    def turned(columns):
        heads_part = columns.reshape(row_count, heads, HEAD_DIM)
        return rotate(heads_part, cosine, sine_table, 1.0).reshape(row_count, groups, slab)

    pack = jnp.stack(
        [
            turned(joined_act[:, :width]),
            turned(joined_act[:, width : 2 * width]),
            joined_act[:, 2 * width :].reshape(row_count, groups, slab),
        ],
        axis=2,
    )
    pack = pack.astype(jnp.bfloat16).reshape(row_count, 3 * width)
    block_first = lax.axis_index("dp") * block_rows
    marks = jnp.pad(bounds.T - (block_first - LMAX), ((0, 6), (0, 0)))
    window, marks_all, attended_heads, log_norm, attended, wide_half, out_half, down_half = front(
        pack, marks, shards, pieces([v.shape[1] for v in shards], 1408),
        ("grouped", "full", "full"), LMAX, 3,
    )
    ranges = jnp.stack(
        [marks_all[:, 0, 0] // KEY_TILE, (marks_all[:, 1, row_count - 1] + KEY_TILE - 1) // KEY_TILE],
        axis=1,
    )
    residual = stream + jnp.dot(attended, out_half, preferred_element_type=jnp.float32)
    normed_two, scale_two = normalize(residual)
    hidden_in = (normed_two * gain_two).astype(jnp.bfloat16)
    wide_act = jnp.dot(hidden_in, wide_half, preferred_element_type=jnp.float32)
    inner_part = wide_act[:, :ff_width]
    gate_part = wide_act[:, ff_width:]
    activation, gelu_slope = gelu_parts(inner_part)
    gated = (activation * gate_part).astype(jnp.bfloat16)
    output = residual + jnp.einsum(
        "rf,df->rd", gated, down_half, preferred_element_type=jnp.float32
    )
    cot_half = cotangent.astype(jnp.bfloat16)
    spare = -ff_width % 128
    down_local = jnp.einsum(
        "rd,rf->df", cot_half, jnp.pad(gated, ((0, 0), (0, spare))), preferred_element_type=jnp.float32
    )
    grad_gated = jnp.dot(cot_half, down_half, preferred_element_type=jnp.float32)
    grad_inner = (grad_gated * gate_part * gelu_slope).astype(jnp.bfloat16)
    grad_gate = (grad_gated * activation).astype(jnp.bfloat16)
    grad_wide = jnp.concatenate([grad_inner, grad_gate], axis=1)
    wide_local = jnp.einsum("rd,rf->df", hidden_in, grad_wide, preferred_element_type=jnp.float32)
    grad_hidden = jnp.einsum("rf,df->rd", grad_wide, wide_half, preferred_element_type=jnp.float32)
    gain_two_local = jnp.sum(grad_hidden * normed_two, axis=0)
    grad_resid = cotangent + norm_back(grad_hidden * gain_two, normed_two, scale_two)
    resid_half = grad_resid.astype(jnp.bfloat16)
    out_local = jnp.einsum("rd,re->de", attended, resid_half, preferred_element_type=jnp.float32)
    out_local = with_column(out_local, gain_two_local, OUT_PAD)
    grad_attended = jnp.einsum(
        "re,de->rd", resid_half, out_half, preferred_element_type=jnp.float32
    ).astype(jnp.bfloat16)
    grad_heads = swap(grad_attended, True, 5)
    grad_query, grad_window = attend_back(
        ranges, window, marks_all, log_norm, attended_heads, grad_heads, LMAX
    )
    peers = lax.axis_size("dp")
    up = [(i, i + 1) for i in range(peers - 1)]
    down = [(j, i) for i, j in up]
    rim = grad_window[:LMAX].astype(jnp.bfloat16), grad_window[block_rows + LMAX :].astype(jnp.bfloat16)
    from_next = lax.ppermute(rim[0], "dp", down).astype(jnp.float32)
    from_previous = lax.ppermute(rim[1], "dp", up).astype(jnp.float32)
    centre = grad_window[LMAX : LMAX + block_rows]
    extra = block_rows - LMAX
    centre = centre + jnp.pad(from_previous, ((0, extra), (0, 0)))
    centre = centre + jnp.pad(from_next, ((extra, 0), (0, 0)))
    block_tokens = block_first - LMAX + jnp.arange(LMAX, LMAX + block_rows, dtype=jnp.int32)
    block_starts = marks_all[:, 0, :].reshape(block_rows) + (block_first - LMAX)
    block_cos, block_sin = rope_tables(block_tokens - block_starts)

    def turned_back(columns):
        heads_part = columns.reshape(block_rows, heads // groups, HEAD_DIM)
        return rotate(heads_part, block_cos, block_sin, -1.0).reshape(block_rows, slab)

    grad_pack = jnp.concatenate(
        [turned_back(grad_query), turned_back(centre[:, :slab]), centre[:, slab:]], axis=1
    ).astype(jnp.bfloat16)
    grad_joined = swap(grad_pack, False, 6)
    grad_joined = grad_joined.reshape(row_count, groups, 3, slab)
    grad_joined = grad_joined.transpose(0, 2, 1, 3).reshape(row_count, 3 * width)
    joined_local = jnp.einsum(
        "rd,re->de", normed_in, grad_joined, preferred_element_type=jnp.float32
    )
    grad_normed = jnp.einsum(
        "re,de->rd", grad_joined, joined_half, preferred_element_type=jnp.float32
    )
    gain_one_local = jnp.sum(grad_normed * normed_one, axis=0)
    stream_grad = grad_resid + norm_back(grad_normed * gain_one, normed_one, scale_one)
    joined_local = with_column(joined_local, gain_one_local, GAIN_PAD)
    locals_half = [
        v.astype(jnp.bfloat16)
        for v in (wide_local, down_local, out_local, joined_local)
    ]
    wide_grad, down_sum, out_sum, joined_sum = scatter_all(
        locals_half, pieces([v.shape[1] for v in locals_half]), 2
    )
    joined_grad = joined_sum[:, : 3 * width]
    gain_first_grad = joined_sum[:, 3 * width]
    out_grad = out_sum[:, :width]
    gain_second_grad = out_sum[:, width]
    down_grad = down_sum[:, :ff_width]
    joined_new, joined_momentum_new, joined_variance_new = adam_step(
        joined_proj, joined_grad, joined_momentum, joined_variance, WEIGHT_DECAY
    )
    out_new, out_momentum_new, out_variance_new = adam_step(
        out_proj, out_grad, out_momentum, out_variance, WEIGHT_DECAY
    )
    wide_new, wide_momentum_new, wide_variance_new = adam_step(
        wide_proj, wide_grad, wide_momentum, wide_variance, WEIGHT_DECAY
    )
    down_new, down_momentum_new, down_variance_new = adam_step(
        down_proj, down_grad, down_momentum, down_variance, WEIGHT_DECAY
    )
    gain_first_new, gain_first_momentum_new, gain_first_variance_new = adam_step(
        gain_first, gain_first_grad, gain_first_momentum, gain_first_variance, 0.0
    )
    gain_second_new, gain_second_momentum_new, gain_second_variance_new = adam_step(
        gain_second, gain_second_grad, gain_second_momentum, gain_second_variance, 0.0
    )
    return (
        output,
        stream_grad,
        joined_grad,
        out_grad,
        wide_grad,
        down_grad,
        gain_first_grad,
        gain_second_grad,
        joined_new,
        out_new,
        wide_new,
        down_new,
        gain_first_new,
        gain_second_new,
        joined_momentum_new,
        out_momentum_new,
        wide_momentum_new,
        down_momentum_new,
        gain_first_momentum_new,
        gain_second_momentum_new,
        joined_variance_new,
        out_variance_new,
        wide_variance_new,
        down_variance_new,
        gain_first_variance_new,
        gain_second_variance_new,
    )


def solution(mesh):
    placed = (
        P(("dp", "group"), None),
        P(("dp", "group"), None),
        P(("dp", "group"), None),
        P(("dp", "group"), None),
        P(("dp", "group"), None),
        P(("dp", "group"), None),
        P(("dp", "group"), None),
        P(("dp", "group")),
        P(("dp", "group")),
        P(("dp", "group"), None),
        P(("dp", "group"), None),
        P(("dp", "group"), None),
        P(("dp", "group"), None),
        P(("dp", "group")),
        P(("dp", "group")),
        P(("dp", "group"), None),
        P(("dp", "group"), None),
        P(("dp", "group"), None),
        P(("dp", "group"), None),
        P(("dp", "group")),
        P(("dp", "group")),
    )
    return jax.shard_map(
        on_device,
        mesh=mesh,
        in_specs=placed,
        out_specs=(
            P(("dp", "group"), None),
            P(("dp", "group"), None),
            P(("dp", "group"), None),
            P(("dp", "group"), None),
            P(("dp", "group"), None),
            P(("dp", "group"), None),
            P(("dp", "group")),
            P(("dp", "group")),
            P(("dp", "group"), None),
            P(("dp", "group"), None),
            P(("dp", "group"), None),
            P(("dp", "group"), None),
            P(("dp", "group")),
            P(("dp", "group")),
            P(("dp", "group"), None),
            P(("dp", "group"), None),
            P(("dp", "group"), None),
            P(("dp", "group"), None),
            P(("dp", "group")),
            P(("dp", "group")),
            P(("dp", "group"), None),
            P(("dp", "group"), None),
            P(("dp", "group"), None),
            P(("dp", "group"), None),
            P(("dp", "group")),
            P(("dp", "group")),
        ),
        check_vma=False,
    )
```

```python
import functools
import math

import jax
import jax.numpy as jnp
from jax import lax
from jax.experimental import pallas as pl
from jax.experimental.pallas import tpu as pltpu
from jax.sharding import PartitionSpec as P

HEAD_DIM = 64
LMAX = 1024
STEP = 4
GAIN_PAD = 384
OUT_PAD = 128


EPSILON = 1e-05
ROPE_BASE = 160000.0
LEARN_RATE = 0.02
BETA_ONE = 0.9
BETA_TWO = 0.98
ADAM_EPSILON = 1e-06
WEIGHT_DECAY = 0.1
NEG_LARGE = -1e30
MESH = pl.DeviceIdType.MESH


def normalize(values):
    centred = values - jnp.mean(values, axis=1, keepdims=True)
    row_scale = lax.rsqrt(jnp.mean(centred * centred, axis=1, keepdims=True) + EPSILON)
    return (centred * row_scale, row_scale)


def norm_back(grad_hat, normed, row_scale):
    mean_one = jnp.mean(grad_hat, axis=1, keepdims=True)
    mean_two = jnp.mean(grad_hat * normed, axis=1, keepdims=True)
    return row_scale * (grad_hat - mean_one - normed * mean_two)


def rope_tables(positions):
    half_dim = HEAD_DIM // 2
    freqs = jnp.exp(
        jnp.arange(half_dim, dtype=jnp.float32) * (-2.0 * math.log(ROPE_BASE) / HEAD_DIM)
    )
    angles = positions.astype(jnp.float32)[:, None] * freqs[None, :]
    return (jnp.cos(angles), jnp.sin(angles))


def rotate(values, cosine, sine_table, sign):
    half_dim = values.shape[-1] // 2
    front_half = values[..., :half_dim]
    second = values[..., half_dim:]
    cos_part = cosine[:, None, :]
    sin_part = sine_table[:, None, :] * sign
    return jnp.concatenate(
        [front_half * cos_part - second * sin_part, second * cos_part + front_half * sin_part],
        axis=-1,
    )


def gelu_parts(inner_part):
    cdf_part = 0.5 * (1.0 + lax.erf(inner_part * (1.0 / math.sqrt(2.0))))
    activation = inner_part * cdf_part
    gelu_slope = cdf_part + inner_part * jnp.exp(-0.5 * inner_part * inner_part) * (
        1.0 / math.sqrt(2.0 * math.pi)
    )
    return (activation, gelu_slope)


def adam_step(weight, gradient, momentum, variance, decay_rate):
    new_momentum = BETA_ONE * momentum + (1.0 - BETA_ONE) * gradient
    new_variance = BETA_TWO * variance + (1.0 - BETA_TWO) * gradient * gradient
    update = (
        new_momentum
        / (1.0 - BETA_ONE**STEP)
        / (jnp.sqrt(new_variance / (1.0 - BETA_TWO**STEP)) + ADAM_EPSILON)
    )
    return (weight - LEARN_RATE * (update + decay_rate * weight), new_momentum, new_variance)


def grid_place(peers, groups):
    place, member = lax.axis_index("dp"), lax.axis_index("group")
    parity = lax.rem(place, 2)
    bits = []
    power = 2
    while power < peers:
        bits.append((1 - 2 * lax.rem(place // power, 2)) * power)
        power *= 2
    hops = [(1 - parity) * a + parity * b for a, b in zip(bits, reversed(bits))]
    return place, member, hops, 1 - 2 * parity


def combos(count):
    return [tuple((i >> p) & 1 for p in range(count)) for i in range(2**count)]


def offset(combo, hops):
    total = 0
    for taken, hop in zip(combo, hops):
        if taken:
            total = total + hop
    return total


def meet(place, member, hops, last, groups):
    barrier = pltpu.get_barrier_semaphore()
    for step in range(1, groups):
        pl.semaphore_signal(
            barrier, inc=1, device_id=(place, lax.rem(member + step, groups)), device_id_type=MESH
        )
    for hop in list(hops) + [last]:
        pl.semaphore_signal(barrier, inc=1, device_id=(place + hop, member), device_id_type=MESH)
    pl.semaphore_wait(barrier, groups - 1 + len(hops) + 1)


def pieces(widths, largest=2688):
    found = []
    for a, width in enumerate(widths):
        if width <= largest:
            found.append((a, 0, width))
            continue
        parts = -(-width // largest)
        part = -(-width // (128 * parts)) * 128
        for lo in range(0, width, part):
            found.append((a, lo, min(part, width - lo)))
    return tuple(found)


def gather_steps(position, groups, chunks, ins, outs, sems, modes):
    place, member, hops, last = position
    send_sem, recv_sem, own_sem = sems
    phases = len(hops)
    n_chunks = len(chunks)
    base = groups - 1

    def copy(src, dst, k, slot, device):
        return pltpu.make_async_remote_copy(
            src_ref=src, dst_ref=dst, send_sem=send_sem.at[k, slot], recv_sem=recv_sem.at[k, slot],
            device_id=device, device_id_type=MESH,
        )

    def block(k, combo):
        a, lo, width = chunks[k]
        rows = ins[a].shape[0] * (groups if modes[a] == "full" else 1)
        at = (place + offset(combo, hops)) * rows
        return outs[a].at[pl.ds(at, rows), pl.ds(lo, width)]

    pending = [{p: [] for p in range(phases + 1)} for _ in range(n_chunks)]

    def launch(k, combo):
        done = max([p + 1 for p, taken in enumerate(combo) if taken], default=0)
        ref = block(k, combo)
        for p in range(done, phases):
            slot = base + sum(2**q for q in range(p)) + sum(t << q for q, t in enumerate(combo[:p]))
            c = copy(ref, ref, k, slot, (place + hops[p], member))
            c.start()
            pending[k][p].append((c, combo))
        slot = base + (2**phases - 1) + sum(t << q for q, t in enumerate(combo))
        c = copy(ref, ref, k, slot, (place + last, member))
        c.start()
        pending[k][phases].append((c, combo))

    first, own = [], []
    for k, (a, lo, width) in enumerate(chunks):
        rows = ins[a].shape[0]
        start = {"full": (place * groups + member) * rows, "group": member * rows, "grouped": place * rows}
        mine = outs[a].at[pl.ds(start[modes[a]], rows), pl.ds(lo, width)]
        src = ins[a].at[:, pl.ds(lo, width)]
        keep = pltpu.make_async_copy(src, mine, own_sem.at[k])
        keep.start()
        row = []
        if modes[a] != "grouped":
            for step in range(1, groups):
                c = copy(src, mine, k, step - 1, (place, lax.rem(member + step, groups)))
                c.start()
                row.append(c)
        first.append(row)
        own.append(keep)
    for k, (a, _, _) in enumerate(chunks):
        if modes[a] == "grouped":
            own[k].wait()
            launch(k, (0,) * phases)
    yield

    for step in range(n_chunks + phases):
        for level in range(phases + 1):
            k = step - level
            if not 0 <= k < n_chunks:
                continue
            if level == 0:
                if modes[chunks[k][0]] == "grouped":
                    continue
                for c in first[k]:
                    c.wait_recv()
                own[k].wait()
                if modes[chunks[k][0]] == "full":
                    launch(k, (0,) * phases)
            else:
                p = level - 1
                for c, combo in pending[k][p]:
                    c.wait_recv()
                    launch(k, tuple(1 if q == p else t for q, t in enumerate(combo)))
        yield
    for k in range(n_chunks):
        for c, _ in pending[k][phases]:
            c.wait_recv()
    for k in range(n_chunks):
        for c in first[k]:
            c.wait_send()
        for p in pending[k]:
            for c, _ in pending[k][p]:
                c.wait_send()


def gather_kernel(peers, groups, chunks, modes, *refs):
    count = len(modes)
    ins, outs = refs[:count], refs[count : 2 * count]
    position = grid_place(peers, groups)
    meet(*position, groups)
    for _ in gather_steps(position, groups, chunks, ins, outs, refs[2 * count :], modes):
        pass


def gathered_shape(a, mode, peers, groups):
    copies = {"full": peers * groups, "group": groups, "grouped": peers}[mode]
    return jax.ShapeDtypeStruct((a.shape[0] * copies, a.shape[1]), a.dtype)


def gather_all(arrays, chunks, modes, collective_id):
    peers, groups = lax.axis_size("dp"), lax.axis_size("group")
    phases = peers.bit_length() - 2
    slots = groups - 1 + 2 ** (phases + 1) - 1
    return pl.pallas_call(
        functools.partial(gather_kernel, peers, groups, chunks, modes),
        out_shape=[gathered_shape(a, m, peers, groups) for a, m in zip(arrays, modes)],
        in_specs=[pl.BlockSpec(memory_space=pl.ANY)] * len(arrays),
        out_specs=[pl.BlockSpec(memory_space=pl.ANY)] * len(arrays),
        scratch_shapes=[
            pltpu.SemaphoreType.DMA((len(chunks), slots)),
            pltpu.SemaphoreType.DMA((len(chunks), slots)),
            pltpu.SemaphoreType.DMA((len(chunks),)),
        ],
        compiler_params=pltpu.CompilerParams(collective_id=collective_id, has_side_effects=True),
    )(*arrays)


def scatter_kernel(peers, groups, chunks, count, phases, swapped, *refs):
    n_chunks = len(chunks)
    extra = int(swapped)
    ins, outs = refs[:count], refs[count + extra : 2 * count + extra]
    rest = list(refs[2 * count + 2 * extra :])
    if swapped:
        swap_in, swap_out = refs[count], refs[2 * count + extra]
        *rest, swap_send, swap_recv, swap_own = rest
    send_sem, recv_sem, own_sem = rest[-3:]
    mine, from_core, from_group = (rest[i * n_chunks : (i + 1) * n_chunks] for i in range(3))
    from_hops = [rest[(3 + p) * n_chunks : (4 + p) * n_chunks] for p in range(phases)]
    place, member, hops, last = grid_place(peers, groups)
    meet(place, member, hops, last, groups)
    every = combos(phases)
    rows = mine[0].shape[1]
    shard = rows // groups
    tile = 16

    def copy(src, dst, k, slot, device):
        return pltpu.make_async_remote_copy(
            src_ref=src, dst_ref=dst, send_sem=send_sem.at[k, slot], recv_sem=recv_sem.at[k, slot],
            device_id=device, device_id_type=MESH,
        )

    def number(combo):
        return sum(t << q for q, t in enumerate(combo))

    def add_rows(target, source, at):
        def body(i, carry):
            span = pl.ds(pl.multiple_of(i * tile, tile), tile)
            total = target[at, span].astype(jnp.float32) + source[at, span].astype(jnp.float32)
            target[at, span] = total.astype(target.dtype)
            return carry

        lax.fori_loop(0, rows // tile, body, 0)

    swaps = []
    if swapped:
        span, slab = swap_out.shape[0], swap_in.shape[1]
        landing = swap_out.at[:, pl.ds(pl.multiple_of(member * slab, slab), slab)]
        for step in range(1, groups):
            to = lax.rem(member + step, groups)
            c = pltpu.make_async_remote_copy(
                src_ref=swap_in.at[pl.ds(to * span, span), :], dst_ref=landing,
                send_sem=swap_send.at[step - 1], recv_sem=swap_recv.at[step - 1],
                device_id=(place, to), device_id_type=MESH,
            )
            c.start()
            swaps.append(c)
        c = pltpu.make_async_copy(
            swap_in.at[pl.ds(member * span, span), :], landing, swap_own.at[0]
        )
        c.start()
        swaps.append(c)

    core_copies, own_copies = [], []
    for k, (a, lo, width) in enumerate(chunks):
        cols = pl.ds(lo, width)
        sent, kept = [], []
        for combo in every:
            s = number(combo)
            theirs = place + last + offset(combo, hops[::-1])
            c = copy(
                ins[a].at[pl.ds(theirs * rows, rows), cols], from_core[k].at[s], k, s,
                (place + last, member),
            )
            c.start()
            sent.append(c)
            ours = place + offset(combo, hops)
            c = pltpu.make_async_copy(
                ins[a].at[pl.ds(ours * rows, rows), cols], mine[k].at[s], own_sem.at[k, s]
            )
            c.start()
            kept.append(c)
        core_copies.append(sent)
        own_copies.append(kept)

    hop_copies = [[[] for _ in range(phases)] for _ in range(n_chunks)]
    group_copies = [[] for _ in range(n_chunks)]

    def send_on(k, p):
        if p < 0:
            for step in range(1, groups):
                to = lax.rem(member + step, groups)
                c = copy(
                    mine[k].at[0, pl.ds(pl.multiple_of(to * shard, shard), shard)],
                    from_group[k].at[step - 1],
                    k, 2 ** (phases + 1) - 1 + step - 1, (place, to),
                )
                c.start()
                group_copies[k].append(c)
            return
        base = 2**phases + sum(2**q for q in range(p))
        for combo in combos(p):
            s = number(combo)
            c = copy(
                mine[k].at[s + 2**p], from_hops[p][k].at[s], k, base + s,
                (place + hops[p], member),
            )
            c.start()
            hop_copies[k][p].append(c)

    for step in range(n_chunks + phases + 1):
        for level in range(phases + 2):
            k = step - level
            if not 0 <= k < n_chunks:
                continue
            a, lo, width = chunks[k]
            if level == 0:
                for combo in every:
                    s = number(combo)
                    core_copies[k][s].wait_recv()
                    own_copies[k][s].wait()
                    add_rows(mine[k], from_core[k], s)
                send_on(k, phases - 1)
            elif level <= phases:
                p = phases - level
                for s, c in enumerate(hop_copies[k][p]):
                    c.wait_recv()
                    add_rows(mine[k], from_hops[p][k], s)
                send_on(k, p - 1)
            else:
                for c in group_copies[k]:
                    c.wait_recv()
                own = pl.ds(pl.multiple_of(member * shard, shard), shard)
                total = mine[k][0, own].astype(jnp.float32)
                for step_in in range(groups - 1):
                    total = total + from_group[k][step_in].astype(jnp.float32)
                outs[a][:, pl.ds(lo, width)] = total
    for k in range(n_chunks):
        for c in core_copies[k] + group_copies[k]:
            c.wait_send()
        for p in range(phases):
            for c in hop_copies[k][p]:
                c.wait_send()
    for c in swaps:
        c.wait()


def scatter_all(arrays, chunks, collective_id, to_swap=None):
    peers, groups = lax.axis_size("dp"), lax.axis_size("group")
    phases = peers.bit_length() - 2
    slots = groups - 1 + 2 ** (phases + 1) - 1
    rows = arrays[0].shape[0] // peers
    shard = rows // groups
    kind = arrays[0].dtype
    swapped = [] if to_swap is None else [to_swap]
    return pl.pallas_call(
        functools.partial(scatter_kernel, peers, groups, chunks, len(arrays), phases, bool(swapped)),
        out_shape=[jax.ShapeDtypeStruct((shard, a.shape[1]), jnp.float32) for a in arrays]
        + [
            jax.ShapeDtypeStruct((x.shape[0] // groups, x.shape[1] * groups), x.dtype)
            for x in swapped
        ],
        in_specs=[pl.BlockSpec(memory_space=pl.ANY)] * (len(arrays) + len(swapped)),
        out_specs=[pl.BlockSpec(memory_space=pltpu.VMEM)] * len(arrays)
        + [pl.BlockSpec(memory_space=pl.ANY)] * len(swapped),
        scratch_shapes=[
            pltpu.VMEM((depth, height, width), kind)
            for depth, height in [(2**phases, rows)] * 2
            + [(groups - 1, shard)]
            + [(2**p, rows) for p in range(phases)]
            for _, _, width in chunks
        ]
        + [
            pltpu.SemaphoreType.DMA((len(chunks), slots)),
            pltpu.SemaphoreType.DMA((len(chunks), slots)),
            pltpu.SemaphoreType.DMA((len(chunks), 2**phases)),
        ]
        + [pltpu.SemaphoreType.DMA((n,)) for _ in swapped for n in (groups - 1, groups - 1, 1)],
        compiler_params=pltpu.CompilerParams(
            collective_id=collective_id, has_side_effects=True, vmem_limit_bytes=60 * 2**20
        ),
    )(*arrays, *swapped)


def swap_kernel(groups, to_heads, x, y, send_sem, recv_sem, own_sem):
    place, member = lax.axis_index("dp"), lax.axis_index("group")
    barrier = pltpu.get_barrier_semaphore()
    for step in range(1, groups):
        pl.semaphore_signal(
            barrier, inc=1, device_id=(place, lax.rem(member + step, groups)), device_id_type=MESH
        )
    pl.semaphore_wait(barrier, groups - 1)
    rows = x.shape[0] if to_heads else y.shape[0]
    slab = y.shape[1] if to_heads else x.shape[1]

    def ends(to):
        if to_heads:
            src = x.at[:, pl.ds(pl.multiple_of(to * slab, slab), slab)]
            return src, y.at[pl.ds(member * rows, rows), :]
        src = x.at[pl.ds(to * rows, rows), :]
        return src, y.at[:, pl.ds(pl.multiple_of(member * slab, slab), slab)]

    copies = []
    for step in range(1, groups):
        to = lax.rem(member + step, groups)
        src, dst = ends(to)
        c = pltpu.make_async_remote_copy(
            src_ref=src, dst_ref=dst, send_sem=send_sem.at[step - 1],
            recv_sem=recv_sem.at[step - 1], device_id=(place, to), device_id_type=MESH,
        )
        c.start()
        copies.append(c)
    own = pltpu.make_async_copy(*ends(member), own_sem.at[0])
    own.start()
    own.wait()
    for c in copies:
        c.wait()


def swap(x, to_heads, collective_id):
    groups = lax.axis_size("group")
    rows, columns = x.shape
    shape = (rows * groups, columns // groups) if to_heads else (rows // groups, columns * groups)
    return pl.pallas_call(
        functools.partial(swap_kernel, groups, to_heads),
        out_shape=jax.ShapeDtypeStruct(shape, x.dtype),
        in_specs=[pl.BlockSpec(memory_space=pl.ANY)],
        out_specs=pl.BlockSpec(memory_space=pl.ANY),
        scratch_shapes=[
            pltpu.SemaphoreType.DMA((groups - 1,)),
            pltpu.SemaphoreType.DMA((groups - 1,)),
            pltpu.SemaphoreType.DMA((1,)),
        ],
        compiler_params=pltpu.CompilerParams(collective_id=collective_id, has_side_effects=True),
    )(x)


KEY_TILE = 256
PAIR = 2 * HEAD_DIM


def dot(a, b):
    return jnp.dot(a, b, preferred_element_type=jnp.float32)


def dot_rows(a, b):
    return lax.dot_general(a, b, (((1,), (1,)), ((), ())), preferred_element_type=jnp.float32)


def only_head(values, which):
    lane = lax.broadcasted_iota(jnp.int32, values.shape, 1)
    inside = (lane >= which * HEAD_DIM) & (lane < (which + 1) * HEAD_DIM)
    return jnp.where(inside, values, jnp.zeros_like(values))


def inside_mask(marks_ref, tile, rows):
    key = tile * KEY_TILE + lax.broadcasted_iota(jnp.int32, (KEY_TILE, rows), 0)
    return (key >= marks_ref[0, 0:1, :]) & (key < marks_ref[0, 1:2, :])


def front_kernel(peers, groups, halo, chunks, modes, *refs):
    count = len(modes)
    pack, marks, *shards = refs[: 2 + count]
    rest = refs[2 + count :]
    window_out, marks_out, heads_out, norm_out, attended_out, *gathered = rest[: 5 + count]
    (
        window, marks_all, peak, total, acc, send_sem, recv_sem, own_sem, swap_send, swap_recv,
        *gather_sems,
    ) = rest[5 + count :]
    position = grid_place(peers, groups)
    place, member, hops, last = position
    rows = pack.shape[0]
    slab = window.shape[1]
    third = slab // 3
    heads = third // HEAD_DIM
    block = rows * groups
    has_up = place < peers - 1
    has_down = place > 0
    sides = (place + peers - 1) // peers + 1 - place // (peers - 1)

    barrier = pltpu.get_barrier_semaphore()
    for step in range(1, groups):
        pl.semaphore_signal(
            barrier, inc=1, device_id=(place, lax.rem(member + step, groups)), device_id_type=MESH
        )
    for hop in list(hops) + [last]:
        pl.semaphore_signal(barrier, inc=1, device_id=(place + hop, member), device_id_type=MESH)
    for near, there in ((1, has_up), (-1, has_down)):

        @pl.when(there)
        def _():
            pl.semaphore_signal(
                barrier, inc=1, device_id=(place + near, member), device_id_type=MESH
            )

    pl.semaphore_wait(barrier, groups + len(hops) + sides)

    def columns(of):
        return pl.ds(pl.multiple_of(of * slab, slab), slab)

    def copy(src, dst, slot, device):
        return pltpu.make_async_remote_copy(
            src_ref=src, dst_ref=dst, send_sem=send_sem.at[slot], recv_sem=recv_sem.at[slot],
            device_id=device, device_id_type=MESH,
        )

    mine = window.at[pl.ds(halo + member * rows, rows), :]
    from_group = []
    for step in range(1, groups):
        to = lax.rem(member + step, groups)
        c = copy(pack.at[:, columns(to)], mine, step - 1, (place, to))
        c.start()
        m = copy(marks.at[...], marks_all.at[member], groups - 2 + step, (place, to))
        m.start()
        from_group.append((c, m))
    own = pltpu.make_async_copy(pack.at[:, columns(member)], mine, own_sem.at[0])
    own.start()
    own_marks = pltpu.make_async_copy(marks.at[...], marks_all.at[member], own_sem.at[1])
    own_marks.start()

    gather = gather_steps(position, groups, chunks, shards, gathered, gather_sems, modes)
    next(gather)

    pairs_at = pl.ds(third, 2 * third)

    @pl.when(place == 0)
    def _():
        window[pl.ds(0, halo), :] = jnp.zeros((halo, slab), window.dtype)

    @pl.when(place == peers - 1)
    def _():
        window[pl.ds(halo + block, halo), :] = jnp.zeros((halo, slab), window.dtype)

    peak[...] = jnp.full_like(peak, NEG_LARGE)
    total[...] = jnp.zeros_like(total)
    acc[...] = jnp.zeros_like(acc)

    moved = []
    if halo == block:
        for step in range(groups):
            if step == 0:
                own.wait()
            else:
                from_group[step - 1][0].wait_recv()
            of = lax.rem(member + groups - step, groups)
            src = window.at[pl.ds(halo + of * rows, rows), pairs_at]
            up = copy(
                src, window.at[pl.ds(of * rows, rows), pairs_at],
                2 * groups - 2 + step, (place + 1, member),
            )
            down = copy(
                src, window.at[pl.ds(halo + block + of * rows, rows), pairs_at],
                3 * groups - 2 + step, (place - 1, member),
            )
            moved.append((up, down))

            @pl.when(has_up)
            def _():
                up.start()

            @pl.when(has_down)
            def _():
                down.start()

            next(gather, None)
    else:
        own.wait()
        for c, _ in from_group:
            c.wait_recv()
        up = copy(
            window.at[pl.ds(block, halo), pairs_at], window.at[pl.ds(0, halo), pairs_at],
            2 * groups - 2, (place + 1, member),
        )
        down = copy(
            window.at[pl.ds(halo, halo), pairs_at], window.at[pl.ds(halo + block, halo), pairs_at],
            3 * groups - 2, (place - 1, member),
        )
        moved.append((up, down))

        @pl.when(has_up)
        def _():
            up.start()

        @pl.when(has_down)
        def _():
            down.start()

    own_marks.wait()
    for _, m in from_group:
        m.wait_recv()

    def visit(i, first, stop):
        at = pl.ds(halo + i * rows, rows)

        def step(tile, carry):
            keys_at = pl.ds(pl.multiple_of(tile * KEY_TILE, KEY_TILE), KEY_TILE)
            key = tile * KEY_TILE + lax.broadcasted_iota(jnp.int32, (KEY_TILE, rows), 0)
            inside = (key >= marks_all[i, 0:1, :]) & (key < marks_all[i, 1:2, :])
            for pair in range(heads // 2):
                lo = pair * PAIR
                keys = window[keys_at, third + lo : third + lo + PAIR]
                values_t = window[keys_at, 2 * third + lo : 2 * third + lo + PAIR].T
                queries = window[at, lo : lo + PAIR]
                for which in range(2):
                    h = 2 * pair + which
                    scores = dot_rows(keys, only_head(queries, which)) * HEAD_DIM ** (-0.5)
                    scores = jnp.where(inside, scores, NEG_LARGE)
                    old = peak[i, h : h + 1]
                    new = jnp.maximum(old, jnp.max(scores, axis=0, keepdims=True))
                    probs = jnp.exp(scores - new)
                    fade = jnp.exp(old - new)
                    peak[i, h : h + 1] = new
                    total[i, h : h + 1] = total[i, h : h + 1] * fade + jnp.sum(
                        probs, axis=0, keepdims=True
                    )
                    mixed = dot(
                        values_t[which * HEAD_DIM : (which + 1) * HEAD_DIM],
                        probs.astype(jnp.bfloat16),
                    )
                    acc[i, h] = acc[i, h] * fade + mixed
            return carry

        if stop > first:
            lax.fori_loop(first, stop, step, 0)

    own_first, own_stop = halo // KEY_TILE, (halo + block) // KEY_TILE
    for i in range(groups):
        visit(i, own_first, own_stop)
        next(gather, None)

    for up, down in moved:

        @pl.when(has_up)
        def _():
            down.wait_recv()

        @pl.when(has_down)
        def _():
            up.wait_recv()

    keep = pltpu.make_async_copy(window, window_out, own_sem.at[2])
    keep.start()

    def give(i):
        return pltpu.make_async_remote_copy(
            src_ref=heads_out.at[pl.ds(i * rows, rows), :],
            dst_ref=attended_out.at[:, pl.ds(pl.multiple_of(member * third, third), third)],
            send_sem=swap_send.at[i], recv_sem=swap_recv.at[member],
            device_id=(place, i), device_id_type=MESH,
        )

    def keep_own(i):
        return pltpu.make_async_copy(
            heads_out.at[pl.ds(i * rows, rows), :],
            attended_out.at[:, pl.ds(i * third, third)],
            own_sem.at[3],
        )

    for i in range(groups):
        span = (i * rows // KEY_TILE, -(-(i * rows + rows + 2 * halo) // KEY_TILE))
        visit(i, span[0], min(own_first, span[1]))
        visit(i, max(own_stop, span[0]), span[1])
        for pair in range(heads // 2):
            parts = [acc[i, h] / total[i, h : h + 1] for h in (2 * pair, 2 * pair + 1)]
            both = jnp.concatenate(parts, axis=0).T
            heads_out[i * rows : (i + 1) * rows, pair * PAIR : (pair + 1) * PAIR] = both.astype(
                heads_out.dtype
            )

        @pl.when(member != i)
        def _():
            give(i).start()

        @pl.when(member == i)
        def _():
            keep_own(i).start()

        next(gather, None)
    norm_out[...] = peak[...] + jnp.log(total[...])
    marks_out[...] = marks_all[...]
    for _ in gather:
        pass

    for c, m in from_group:
        c.wait_send()
        m.wait_send()
    for up, down in moved:

        @pl.when(has_up)
        def _():
            up.wait_send()

        @pl.when(has_down)
        def _():
            down.wait_send()

    for i in range(groups):

        @pl.when(member != i)
        def _():
            give(i).wait_send()
            pltpu.make_async_remote_copy(
                src_ref=heads_out.at[pl.ds(i * rows, rows), :],
                dst_ref=attended_out.at[:, pl.ds(i * third, third)],
                send_sem=swap_send.at[i], recv_sem=swap_recv.at[i],
                device_id=(place, i), device_id_type=MESH,
            ).wait_recv()

        @pl.when(member == i)
        def _():
            keep_own(i).wait()

    keep.wait()


def front(pack, marks, shards, chunks, modes, halo, collective_id):
    peers, groups = lax.axis_size("dp"), lax.axis_size("group")
    rows, columns = pack.shape
    block = rows * groups
    span = block + 2 * halo
    slab = columns // groups
    third = slab // 3
    heads = third // HEAD_DIM
    phases = peers.bit_length() - 2
    slots = groups - 1 + 2 ** (phases + 1) - 1
    count = len(shards)
    anywhere, inside = pl.BlockSpec(memory_space=pl.ANY), pl.BlockSpec(memory_space=pltpu.VMEM)
    return pl.pallas_call(
        functools.partial(front_kernel, peers, groups, halo, chunks, modes),
        out_shape=[
            jax.ShapeDtypeStruct((span, slab), pack.dtype),
            jax.ShapeDtypeStruct((groups, *marks.shape), marks.dtype),
            jax.ShapeDtypeStruct((block, third), pack.dtype),
            jax.ShapeDtypeStruct((groups, heads, rows), jnp.float32),
            jax.ShapeDtypeStruct((rows, third * groups), pack.dtype),
        ]
        + [gathered_shape(a, m, peers, groups) for a, m in zip(shards, modes)],
        in_specs=[anywhere] * (2 + count),
        out_specs=[anywhere, inside, inside, inside, anywhere] + [anywhere] * count,
        scratch_shapes=[
            pltpu.VMEM((span, slab), pack.dtype),
            pltpu.VMEM((groups, *marks.shape), marks.dtype),
            pltpu.VMEM((groups, heads, rows), jnp.float32),
            pltpu.VMEM((groups, heads, rows), jnp.float32),
            pltpu.VMEM((groups, heads, HEAD_DIM, rows), jnp.float32),
            pltpu.SemaphoreType.DMA((4 * groups,)),
            pltpu.SemaphoreType.DMA((4 * groups,)),
            pltpu.SemaphoreType.DMA((4,)),
            pltpu.SemaphoreType.DMA((groups,)),
            pltpu.SemaphoreType.DMA((groups,)),
            pltpu.SemaphoreType.DMA((len(chunks), slots)),
            pltpu.SemaphoreType.DMA((len(chunks), slots)),
            pltpu.SemaphoreType.DMA((len(chunks),)),
        ],
        compiler_params=pltpu.CompilerParams(
            collective_id=collective_id, has_side_effects=True, vmem_limit_bytes=48 * 2**20
        ),
    )(pack, marks, *shards)


def attend_back_kernel(
    ranges, query_ref, window_ref, marks_ref, norm_ref, out_ref, grad_ref,
    grad_query_ref, grad_pair_ref, acc,
):
    block = pl.program_id(0)
    rows = query_ref.shape[0]
    heads = query_ref.shape[1] // 3 // HEAD_DIM
    third = heads * HEAD_DIM

    @pl.when(block == 0)
    def _():
        grad_pair_ref[...] = jnp.zeros_like(grad_pair_ref)

    acc[...] = jnp.zeros_like(acc)
    deltas = []
    for pair in range(heads // 2):
        at = slice(pair * PAIR, (pair + 1) * PAIR)
        product = grad_ref[:, at].astype(jnp.float32) * out_ref[:, at].astype(jnp.float32)
        product = product.T
        for which in range(2):
            part = product[which * HEAD_DIM : (which + 1) * HEAD_DIM]
            deltas.append(jnp.sum(part, axis=0, keepdims=True))

    def step(tile, carry):
        keys_at = pl.ds(pl.multiple_of(tile * KEY_TILE, KEY_TILE), KEY_TILE)
        inside = inside_mask(marks_ref, tile, rows)
        for pair in range(heads // 2):
            lo = pair * PAIR
            keys = window_ref[keys_at, third + lo : third + lo + PAIR]
            keys_t = keys.T
            values = window_ref[keys_at, 2 * third + lo : 2 * third + lo + PAIR]
            queries = query_ref[:, lo : lo + PAIR]
            grads = grad_ref[:, lo : lo + PAIR]
            probs_both, scores_both, queries_both, grads_both = [], [], [], []
            for which in range(2):
                h = 2 * pair + which
                query, grad = only_head(queries, which), only_head(grads, which)
                scores = dot_rows(keys, query) * HEAD_DIM ** (-0.5)
                probs = jnp.where(inside, jnp.exp(scores - norm_ref[0, h : h + 1]), 0.0)
                grad_prob = dot_rows(values, grad)
                grad_score = (probs * (grad_prob - deltas[h])).astype(jnp.bfloat16)
                acc[h] += dot(keys_t[which * HEAD_DIM : (which + 1) * HEAD_DIM], grad_score)
                probs_both.append(probs.astype(jnp.bfloat16))
                scores_both.append(grad_score)
                queries_both.append(query)
                grads_both.append(grad)
            grad_key = dot(
                jnp.concatenate(scores_both, axis=1), jnp.concatenate(queries_both, axis=0)
            ) * HEAD_DIM ** (-0.5)
            grad_value = dot(
                jnp.concatenate(probs_both, axis=1), jnp.concatenate(grads_both, axis=0)
            )
            grad_pair_ref[keys_at, lo : lo + PAIR] += grad_key
            grad_pair_ref[keys_at, third + lo : third + lo + PAIR] += grad_value
        return carry

    lax.fori_loop(ranges[block, 0], ranges[block, 1], step, 0)
    for pair in range(heads // 2):
        both = jnp.concatenate([acc[2 * pair], acc[2 * pair + 1]], axis=0).T
        grad_query_ref[:, pair * PAIR : (pair + 1) * PAIR] = both * HEAD_DIM ** (-0.5)


def attend_back(ranges, window, marks, log_norm, attended, grad_attended, halo):
    groups, _, rows = marks.shape
    span, slab = window.shape
    third = slab // 3
    heads = third // HEAD_DIM
    first = halo // rows
    return pl.pallas_call(
        attend_back_kernel,
        grid_spec=pltpu.PrefetchScalarGridSpec(
            num_scalar_prefetch=1,
            grid=(groups,),
            in_specs=[
                pl.BlockSpec((rows, slab), lambda i, r: (first + i, 0)),
                pl.BlockSpec((span, slab), lambda i, r: (0, 0)),
                pl.BlockSpec((1, 8, rows), lambda i, r: (i, 0, 0)),
                pl.BlockSpec((1, heads, rows), lambda i, r: (i, 0, 0)),
                pl.BlockSpec((rows, third), lambda i, r: (i, 0)),
                pl.BlockSpec((rows, third), lambda i, r: (i, 0)),
            ],
            out_specs=[
                pl.BlockSpec((rows, third), lambda i, r: (i, 0)),
                pl.BlockSpec((span, 2 * third), lambda i, r: (0, 0)),
            ],
            scratch_shapes=[pltpu.VMEM((heads, HEAD_DIM, rows), jnp.float32)],
        ),
        out_shape=[
            jax.ShapeDtypeStruct((groups * rows, third), jnp.float32),
            jax.ShapeDtypeStruct((span, 2 * third), jnp.float32),
        ],
        compiler_params=pltpu.CompilerParams(vmem_limit_bytes=56 * 2**20),
    )(ranges, window, window, marks, log_norm, attended, grad_attended)


def with_column(matrix, column, extra):
    return jnp.concatenate([matrix, jnp.pad(column[:, None], ((0, 0), (0, extra - 1)))], axis=1)


def on_device(
    stream,
    cotangent,
    bounds,
    joined_proj,
    out_proj,
    wide_proj,
    down_proj,
    gain_first,
    gain_second,
    joined_momentum,
    out_momentum,
    wide_momentum,
    down_momentum,
    gain_first_momentum,
    gain_second_momentum,
    joined_variance,
    out_variance,
    wide_variance,
    down_variance,
    gain_first_variance,
    gain_second_variance,
):
    row_count = stream.shape[0]
    width = stream.shape[1]
    heads = width // HEAD_DIM
    both = ("dp", "group")
    gains = jnp.stack([gain_first, gain_second], axis=1)
    gains = jnp.pad(gains, ((0, 0), (0, GAIN_PAD - 2)))
    joined_gains = jnp.concatenate([joined_proj, gains], axis=1).astype(jnp.bfloat16)
    wide_shard = wide_proj.astype(jnp.bfloat16)
    joined_gains, wide_shard = gather_all(
        [joined_gains, wide_shard],
        pieces([joined_gains.shape[1], wide_shard.shape[1]], 1152),
        ("full", "group"),
        1,
    )
    shards = [wide_shard, out_proj.astype(jnp.bfloat16), down_proj.astype(jnp.bfloat16)]
    joined_half = joined_gains[:, : 3 * width]
    gain_one_half = joined_gains[:, 3 * width]
    gain_two_half = joined_gains[:, 3 * width + 1]
    gain_one = gain_one_half.astype(jnp.float32)
    gain_two = gain_two_half.astype(jnp.float32)
    ff_width = down_proj.shape[1]
    first_row = lax.axis_index(("dp", "group")) * row_count
    token_index = first_row + jnp.arange(row_count, dtype=jnp.int32)
    seq_starts = bounds[:, 0]
    seq_ends = bounds[:, 1]
    cosine, sine_table = rope_tables(token_index - seq_starts)
    normed_one, scale_one = normalize(stream)
    normed_in = (normed_one * gain_one).astype(jnp.bfloat16)
    joined_act = jnp.dot(normed_in, joined_half, preferred_element_type=jnp.float32)
    groups = lax.axis_size("group")
    block_rows = row_count * groups
    slab = width // groups

    def turned(columns):
        heads_part = columns.reshape(row_count, heads, HEAD_DIM)
        return rotate(heads_part, cosine, sine_table, 1.0).reshape(row_count, groups, slab)

    pack = jnp.stack(
        [
            turned(joined_act[:, :width]),
            turned(joined_act[:, width : 2 * width]),
            joined_act[:, 2 * width :].reshape(row_count, groups, slab),
        ],
        axis=2,
    )
    pack = pack.astype(jnp.bfloat16).reshape(row_count, 3 * width)
    block_first = lax.axis_index("dp") * block_rows
    marks = jnp.pad(bounds.T - (block_first - LMAX), ((0, 6), (0, 0)))
    window, marks_all, attended_heads, log_norm, attended, wide_half, out_half, down_half = front(
        pack, marks, shards, pieces([v.shape[1] for v in shards], 1408),
        ("grouped", "full", "full"), LMAX, 3,
    )
    ranges = jnp.stack(
        [marks_all[:, 0, 0] // KEY_TILE, (marks_all[:, 1, row_count - 1] + KEY_TILE - 1) // KEY_TILE],
        axis=1,
    )
    residual = stream + jnp.dot(attended, out_half, preferred_element_type=jnp.float32)
    normed_two, scale_two = normalize(residual)
    hidden_in = (normed_two * gain_two).astype(jnp.bfloat16)
    wide_act = jnp.dot(hidden_in, wide_half, preferred_element_type=jnp.float32)
    inner_part = wide_act[:, :ff_width]
    gate_part = wide_act[:, ff_width:]
    activation, gelu_slope = gelu_parts(inner_part)
    gated = (activation * gate_part).astype(jnp.bfloat16)
    output = residual + jnp.einsum(
        "rf,df->rd", gated, down_half, preferred_element_type=jnp.float32
    )
    cot_half = cotangent.astype(jnp.bfloat16)
    spare = -ff_width % 128
    down_local = jnp.einsum(
        "rd,rf->df", cot_half, jnp.pad(gated, ((0, 0), (0, spare))), preferred_element_type=jnp.float32
    )
    grad_gated = jnp.dot(cot_half, down_half, preferred_element_type=jnp.float32)
    grad_inner = (grad_gated * gate_part * gelu_slope).astype(jnp.bfloat16)
    grad_gate = (grad_gated * activation).astype(jnp.bfloat16)
    grad_wide = jnp.concatenate([grad_inner, grad_gate], axis=1)
    wide_local = jnp.einsum("rd,rf->df", hidden_in, grad_wide, preferred_element_type=jnp.float32)
    grad_hidden = jnp.einsum("rf,df->rd", grad_wide, wide_half, preferred_element_type=jnp.float32)
    gain_two_local = jnp.sum(grad_hidden * normed_two, axis=0)
    grad_resid = cotangent + norm_back(grad_hidden * gain_two, normed_two, scale_two)
    resid_half = grad_resid.astype(jnp.bfloat16)
    out_local = jnp.einsum("rd,re->de", attended, resid_half, preferred_element_type=jnp.float32)
    out_local = with_column(out_local, gain_two_local, OUT_PAD)
    grad_attended = jnp.einsum(
        "re,de->rd", resid_half, out_half, preferred_element_type=jnp.float32
    ).astype(jnp.bfloat16)
    grad_heads = swap(grad_attended, True, 5)
    grad_query, grad_window = attend_back(
        ranges, window, marks_all, log_norm, attended_heads, grad_heads, LMAX
    )
    peers = lax.axis_size("dp")
    up = [(i, i + 1) for i in range(peers - 1)]
    down = [(j, i) for i, j in up]
    rim = grad_window[:LMAX].astype(jnp.bfloat16), grad_window[block_rows + LMAX :].astype(jnp.bfloat16)
    from_next = lax.ppermute(rim[0], "dp", down).astype(jnp.float32)
    from_previous = lax.ppermute(rim[1], "dp", up).astype(jnp.float32)
    centre = grad_window[LMAX : LMAX + block_rows]
    extra = block_rows - LMAX
    centre = centre + jnp.pad(from_previous, ((0, extra), (0, 0)))
    centre = centre + jnp.pad(from_next, ((extra, 0), (0, 0)))
    block_tokens = block_first - LMAX + jnp.arange(LMAX, LMAX + block_rows, dtype=jnp.int32)
    block_starts = marks_all[:, 0, :].reshape(block_rows) + (block_first - LMAX)
    block_cos, block_sin = rope_tables(block_tokens - block_starts)

    def turned_back(columns):
        heads_part = columns.reshape(block_rows, heads // groups, HEAD_DIM)
        return rotate(heads_part, block_cos, block_sin, -1.0).reshape(block_rows, slab)

    grad_pack = jnp.concatenate(
        [turned_back(grad_query), turned_back(centre[:, :slab]), centre[:, slab:]], axis=1
    ).astype(jnp.bfloat16)
    locals_half = [v.astype(jnp.bfloat16) for v in (wide_local, down_local, out_local)]
    wide_grad, down_sum, out_sum, grad_joined = scatter_all(
        locals_half, pieces([v.shape[1] for v in locals_half], 1408), 2, grad_pack
    )
    grad_joined = grad_joined.reshape(row_count, groups, 3, slab)
    grad_joined = grad_joined.transpose(0, 2, 1, 3).reshape(row_count, 3 * width)
    joined_local = jnp.einsum(
        "rd,re->de", normed_in, grad_joined, preferred_element_type=jnp.float32
    )
    grad_normed = jnp.einsum(
        "re,de->rd", grad_joined, joined_half, preferred_element_type=jnp.float32
    )
    gain_one_local = jnp.sum(grad_normed * normed_one, axis=0)
    stream_grad = grad_resid + norm_back(grad_normed * gain_one, normed_one, scale_one)
    joined_local = with_column(joined_local, gain_one_local, GAIN_PAD)
    joined_half_local = joined_local.astype(jnp.bfloat16)
    (joined_sum,) = scatter_all([joined_half_local], pieces([joined_local.shape[1]], 640), 6)
    joined_grad = joined_sum[:, : 3 * width]
    gain_first_grad = joined_sum[:, 3 * width]
    out_grad = out_sum[:, :width]
    gain_second_grad = out_sum[:, width]
    down_grad = down_sum[:, :ff_width]
    joined_new, joined_momentum_new, joined_variance_new = adam_step(
        joined_proj, joined_grad, joined_momentum, joined_variance, WEIGHT_DECAY
    )
    out_new, out_momentum_new, out_variance_new = adam_step(
        out_proj, out_grad, out_momentum, out_variance, WEIGHT_DECAY
    )
    wide_new, wide_momentum_new, wide_variance_new = adam_step(
        wide_proj, wide_grad, wide_momentum, wide_variance, WEIGHT_DECAY
    )
    down_new, down_momentum_new, down_variance_new = adam_step(
        down_proj, down_grad, down_momentum, down_variance, WEIGHT_DECAY
    )
    gain_first_new, gain_first_momentum_new, gain_first_variance_new = adam_step(
        gain_first, gain_first_grad, gain_first_momentum, gain_first_variance, 0.0
    )
    gain_second_new, gain_second_momentum_new, gain_second_variance_new = adam_step(
        gain_second, gain_second_grad, gain_second_momentum, gain_second_variance, 0.0
    )
    return (
        output,
        stream_grad,
        joined_grad,
        out_grad,
        wide_grad,
        down_grad,
        gain_first_grad,
        gain_second_grad,
        joined_new,
        out_new,
        wide_new,
        down_new,
        gain_first_new,
        gain_second_new,
        joined_momentum_new,
        out_momentum_new,
        wide_momentum_new,
        down_momentum_new,
        gain_first_momentum_new,
        gain_second_momentum_new,
        joined_variance_new,
        out_variance_new,
        wide_variance_new,
        down_variance_new,
        gain_first_variance_new,
        gain_second_variance_new,
    )


def solution(mesh):
    placed = (
        P(("dp", "group"), None),
        P(("dp", "group"), None),
        P(("dp", "group"), None),
        P(("dp", "group"), None),
        P(("dp", "group"), None),
        P(("dp", "group"), None),
        P(("dp", "group"), None),
        P(("dp", "group")),
        P(("dp", "group")),
        P(("dp", "group"), None),
        P(("dp", "group"), None),
        P(("dp", "group"), None),
        P(("dp", "group"), None),
        P(("dp", "group")),
        P(("dp", "group")),
        P(("dp", "group"), None),
        P(("dp", "group"), None),
        P(("dp", "group"), None),
        P(("dp", "group"), None),
        P(("dp", "group")),
        P(("dp", "group")),
    )
    return jax.shard_map(
        on_device,
        mesh=mesh,
        in_specs=placed,
        out_specs=(
            P(("dp", "group"), None),
            P(("dp", "group"), None),
            P(("dp", "group"), None),
            P(("dp", "group"), None),
            P(("dp", "group"), None),
            P(("dp", "group"), None),
            P(("dp", "group")),
            P(("dp", "group")),
            P(("dp", "group"), None),
            P(("dp", "group"), None),
            P(("dp", "group"), None),
            P(("dp", "group"), None),
            P(("dp", "group")),
            P(("dp", "group")),
            P(("dp", "group"), None),
            P(("dp", "group"), None),
            P(("dp", "group"), None),
            P(("dp", "group"), None),
            P(("dp", "group")),
            P(("dp", "group")),
            P(("dp", "group"), None),
            P(("dp", "group"), None),
            P(("dp", "group"), None),
            P(("dp", "group"), None),
            P(("dp", "group")),
            P(("dp", "group")),
        ),
        check_vma=False,
    )
```

```python
import functools
import math

import jax
import jax.numpy as jnp
from jax import lax
from jax.experimental import pallas as pl
from jax.experimental.pallas import tpu as pltpu
from jax.sharding import PartitionSpec as P

HEAD_DIM = 64
LMAX = 1024
STEP = 4
GAIN_PAD = 384
OUT_PAD = 128


EPSILON = 1e-05
ROPE_BASE = 160000.0
LEARN_RATE = 0.02
BETA_ONE = 0.9
BETA_TWO = 0.98
ADAM_EPSILON = 1e-06
WEIGHT_DECAY = 0.1
NEG_LARGE = -1e30
MESH = pl.DeviceIdType.MESH


def normalize(values):
    centred = values - jnp.mean(values, axis=1, keepdims=True)
    row_scale = lax.rsqrt(jnp.mean(centred * centred, axis=1, keepdims=True) + EPSILON)
    return (centred * row_scale, row_scale)


def norm_back(grad_hat, normed, row_scale):
    mean_one = jnp.mean(grad_hat, axis=1, keepdims=True)
    mean_two = jnp.mean(grad_hat * normed, axis=1, keepdims=True)
    return row_scale * (grad_hat - mean_one - normed * mean_two)


def rope_tables(positions):
    half_dim = HEAD_DIM // 2
    freqs = jnp.exp(
        jnp.arange(half_dim, dtype=jnp.float32) * (-2.0 * math.log(ROPE_BASE) / HEAD_DIM)
    )
    angles = positions.astype(jnp.float32)[:, None] * freqs[None, :]
    return (jnp.cos(angles), jnp.sin(angles))


def rotate(values, cosine, sine_table, sign):
    half_dim = values.shape[-1] // 2
    front_half = values[..., :half_dim]
    second = values[..., half_dim:]
    cos_part = cosine[:, None, :]
    sin_part = sine_table[:, None, :] * sign
    return jnp.concatenate(
        [front_half * cos_part - second * sin_part, second * cos_part + front_half * sin_part],
        axis=-1,
    )


def gelu_parts(inner_part):
    cdf_part = 0.5 * (1.0 + lax.erf(inner_part * (1.0 / math.sqrt(2.0))))
    activation = inner_part * cdf_part
    gelu_slope = cdf_part + inner_part * jnp.exp(-0.5 * inner_part * inner_part) * (
        1.0 / math.sqrt(2.0 * math.pi)
    )
    return (activation, gelu_slope)


def adam_step(weight, gradient, momentum, variance, decay_rate):
    new_momentum = BETA_ONE * momentum + (1.0 - BETA_ONE) * gradient
    new_variance = BETA_TWO * variance + (1.0 - BETA_TWO) * gradient * gradient
    update = (
        new_momentum
        / (1.0 - BETA_ONE**STEP)
        / (jnp.sqrt(new_variance / (1.0 - BETA_TWO**STEP)) + ADAM_EPSILON)
    )
    return (weight - LEARN_RATE * (update + decay_rate * weight), new_momentum, new_variance)


def grid_place(peers, groups):
    place, member = lax.axis_index("dp"), lax.axis_index("group")
    parity = lax.rem(place, 2)
    bits = []
    power = 2
    while power < peers:
        bits.append((1 - 2 * lax.rem(place // power, 2)) * power)
        power *= 2
    hops = [(1 - parity) * a + parity * b for a, b in zip(bits, reversed(bits))]
    return place, member, hops, 1 - 2 * parity


def combos(count):
    return [tuple((i >> p) & 1 for p in range(count)) for i in range(2**count)]


def offset(combo, hops):
    total = 0
    for taken, hop in zip(combo, hops):
        if taken:
            total = total + hop
    return total


def meet(place, member, hops, last, groups):
    barrier = pltpu.get_barrier_semaphore()
    for step in range(1, groups):
        pl.semaphore_signal(
            barrier, inc=1, device_id=(place, lax.rem(member + step, groups)), device_id_type=MESH
        )
    for hop in list(hops) + [last]:
        pl.semaphore_signal(barrier, inc=1, device_id=(place + hop, member), device_id_type=MESH)
    pl.semaphore_wait(barrier, groups - 1 + len(hops) + 1)


def pieces(widths, largest=2688):
    found = []
    for a, width in enumerate(widths):
        if width <= largest:
            found.append((a, 0, width))
            continue
        parts = -(-width // largest)
        part = -(-width // (128 * parts)) * 128
        for lo in range(0, width, part):
            found.append((a, lo, min(part, width - lo)))
    return tuple(found)


def gather_steps(position, groups, chunks, ins, outs, sems, modes):
    place, member, hops, last = position
    send_sem, recv_sem, own_sem = sems
    phases = len(hops)
    n_chunks = len(chunks)
    base = groups - 1

    def copy(src, dst, k, slot, device):
        return pltpu.make_async_remote_copy(
            src_ref=src, dst_ref=dst, send_sem=send_sem.at[k, slot], recv_sem=recv_sem.at[k, slot],
            device_id=device, device_id_type=MESH,
        )

    def block(k, combo):
        a, lo, width = chunks[k]
        rows = ins[a].shape[0] * (groups if modes[a] == "full" else 1)
        at = (place + offset(combo, hops)) * rows
        return outs[a].at[pl.ds(at, rows), pl.ds(lo, width)]

    pending = [{p: [] for p in range(phases + 1)} for _ in range(n_chunks)]

    def launch(k, combo):
        done = max([p + 1 for p, taken in enumerate(combo) if taken], default=0)
        ref = block(k, combo)
        for p in range(done, phases):
            slot = base + sum(2**q for q in range(p)) + sum(t << q for q, t in enumerate(combo[:p]))
            c = copy(ref, ref, k, slot, (place + hops[p], member))
            c.start()
            pending[k][p].append((c, combo))
        slot = base + (2**phases - 1) + sum(t << q for q, t in enumerate(combo))
        c = copy(ref, ref, k, slot, (place + last, member))
        c.start()
        pending[k][phases].append((c, combo))

    first, own = [], []
    for k, (a, lo, width) in enumerate(chunks):
        rows = ins[a].shape[0]
        start = {"full": (place * groups + member) * rows, "group": member * rows, "grouped": place * rows}
        mine = outs[a].at[pl.ds(start[modes[a]], rows), pl.ds(lo, width)]
        src = ins[a].at[:, pl.ds(lo, width)]
        keep = pltpu.make_async_copy(src, mine, own_sem.at[k])
        keep.start()
        row = []
        if modes[a] != "grouped":
            for step in range(1, groups):
                c = copy(src, mine, k, step - 1, (place, lax.rem(member + step, groups)))
                c.start()
                row.append(c)
        first.append(row)
        own.append(keep)
    yield
    for k, (a, _, _) in enumerate(chunks):
        if modes[a] == "grouped":
            own[k].wait()
            launch(k, (0,) * phases)
    yield

    for step in range(n_chunks + phases):
        for level in range(phases + 1):
            k = step - level
            if not 0 <= k < n_chunks:
                continue
            if level == 0:
                if modes[chunks[k][0]] == "grouped":
                    continue
                for c in first[k]:
                    c.wait_recv()
                own[k].wait()
                if modes[chunks[k][0]] == "full":
                    launch(k, (0,) * phases)
            else:
                p = level - 1
                for c, combo in pending[k][p]:
                    c.wait_recv()
                    launch(k, tuple(1 if q == p else t for q, t in enumerate(combo)))
        yield
    for k in range(n_chunks):
        for c, _ in pending[k][phases]:
            c.wait_recv()
    for k in range(n_chunks):
        for c in first[k]:
            c.wait_send()
        for p in pending[k]:
            for c, _ in pending[k][p]:
                c.wait_send()


def gather_kernel(peers, groups, chunks, modes, *refs):
    count = len(modes)
    ins, outs = refs[:count], refs[count : 2 * count]
    position = grid_place(peers, groups)
    meet(*position, groups)
    for _ in gather_steps(position, groups, chunks, ins, outs, refs[2 * count :], modes):
        pass


def gathered_shape(a, mode, peers, groups):
    copies = {"full": peers * groups, "group": groups, "grouped": peers}[mode]
    return jax.ShapeDtypeStruct((a.shape[0] * copies, a.shape[1]), a.dtype)


def gather_all(arrays, chunks, modes, collective_id):
    peers, groups = lax.axis_size("dp"), lax.axis_size("group")
    phases = peers.bit_length() - 2
    slots = groups - 1 + 2 ** (phases + 1) - 1
    return pl.pallas_call(
        functools.partial(gather_kernel, peers, groups, chunks, modes),
        out_shape=[gathered_shape(a, m, peers, groups) for a, m in zip(arrays, modes)],
        in_specs=[pl.BlockSpec(memory_space=pl.ANY)] * len(arrays),
        out_specs=[pl.BlockSpec(memory_space=pl.ANY)] * len(arrays),
        scratch_shapes=[
            pltpu.SemaphoreType.DMA((len(chunks), slots)),
            pltpu.SemaphoreType.DMA((len(chunks), slots)),
            pltpu.SemaphoreType.DMA((len(chunks),)),
        ],
        compiler_params=pltpu.CompilerParams(collective_id=collective_id, has_side_effects=True),
    )(*arrays)


def scatter_kernel(peers, groups, chunks, count, phases, swapped, *refs):
    n_chunks = len(chunks)
    extra = int(swapped)
    ins, outs = refs[:count], refs[count + extra : 2 * count + extra]
    rest = list(refs[2 * count + 2 * extra :])
    if swapped:
        swap_in, swap_out = refs[count], refs[2 * count + extra]
        *rest, swap_send, swap_recv, swap_own = rest
    send_sem, recv_sem, own_sem = rest[-3:]
    mine, from_core, from_group = (rest[i * n_chunks : (i + 1) * n_chunks] for i in range(3))
    from_hops = [rest[(3 + p) * n_chunks : (4 + p) * n_chunks] for p in range(phases)]
    place, member, hops, last = grid_place(peers, groups)
    meet(place, member, hops, last, groups)
    every = combos(phases)
    rows = mine[0].shape[1]
    shard = rows // groups
    tile = 16

    def copy(src, dst, k, slot, device):
        return pltpu.make_async_remote_copy(
            src_ref=src, dst_ref=dst, send_sem=send_sem.at[k, slot], recv_sem=recv_sem.at[k, slot],
            device_id=device, device_id_type=MESH,
        )

    def number(combo):
        return sum(t << q for q, t in enumerate(combo))

    def add_rows(target, source, at):
        def body(i, carry):
            span = pl.ds(pl.multiple_of(i * tile, tile), tile)
            total = target[at, span].astype(jnp.float32) + source[at, span].astype(jnp.float32)
            target[at, span] = total.astype(target.dtype)
            return carry

        lax.fori_loop(0, rows // tile, body, 0)

    swaps = []
    if swapped:
        span, slab = swap_out.shape[0], swap_in.shape[1]
        landing = swap_out.at[:, pl.ds(pl.multiple_of(member * slab, slab), slab)]
        for step in range(1, groups):
            to = lax.rem(member + step, groups)
            c = pltpu.make_async_remote_copy(
                src_ref=swap_in.at[pl.ds(to * span, span), :], dst_ref=landing,
                send_sem=swap_send.at[step - 1], recv_sem=swap_recv.at[step - 1],
                device_id=(place, to), device_id_type=MESH,
            )
            c.start()
            swaps.append(c)
        c = pltpu.make_async_copy(
            swap_in.at[pl.ds(member * span, span), :], landing, swap_own.at[0]
        )
        c.start()
        swaps.append(c)

    core_copies, own_copies = [], []
    for k, (a, lo, width) in enumerate(chunks):
        cols = pl.ds(lo, width)
        sent, kept = [], []
        for combo in every:
            s = number(combo)
            theirs = place + last + offset(combo, hops[::-1])
            c = copy(
                ins[a].at[pl.ds(theirs * rows, rows), cols], from_core[k].at[s], k, s,
                (place + last, member),
            )
            c.start()
            sent.append(c)
            ours = place + offset(combo, hops)
            c = pltpu.make_async_copy(
                ins[a].at[pl.ds(ours * rows, rows), cols], mine[k].at[s], own_sem.at[k, s]
            )
            c.start()
            kept.append(c)
        core_copies.append(sent)
        own_copies.append(kept)

    hop_copies = [[[] for _ in range(phases)] for _ in range(n_chunks)]
    group_copies = [[] for _ in range(n_chunks)]

    def send_on(k, p):
        if p < 0:
            for step in range(1, groups):
                to = lax.rem(member + step, groups)
                c = copy(
                    mine[k].at[0, pl.ds(pl.multiple_of(to * shard, shard), shard)],
                    from_group[k].at[step - 1],
                    k, 2 ** (phases + 1) - 1 + step - 1, (place, to),
                )
                c.start()
                group_copies[k].append(c)
            return
        base = 2**phases + sum(2**q for q in range(p))
        for combo in combos(p):
            s = number(combo)
            c = copy(
                mine[k].at[s + 2**p], from_hops[p][k].at[s], k, base + s,
                (place + hops[p], member),
            )
            c.start()
            hop_copies[k][p].append(c)

    for step in range(n_chunks + phases + 1):
        for level in range(phases + 2):
            k = step - level
            if not 0 <= k < n_chunks:
                continue
            a, lo, width = chunks[k]
            if level == 0:
                for combo in every:
                    s = number(combo)
                    core_copies[k][s].wait_recv()
                    own_copies[k][s].wait()
                    add_rows(mine[k], from_core[k], s)
                send_on(k, phases - 1)
            elif level <= phases:
                p = phases - level
                for s, c in enumerate(hop_copies[k][p]):
                    c.wait_recv()
                    add_rows(mine[k], from_hops[p][k], s)
                send_on(k, p - 1)
            else:
                for c in group_copies[k]:
                    c.wait_recv()
                own = pl.ds(pl.multiple_of(member * shard, shard), shard)
                total = mine[k][0, own].astype(jnp.float32)
                for step_in in range(groups - 1):
                    total = total + from_group[k][step_in].astype(jnp.float32)
                outs[a][:, pl.ds(lo, width)] = total
    for k in range(n_chunks):
        for c in core_copies[k] + group_copies[k]:
            c.wait_send()
        for p in range(phases):
            for c in hop_copies[k][p]:
                c.wait_send()
    for c in swaps:
        c.wait()


def scatter_all(arrays, chunks, collective_id, to_swap=None):
    peers, groups = lax.axis_size("dp"), lax.axis_size("group")
    phases = peers.bit_length() - 2
    slots = groups - 1 + 2 ** (phases + 1) - 1
    rows = arrays[0].shape[0] // peers
    shard = rows // groups
    kind = arrays[0].dtype
    swapped = [] if to_swap is None else [to_swap]
    return pl.pallas_call(
        functools.partial(scatter_kernel, peers, groups, chunks, len(arrays), phases, bool(swapped)),
        out_shape=[jax.ShapeDtypeStruct((shard, a.shape[1]), jnp.float32) for a in arrays]
        + [
            jax.ShapeDtypeStruct((x.shape[0] // groups, x.shape[1] * groups), x.dtype)
            for x in swapped
        ],
        in_specs=[pl.BlockSpec(memory_space=pl.ANY)] * (len(arrays) + len(swapped)),
        out_specs=[pl.BlockSpec(memory_space=pltpu.VMEM)] * len(arrays)
        + [pl.BlockSpec(memory_space=pl.ANY)] * len(swapped),
        scratch_shapes=[
            pltpu.VMEM((depth, height, width), kind)
            for depth, height in [(2**phases, rows)] * 2
            + [(groups - 1, shard)]
            + [(2**p, rows) for p in range(phases)]
            for _, _, width in chunks
        ]
        + [
            pltpu.SemaphoreType.DMA((len(chunks), slots)),
            pltpu.SemaphoreType.DMA((len(chunks), slots)),
            pltpu.SemaphoreType.DMA((len(chunks), 2**phases)),
        ]
        + [pltpu.SemaphoreType.DMA((n,)) for _ in swapped for n in (groups - 1, groups - 1, 1)],
        compiler_params=pltpu.CompilerParams(
            collective_id=collective_id, has_side_effects=True, vmem_limit_bytes=60 * 2**20
        ),
    )(*arrays, *swapped)


def swap_kernel(groups, to_heads, x, y, send_sem, recv_sem, own_sem):
    place, member = lax.axis_index("dp"), lax.axis_index("group")
    barrier = pltpu.get_barrier_semaphore()
    for step in range(1, groups):
        pl.semaphore_signal(
            barrier, inc=1, device_id=(place, lax.rem(member + step, groups)), device_id_type=MESH
        )
    pl.semaphore_wait(barrier, groups - 1)
    rows = x.shape[0] if to_heads else y.shape[0]
    slab = y.shape[1] if to_heads else x.shape[1]

    def ends(to):
        if to_heads:
            src = x.at[:, pl.ds(pl.multiple_of(to * slab, slab), slab)]
            return src, y.at[pl.ds(member * rows, rows), :]
        src = x.at[pl.ds(to * rows, rows), :]
        return src, y.at[:, pl.ds(pl.multiple_of(member * slab, slab), slab)]

    copies = []
    for step in range(1, groups):
        to = lax.rem(member + step, groups)
        src, dst = ends(to)
        c = pltpu.make_async_remote_copy(
            src_ref=src, dst_ref=dst, send_sem=send_sem.at[step - 1],
            recv_sem=recv_sem.at[step - 1], device_id=(place, to), device_id_type=MESH,
        )
        c.start()
        copies.append(c)
    own = pltpu.make_async_copy(*ends(member), own_sem.at[0])
    own.start()
    own.wait()
    for c in copies:
        c.wait()


def swap(x, to_heads, collective_id):
    groups = lax.axis_size("group")
    rows, columns = x.shape
    shape = (rows * groups, columns // groups) if to_heads else (rows // groups, columns * groups)
    return pl.pallas_call(
        functools.partial(swap_kernel, groups, to_heads),
        out_shape=jax.ShapeDtypeStruct(shape, x.dtype),
        in_specs=[pl.BlockSpec(memory_space=pl.ANY)],
        out_specs=pl.BlockSpec(memory_space=pl.ANY),
        scratch_shapes=[
            pltpu.SemaphoreType.DMA((groups - 1,)),
            pltpu.SemaphoreType.DMA((groups - 1,)),
            pltpu.SemaphoreType.DMA((1,)),
        ],
        compiler_params=pltpu.CompilerParams(collective_id=collective_id, has_side_effects=True),
    )(x)


KEY_TILE = 256
PAIR = 2 * HEAD_DIM


def dot(a, b):
    return jnp.dot(a, b, preferred_element_type=jnp.float32)


def dot_rows(a, b):
    return lax.dot_general(a, b, (((1,), (1,)), ((), ())), preferred_element_type=jnp.float32)


def only_head(values, which):
    lane = lax.broadcasted_iota(jnp.int32, values.shape, 1)
    inside = (lane >= which * HEAD_DIM) & (lane < (which + 1) * HEAD_DIM)
    return jnp.where(inside, values, jnp.zeros_like(values))


def inside_mask(marks_ref, tile, rows):
    key = tile * KEY_TILE + lax.broadcasted_iota(jnp.int32, (KEY_TILE, rows), 0)
    return (key >= marks_ref[0, 0:1, :]) & (key < marks_ref[0, 1:2, :])


def front_kernel(peers, groups, halo, chunks, modes, *refs):
    count = len(modes)
    pack, marks, *shards = refs[: 2 + count]
    rest = refs[2 + count :]
    window_out, marks_out, heads_out, norm_out, attended_out, *gathered = rest[: 5 + count]
    (
        window, marks_all, peak, total, acc, send_sem, recv_sem, own_sem, swap_send, swap_recv,
        *gather_sems,
    ) = rest[5 + count :]
    position = grid_place(peers, groups)
    place, member, hops, last = position
    rows = pack.shape[0]
    slab = window.shape[1]
    third = slab // 3
    heads = third // HEAD_DIM
    block = rows * groups
    has_up = place < peers - 1
    has_down = place > 0
    sides = (place + peers - 1) // peers + 1 - place // (peers - 1)

    barrier = pltpu.get_barrier_semaphore()
    for step in range(1, groups):
        pl.semaphore_signal(
            barrier, inc=1, device_id=(place, lax.rem(member + step, groups)), device_id_type=MESH
        )
    for hop in list(hops) + [last]:
        pl.semaphore_signal(barrier, inc=1, device_id=(place + hop, member), device_id_type=MESH)
    for near, there in ((1, has_up), (-1, has_down)):

        @pl.when(there)
        def _():
            pl.semaphore_signal(
                barrier, inc=1, device_id=(place + near, member), device_id_type=MESH
            )

    pl.semaphore_wait(barrier, groups + len(hops) + sides)

    def columns(of):
        return pl.ds(pl.multiple_of(of * slab, slab), slab)

    def copy(src, dst, slot, device):
        return pltpu.make_async_remote_copy(
            src_ref=src, dst_ref=dst, send_sem=send_sem.at[slot], recv_sem=recv_sem.at[slot],
            device_id=device, device_id_type=MESH,
        )

    mine = window.at[pl.ds(halo + member * rows, rows), :]
    from_group = []
    for step in range(1, groups):
        to = lax.rem(member + step, groups)
        c = copy(pack.at[:, columns(to)], mine, step - 1, (place, to))
        c.start()
        m = copy(marks.at[...], marks_all.at[member], groups - 2 + step, (place, to))
        m.start()
        from_group.append((c, m))
    own = pltpu.make_async_copy(pack.at[:, columns(member)], mine, own_sem.at[0])
    own.start()
    own_marks = pltpu.make_async_copy(marks.at[...], marks_all.at[member], own_sem.at[1])
    own_marks.start()

    gather = gather_steps(position, groups, chunks, shards, gathered, gather_sems, modes)
    next(gather)

    pairs_at = pl.ds(third, 2 * third)

    @pl.when(place == 0)
    def _():
        window[pl.ds(0, halo), :] = jnp.zeros((halo, slab), window.dtype)

    @pl.when(place == peers - 1)
    def _():
        window[pl.ds(halo + block, halo), :] = jnp.zeros((halo, slab), window.dtype)

    peak[...] = jnp.full_like(peak, NEG_LARGE)
    total[...] = jnp.zeros_like(total)
    acc[...] = jnp.zeros_like(acc)

    moved = []
    if halo == block:
        for step in range(groups):
            if step == 0:
                own.wait()
            else:
                from_group[step - 1][0].wait_recv()
            of = lax.rem(member + groups - step, groups)
            src = window.at[pl.ds(halo + of * rows, rows), pairs_at]
            up = copy(
                src, window.at[pl.ds(of * rows, rows), pairs_at],
                2 * groups - 2 + step, (place + 1, member),
            )
            down = copy(
                src, window.at[pl.ds(halo + block + of * rows, rows), pairs_at],
                3 * groups - 2 + step, (place - 1, member),
            )
            moved.append((up, down))

            @pl.when(has_up)
            def _():
                up.start()

            @pl.when(has_down)
            def _():
                down.start()

            next(gather, None)
    else:
        own.wait()
        for c, _ in from_group:
            c.wait_recv()
        up = copy(
            window.at[pl.ds(block, halo), pairs_at], window.at[pl.ds(0, halo), pairs_at],
            2 * groups - 2, (place + 1, member),
        )
        down = copy(
            window.at[pl.ds(halo, halo), pairs_at], window.at[pl.ds(halo + block, halo), pairs_at],
            3 * groups - 2, (place - 1, member),
        )
        moved.append((up, down))

        @pl.when(has_up)
        def _():
            up.start()

        @pl.when(has_down)
        def _():
            down.start()

    own_marks.wait()
    for _, m in from_group:
        m.wait_recv()

    def visit(i, first, stop):
        at = pl.ds(halo + i * rows, rows)

        def step(tile, carry):
            keys_at = pl.ds(pl.multiple_of(tile * KEY_TILE, KEY_TILE), KEY_TILE)
            key = tile * KEY_TILE + lax.broadcasted_iota(jnp.int32, (KEY_TILE, rows), 0)
            inside = (key >= marks_all[i, 0:1, :]) & (key < marks_all[i, 1:2, :])
            for pair in range(heads // 2):
                lo = pair * PAIR
                keys = window[keys_at, third + lo : third + lo + PAIR]
                values_t = window[keys_at, 2 * third + lo : 2 * third + lo + PAIR].T
                queries = window[at, lo : lo + PAIR] * jnp.bfloat16(HEAD_DIM ** (-0.5))
                for which in range(2):
                    h = 2 * pair + which
                    scores = dot_rows(keys, only_head(queries, which))
                    scores = jnp.where(inside, scores, NEG_LARGE)
                    old = peak[i, h : h + 1]
                    new = jnp.maximum(old, jnp.max(scores, axis=0, keepdims=True))
                    probs = jnp.exp(scores - new)
                    fade = jnp.exp(old - new)
                    peak[i, h : h + 1] = new
                    total[i, h : h + 1] = total[i, h : h + 1] * fade + jnp.sum(
                        probs, axis=0, keepdims=True
                    )
                    mixed = dot(
                        values_t[which * HEAD_DIM : (which + 1) * HEAD_DIM],
                        probs.astype(jnp.bfloat16),
                    )
                    acc[i, h] = acc[i, h] * fade + mixed
            return carry

        if stop > first:
            lax.fori_loop(first, stop, step, 0)

    own_first, own_stop = halo // KEY_TILE, (halo + block) // KEY_TILE
    for i in range(groups):
        visit(i, own_first, own_stop)
        next(gather, None)

    for up, down in moved:

        @pl.when(has_up)
        def _():
            down.wait_recv()

        @pl.when(has_down)
        def _():
            up.wait_recv()

    keep = pltpu.make_async_copy(window, window_out, own_sem.at[2])
    keep.start()

    def give(i):
        return pltpu.make_async_remote_copy(
            src_ref=heads_out.at[pl.ds(i * rows, rows), :],
            dst_ref=attended_out.at[:, pl.ds(pl.multiple_of(member * third, third), third)],
            send_sem=swap_send.at[i], recv_sem=swap_recv.at[member],
            device_id=(place, i), device_id_type=MESH,
        )

    def keep_own(i):
        return pltpu.make_async_copy(
            heads_out.at[pl.ds(i * rows, rows), :],
            attended_out.at[:, pl.ds(i * third, third)],
            own_sem.at[3],
        )

    for i in range(groups):
        span = (i * rows // KEY_TILE, -(-(i * rows + rows + 2 * halo) // KEY_TILE))
        visit(i, span[0], min(own_first, span[1]))
        visit(i, max(own_stop, span[0]), span[1])
        for pair in range(heads // 2):
            parts = [acc[i, h] / total[i, h : h + 1] for h in (2 * pair, 2 * pair + 1)]
            both = jnp.concatenate(parts, axis=0).T
            heads_out[i * rows : (i + 1) * rows, pair * PAIR : (pair + 1) * PAIR] = both.astype(
                heads_out.dtype
            )

        @pl.when(member != i)
        def _():
            give(i).start()

        @pl.when(member == i)
        def _():
            keep_own(i).start()

        next(gather, None)
    norm_out[...] = peak[...] + jnp.log(total[...])
    marks_out[...] = marks_all[...]
    for _ in gather:
        pass

    for c, m in from_group:
        c.wait_send()
        m.wait_send()
    for up, down in moved:

        @pl.when(has_up)
        def _():
            up.wait_send()

        @pl.when(has_down)
        def _():
            down.wait_send()

    for i in range(groups):

        @pl.when(member != i)
        def _():
            give(i).wait_send()
            pltpu.make_async_remote_copy(
                src_ref=heads_out.at[pl.ds(i * rows, rows), :],
                dst_ref=attended_out.at[:, pl.ds(i * third, third)],
                send_sem=swap_send.at[i], recv_sem=swap_recv.at[i],
                device_id=(place, i), device_id_type=MESH,
            ).wait_recv()

        @pl.when(member == i)
        def _():
            keep_own(i).wait()

    keep.wait()


def front(pack, marks, shards, chunks, modes, halo, collective_id):
    peers, groups = lax.axis_size("dp"), lax.axis_size("group")
    rows, columns = pack.shape
    block = rows * groups
    span = block + 2 * halo
    slab = columns // groups
    third = slab // 3
    heads = third // HEAD_DIM
    phases = peers.bit_length() - 2
    slots = groups - 1 + 2 ** (phases + 1) - 1
    count = len(shards)
    anywhere, inside = pl.BlockSpec(memory_space=pl.ANY), pl.BlockSpec(memory_space=pltpu.VMEM)
    return pl.pallas_call(
        functools.partial(front_kernel, peers, groups, halo, chunks, modes),
        out_shape=[
            jax.ShapeDtypeStruct((span, slab), pack.dtype),
            jax.ShapeDtypeStruct((groups, *marks.shape), marks.dtype),
            jax.ShapeDtypeStruct((block, third), pack.dtype),
            jax.ShapeDtypeStruct((groups, heads, rows), jnp.float32),
            jax.ShapeDtypeStruct((rows, third * groups), pack.dtype),
        ]
        + [gathered_shape(a, m, peers, groups) for a, m in zip(shards, modes)],
        in_specs=[anywhere] * (2 + count),
        out_specs=[anywhere, inside, inside, inside, anywhere] + [anywhere] * count,
        scratch_shapes=[
            pltpu.VMEM((span, slab), pack.dtype),
            pltpu.VMEM((groups, *marks.shape), marks.dtype),
            pltpu.VMEM((groups, heads, rows), jnp.float32),
            pltpu.VMEM((groups, heads, rows), jnp.float32),
            pltpu.VMEM((groups, heads, HEAD_DIM, rows), jnp.float32),
            pltpu.SemaphoreType.DMA((4 * groups,)),
            pltpu.SemaphoreType.DMA((4 * groups,)),
            pltpu.SemaphoreType.DMA((4,)),
            pltpu.SemaphoreType.DMA((groups,)),
            pltpu.SemaphoreType.DMA((groups,)),
            pltpu.SemaphoreType.DMA((len(chunks), slots)),
            pltpu.SemaphoreType.DMA((len(chunks), slots)),
            pltpu.SemaphoreType.DMA((len(chunks),)),
        ],
        compiler_params=pltpu.CompilerParams(
            collective_id=collective_id, has_side_effects=True, vmem_limit_bytes=48 * 2**20
        ),
    )(pack, marks, *shards)


def attend_back_kernel(
    ranges, query_ref, window_ref, marks_ref, norm_ref, out_ref, grad_ref,
    grad_query_ref, grad_pair_ref, acc,
):
    block = pl.program_id(0)
    rows = query_ref.shape[0]
    heads = query_ref.shape[1] // 3 // HEAD_DIM
    third = heads * HEAD_DIM

    @pl.when(block == 0)
    def _():
        grad_pair_ref[...] = jnp.zeros_like(grad_pair_ref)

    acc[...] = jnp.zeros_like(acc)
    deltas = []
    for pair in range(heads // 2):
        at = slice(pair * PAIR, (pair + 1) * PAIR)
        product = grad_ref[:, at].astype(jnp.float32) * out_ref[:, at].astype(jnp.float32)
        product = product.T
        for which in range(2):
            part = product[which * HEAD_DIM : (which + 1) * HEAD_DIM]
            deltas.append(jnp.sum(part, axis=0, keepdims=True))

    def step(tile, carry):
        keys_at = pl.ds(pl.multiple_of(tile * KEY_TILE, KEY_TILE), KEY_TILE)
        inside = inside_mask(marks_ref, tile, rows)
        for pair in range(heads // 2):
            lo = pair * PAIR
            keys = window_ref[keys_at, third + lo : third + lo + PAIR]
            keys_t = keys.T
            values = window_ref[keys_at, 2 * third + lo : 2 * third + lo + PAIR]
            queries = query_ref[:, lo : lo + PAIR] * jnp.bfloat16(HEAD_DIM ** (-0.5))
            grads = grad_ref[:, lo : lo + PAIR]
            probs_both, scores_both, queries_both, grads_both = [], [], [], []
            for which in range(2):
                h = 2 * pair + which
                query, grad = only_head(queries, which), only_head(grads, which)
                scores = dot_rows(keys, query)
                probs = jnp.where(inside, jnp.exp(scores - norm_ref[0, h : h + 1]), 0.0)
                grad_prob = dot_rows(values, grad)
                grad_score = (probs * (grad_prob - deltas[h])).astype(jnp.bfloat16)
                acc[h] += dot(keys_t[which * HEAD_DIM : (which + 1) * HEAD_DIM], grad_score)
                probs_both.append(probs.astype(jnp.bfloat16))
                scores_both.append(grad_score)
                queries_both.append(query)
                grads_both.append(grad)
            grad_key = dot(
                jnp.concatenate(scores_both, axis=1), jnp.concatenate(queries_both, axis=0)
            )
            grad_value = dot(
                jnp.concatenate(probs_both, axis=1), jnp.concatenate(grads_both, axis=0)
            )
            grad_pair_ref[keys_at, lo : lo + PAIR] += grad_key
            grad_pair_ref[keys_at, third + lo : third + lo + PAIR] += grad_value
        return carry

    lax.fori_loop(ranges[block, 0], ranges[block, 1], step, 0)
    for pair in range(heads // 2):
        both = jnp.concatenate([acc[2 * pair], acc[2 * pair + 1]], axis=0).T
        grad_query_ref[:, pair * PAIR : (pair + 1) * PAIR] = both * HEAD_DIM ** (-0.5)


def attend_back(ranges, window, marks, log_norm, attended, grad_attended, halo):
    groups, _, rows = marks.shape
    span, slab = window.shape
    third = slab // 3
    heads = third // HEAD_DIM
    first = halo // rows
    return pl.pallas_call(
        attend_back_kernel,
        grid_spec=pltpu.PrefetchScalarGridSpec(
            num_scalar_prefetch=1,
            grid=(groups,),
            in_specs=[
                pl.BlockSpec((rows, slab), lambda i, r: (first + i, 0)),
                pl.BlockSpec((span, slab), lambda i, r: (0, 0)),
                pl.BlockSpec((1, 8, rows), lambda i, r: (i, 0, 0)),
                pl.BlockSpec((1, heads, rows), lambda i, r: (i, 0, 0)),
                pl.BlockSpec((rows, third), lambda i, r: (i, 0)),
                pl.BlockSpec((rows, third), lambda i, r: (i, 0)),
            ],
            out_specs=[
                pl.BlockSpec((rows, third), lambda i, r: (i, 0)),
                pl.BlockSpec((span, 2 * third), lambda i, r: (0, 0)),
            ],
            scratch_shapes=[pltpu.VMEM((heads, HEAD_DIM, rows), jnp.float32)],
        ),
        out_shape=[
            jax.ShapeDtypeStruct((groups * rows, third), jnp.float32),
            jax.ShapeDtypeStruct((span, 2 * third), jnp.float32),
        ],
        compiler_params=pltpu.CompilerParams(vmem_limit_bytes=56 * 2**20),
    )(ranges, window, window, marks, log_norm, attended, grad_attended)


def with_column(matrix, column, extra):
    return jnp.concatenate([matrix, jnp.pad(column[:, None], ((0, 0), (0, extra - 1)))], axis=1)


def on_device(
    stream,
    cotangent,
    bounds,
    joined_proj,
    out_proj,
    wide_proj,
    down_proj,
    gain_first,
    gain_second,
    joined_momentum,
    out_momentum,
    wide_momentum,
    down_momentum,
    gain_first_momentum,
    gain_second_momentum,
    joined_variance,
    out_variance,
    wide_variance,
    down_variance,
    gain_first_variance,
    gain_second_variance,
):
    row_count = stream.shape[0]
    width = stream.shape[1]
    heads = width // HEAD_DIM
    both = ("dp", "group")
    gains = jnp.stack([gain_first, gain_second], axis=1)
    gains = jnp.pad(gains, ((0, 0), (0, GAIN_PAD - 2)))
    joined_gains = jnp.concatenate([joined_proj, gains], axis=1).astype(jnp.bfloat16)
    wide_shard = wide_proj.astype(jnp.bfloat16)
    joined_gains, wide_shard = gather_all(
        [joined_gains, wide_shard],
        pieces([joined_gains.shape[1], wide_shard.shape[1]], 1152),
        ("full", "group"),
        1,
    )
    shards = [wide_shard, out_proj.astype(jnp.bfloat16), down_proj.astype(jnp.bfloat16)]
    joined_half = joined_gains[:, : 3 * width]
    gain_one_half = joined_gains[:, 3 * width]
    gain_two_half = joined_gains[:, 3 * width + 1]
    gain_one = gain_one_half.astype(jnp.float32)
    gain_two = gain_two_half.astype(jnp.float32)
    ff_width = down_proj.shape[1]
    first_row = lax.axis_index(("dp", "group")) * row_count
    token_index = first_row + jnp.arange(row_count, dtype=jnp.int32)
    seq_starts = bounds[:, 0]
    seq_ends = bounds[:, 1]
    cosine, sine_table = rope_tables(token_index - seq_starts)
    normed_one, scale_one = normalize(stream)
    normed_in = (normed_one * gain_one).astype(jnp.bfloat16)
    joined_act = jnp.dot(normed_in, joined_half, preferred_element_type=jnp.float32)
    groups = lax.axis_size("group")
    block_rows = row_count * groups
    slab = width // groups

    def turned(columns):
        heads_part = columns.reshape(row_count, heads, HEAD_DIM)
        return rotate(heads_part, cosine, sine_table, 1.0).reshape(row_count, groups, slab)

    pack = jnp.stack(
        [
            turned(joined_act[:, :width]),
            turned(joined_act[:, width : 2 * width]),
            joined_act[:, 2 * width :].reshape(row_count, groups, slab),
        ],
        axis=2,
    )
    pack = pack.astype(jnp.bfloat16).reshape(row_count, 3 * width)
    block_first = lax.axis_index("dp") * block_rows
    marks = jnp.pad(bounds.T - (block_first - LMAX), ((0, 6), (0, 0)))
    window, marks_all, attended_heads, log_norm, attended, wide_half, out_half, down_half = front(
        pack, marks, shards, pieces([v.shape[1] for v in shards], 1408),
        ("grouped", "full", "full"), LMAX, 3,
    )
    ranges = jnp.stack(
        [marks_all[:, 0, 0] // KEY_TILE, (marks_all[:, 1, row_count - 1] + KEY_TILE - 1) // KEY_TILE],
        axis=1,
    )
    residual = stream + jnp.dot(attended, out_half, preferred_element_type=jnp.float32)
    normed_two, scale_two = normalize(residual)
    hidden_in = (normed_two * gain_two).astype(jnp.bfloat16)
    wide_act = jnp.dot(hidden_in, wide_half, preferred_element_type=jnp.float32)
    inner_part = wide_act[:, :ff_width]
    gate_part = wide_act[:, ff_width:]
    activation, gelu_slope = gelu_parts(inner_part)
    gated = (activation * gate_part).astype(jnp.bfloat16)
    output = residual + jnp.einsum(
        "rf,df->rd", gated, down_half, preferred_element_type=jnp.float32
    )
    cot_half = cotangent.astype(jnp.bfloat16)
    spare = -ff_width % 128
    down_local = jnp.einsum(
        "rd,rf->df", cot_half, jnp.pad(gated, ((0, 0), (0, spare))), preferred_element_type=jnp.float32
    )
    grad_gated = jnp.dot(cot_half, down_half, preferred_element_type=jnp.float32)
    grad_inner = (grad_gated * gate_part * gelu_slope).astype(jnp.bfloat16)
    grad_gate = (grad_gated * activation).astype(jnp.bfloat16)
    grad_wide = jnp.concatenate([grad_inner, grad_gate], axis=1)
    wide_local = jnp.einsum("rd,rf->df", hidden_in, grad_wide, preferred_element_type=jnp.float32)
    grad_hidden = jnp.einsum("rf,df->rd", grad_wide, wide_half, preferred_element_type=jnp.float32)
    gain_two_local = jnp.sum(grad_hidden * normed_two, axis=0)
    grad_resid = cotangent + norm_back(grad_hidden * gain_two, normed_two, scale_two)
    resid_half = grad_resid.astype(jnp.bfloat16)
    out_local = jnp.einsum("rd,re->de", attended, resid_half, preferred_element_type=jnp.float32)
    out_local = with_column(out_local, gain_two_local, OUT_PAD)
    grad_attended = jnp.einsum(
        "re,de->rd", resid_half, out_half, preferred_element_type=jnp.float32
    ).astype(jnp.bfloat16)
    grad_heads = swap(grad_attended, True, 5)
    grad_query, grad_window = attend_back(
        ranges, window, marks_all, log_norm, attended_heads, grad_heads, LMAX
    )
    peers = lax.axis_size("dp")
    up = [(i, i + 1) for i in range(peers - 1)]
    down = [(j, i) for i, j in up]
    rim = grad_window[:LMAX].astype(jnp.bfloat16), grad_window[block_rows + LMAX :].astype(jnp.bfloat16)
    from_next = lax.ppermute(rim[0], "dp", down).astype(jnp.float32)
    from_previous = lax.ppermute(rim[1], "dp", up).astype(jnp.float32)
    centre = grad_window[LMAX : LMAX + block_rows]
    extra = block_rows - LMAX
    centre = centre + jnp.pad(from_previous, ((0, extra), (0, 0)))
    centre = centre + jnp.pad(from_next, ((extra, 0), (0, 0)))
    block_tokens = block_first - LMAX + jnp.arange(LMAX, LMAX + block_rows, dtype=jnp.int32)
    block_starts = marks_all[:, 0, :].reshape(block_rows) + (block_first - LMAX)
    block_cos, block_sin = rope_tables(block_tokens - block_starts)

    def turned_back(columns):
        heads_part = columns.reshape(block_rows, heads // groups, HEAD_DIM)
        return rotate(heads_part, block_cos, block_sin, -1.0).reshape(block_rows, slab)

    grad_pack = jnp.concatenate(
        [turned_back(grad_query), turned_back(centre[:, :slab]), centre[:, slab:]], axis=1
    ).astype(jnp.bfloat16)
    locals_half = [v.astype(jnp.bfloat16) for v in (wide_local, down_local, out_local)]
    wide_grad, down_sum, out_sum, grad_joined = scatter_all(
        locals_half, pieces([v.shape[1] for v in locals_half], 1408), 2, grad_pack
    )
    grad_joined = grad_joined.reshape(row_count, groups, 3, slab)
    grad_joined = grad_joined.transpose(0, 2, 1, 3).reshape(row_count, 3 * width)
    joined_local = jnp.einsum(
        "rd,re->de", normed_in, grad_joined, preferred_element_type=jnp.float32
    )
    grad_normed = jnp.einsum(
        "re,de->rd", grad_joined, joined_half, preferred_element_type=jnp.float32
    )
    gain_one_local = jnp.sum(grad_normed * normed_one, axis=0)
    stream_grad = grad_resid + norm_back(grad_normed * gain_one, normed_one, scale_one)
    joined_local = with_column(joined_local, gain_one_local, GAIN_PAD)
    joined_half_local = joined_local.astype(jnp.bfloat16)
    (joined_sum,) = scatter_all([joined_half_local], pieces([joined_local.shape[1]], 640), 6)
    joined_grad = joined_sum[:, : 3 * width]
    gain_first_grad = joined_sum[:, 3 * width]
    out_grad = out_sum[:, :width]
    gain_second_grad = out_sum[:, width]
    down_grad = down_sum[:, :ff_width]
    joined_new, joined_momentum_new, joined_variance_new = adam_step(
        joined_proj, joined_grad, joined_momentum, joined_variance, WEIGHT_DECAY
    )
    out_new, out_momentum_new, out_variance_new = adam_step(
        out_proj, out_grad, out_momentum, out_variance, WEIGHT_DECAY
    )
    wide_new, wide_momentum_new, wide_variance_new = adam_step(
        wide_proj, wide_grad, wide_momentum, wide_variance, WEIGHT_DECAY
    )
    down_new, down_momentum_new, down_variance_new = adam_step(
        down_proj, down_grad, down_momentum, down_variance, WEIGHT_DECAY
    )
    gain_first_new, gain_first_momentum_new, gain_first_variance_new = adam_step(
        gain_first, gain_first_grad, gain_first_momentum, gain_first_variance, 0.0
    )
    gain_second_new, gain_second_momentum_new, gain_second_variance_new = adam_step(
        gain_second, gain_second_grad, gain_second_momentum, gain_second_variance, 0.0
    )
    return (
        output,
        stream_grad,
        joined_grad,
        out_grad,
        wide_grad,
        down_grad,
        gain_first_grad,
        gain_second_grad,
        joined_new,
        out_new,
        wide_new,
        down_new,
        gain_first_new,
        gain_second_new,
        joined_momentum_new,
        out_momentum_new,
        wide_momentum_new,
        down_momentum_new,
        gain_first_momentum_new,
        gain_second_momentum_new,
        joined_variance_new,
        out_variance_new,
        wide_variance_new,
        down_variance_new,
        gain_first_variance_new,
        gain_second_variance_new,
    )


def solution(mesh):
    placed = (
        P(("dp", "group"), None),
        P(("dp", "group"), None),
        P(("dp", "group"), None),
        P(("dp", "group"), None),
        P(("dp", "group"), None),
        P(("dp", "group"), None),
        P(("dp", "group"), None),
        P(("dp", "group")),
        P(("dp", "group")),
        P(("dp", "group"), None),
        P(("dp", "group"), None),
        P(("dp", "group"), None),
        P(("dp", "group"), None),
        P(("dp", "group")),
        P(("dp", "group")),
        P(("dp", "group"), None),
        P(("dp", "group"), None),
        P(("dp", "group"), None),
        P(("dp", "group"), None),
        P(("dp", "group")),
        P(("dp", "group")),
    )
    return jax.shard_map(
        on_device,
        mesh=mesh,
        in_specs=placed,
        out_specs=(
            P(("dp", "group"), None),
            P(("dp", "group"), None),
            P(("dp", "group"), None),
            P(("dp", "group"), None),
            P(("dp", "group"), None),
            P(("dp", "group"), None),
            P(("dp", "group")),
            P(("dp", "group")),
            P(("dp", "group"), None),
            P(("dp", "group"), None),
            P(("dp", "group"), None),
            P(("dp", "group"), None),
            P(("dp", "group")),
            P(("dp", "group")),
            P(("dp", "group"), None),
            P(("dp", "group"), None),
            P(("dp", "group"), None),
            P(("dp", "group"), None),
            P(("dp", "group")),
            P(("dp", "group")),
            P(("dp", "group"), None),
            P(("dp", "group"), None),
            P(("dp", "group"), None),
            P(("dp", "group"), None),
            P(("dp", "group")),
            P(("dp", "group")),
        ),
        check_vma=False,
    )
```
